32 devices in a mesh: seq: 16 (over z, x, core), tp: 2 (over y).
Axes of the slice: x: 2, y: 2, z: 4, core: 2. Of those that a mesh axis runs over, the one named last changes fastest.
Arguments:
- tokens: bfloat16 [2048, 2048], P('seq', 'tp'), may hold values from -6 to 6
- attn_gain: bfloat16 [2048], replicated, may hold values from 0.25 to 1.75
- w_query: bfloat16 [2048, 2048], P(None, 'tp'), may hold values from -1 to 9
- w_key: bfloat16 [2048, 2048], P(None, 'tp'), may hold values from -0.125 to 0.125
- w_value: bfloat16 [2048, 2048], P(None, 'tp'), may hold values from -0.125 to 0.125
- w_out: bfloat16 [2048, 2048], P('tp'), may hold values from -0.5 to 0.5
- prefix_keys: bfloat16 [512, 2048], P('seq', 'tp'), may hold values from -6 to 6
- prefix_values: bfloat16 [512, 2048], P('seq', 'tp'), may hold values from -6 to 6
- shard_group: int32 [16], replicated, may hold values from 0 to 1, as said below
- request_group: int32 [8], replicated, may hold values from 0 to 1, as said below
- lengths: int32 [8], replicated, may hold values from 1 to 512, 2048 in all
- moe_gain: bfloat16 [2048], replicated, may hold values from 0.25 to 1.75
- w_router: bfloat16 [2048, 16], replicated, may hold values from -1 to 8
- w_gate: bfloat16 [16, 2048, 1024], P('seq', None, 'tp'), may hold values from -0.125 to 0.125
- w_up: bfloat16 [16, 2048, 1024], P('seq', None, 'tp'), may hold values from -0.125 to 0.125
- w_down: bfloat16 [16, 1024, 2048], P('seq', 'tp'), may hold values from -3 to 3
- routes: int32 [2048, 8], P('seq'), may hold values from 0 to 15, all different within a row; in each aligned block of 128 rows (0 to 127, 128 to 255, ...) at most 96 rows name the same one
- final_gain: bfloat16 [2048], P('tp'), may hold values from 0.25 to 1.75
- w_head: bfloat16 [2048, 50304], P('tp', 'seq'), may hold values from -2 to 9
Outputs:
- hidden: bfloat16 [2048, 2048], P('seq', 'tp')
- log_probs: float32 [8, 50304], P(None, 'seq')
The draws below stay inside these ranges and needn't reach their ends.
Inputs may be any that keep to these rules, and one draw needn't show every extreme that they name: `shard_group`: exactly half of the 16 cache shards belong to each group. `request_group`: exactly half of the requests belong to each group. The lengths sum to 2048; the largest is exactly 512. `routes`: among the rows of one device no expert is named more than 96 times, a bound that some block reaches.
All inputs are finite; a program needn't handle non-finite values.
Results may differ from the reference program's by a relative error of at most 0.017.
The reference program's roundings to bfloat16 on the way count: a program that leaves them out, or rounds other values in their place, can miss the bound.
Values may be sent and summed in bfloat16 or wider, within the bound.
A program may use at most 128 MiB of HBM per device.

```python
import math
import jax
import jax.numpy as jnp
import numpy as np
from jax import lax

D = 2048
HEADS = 16
HD = 128
FFE = 1024
VOCAB = 50304
TOPK = 8
SPAN = 4
TOK_DEV = 128
PDEV = 32
EXPERTS = 16
TOKENS = 2048
REQS = 8
PREFIX = 256
CAP = 96
N_SEQ = 16


def draw_shard_group(key, part):
    order = jax.random.permutation(jax.random.fold_in(key, 11), N_SEQ)
    return (order < N_SEQ // 2).astype(jnp.int32)


def draw_request_group(key, part):
    order = jax.random.permutation(jax.random.fold_in(key, 23), REQS)
    return (order % 2).astype(jnp.int32)


def draw_tokens(key, part):
    noise_key = jax.random.fold_in(key, 31)
    column_frac = jnp.arange(D).astype(jnp.float32)[None, :] / D
    rising = 0.6 + 1.2 * column_frac
    values = jax.random.truncated_normal(noise_key, -3.3, 3.3, (TOKENS, D), jnp.float32) * rising
    return values.astype(jnp.bfloat16)


def draw_w_query(key, part):
    base_key = jax.random.fold_in(key, 43)
    extent = (D, HEADS * HD)
    values = jax.random.truncated_normal(base_key, -4.0, 4.0, extent, jnp.float32) * D ** (-0.5)
    return values.astype(jnp.bfloat16)


def draw_prefix_keys(key, part):
    base_key = jax.random.fold_in(key, 53)
    extent = (N_SEQ * PDEV, HEADS * HD)
    values = jax.random.truncated_normal(base_key, -6.0, 6.0, extent, jnp.float32)
    return values.astype(jnp.bfloat16)


def draw_w_router(key, part):
    base_key = jax.random.fold_in(key, 61)
    extent = (D, EXPERTS)
    values = jax.random.truncated_normal(base_key, -4.0, 4.0, extent, jnp.float32) * D ** (-0.5)
    return values.astype(jnp.bfloat16)


def draw_w_head(key, part):
    base_key = jax.random.fold_in(key, 73)
    extent = (D, VOCAB)
    column_pos = jnp.arange(VOCAB)
    rising = 1.0 + 2.0 * column_pos.astype(jnp.float32) / VOCAB
    values = jax.random.truncated_normal(base_key, -6.0, 6.0, extent, jnp.float32) * 0.07 * rising[None, :]
    return values.astype(jnp.bfloat16)


def steps_of(own_key, shape, cuts, smallest, top_value):
    level = 1.0
    for dim, blocks in cuts:
        heights = jax.random.uniform(jax.random.fold_in(jax.random.fold_in(own_key, 6), dim), (blocks,), jnp.float32, smallest / len(cuts), top_value / len(cuts))
        level = level * jnp.repeat(jnp.exp(heights), shape[dim] // blocks).reshape((-1,) + (1,) * (len(shape) - 1 - dim))
    return level


def length_profile(count, total, limit, lean):
    loads = [(1 << 20) // math.isqrt(standing ** lean) + 1 for standing in range(2, count + 1)]
    spare, given = total - limit - (count - 1), [1] * (count - 1)
    while spare > 0:
        candidates = [i for i in range(count - 1) if given[i] < limit]
        whole, remaining = sum([loads[i] for i in candidates]), spare
        for i in candidates:
            extra = min(limit - given[i], max(1, remaining * loads[i] // whole), spare)
            given[i] = given[i] + extra
            spare = spare - extra
    return np.array([limit] + given)


def ragged_sizes(stream_key, count, total, bound, skew):
    if count == 2:
        one = jax.random.randint(stream_key, (), max(1, total - bound), min(bound, total - 1) + 1)
        return jnp.stack([one, total - one])
    sizes = jnp.asarray(length_profile(count, total, bound, skew), jnp.int32)
    pairs = (count - 1) // 2
    source_of, taker = sizes[1:1 + 2 * pairs:2], sizes[2:2 + 2 * pairs:2]
    slack = jnp.minimum(source_of - 1, bound - taker)
    passed = jax.random.randint(jax.random.fold_in(stream_key, 1), (pairs,), 0, 1 << 20) % (slack + 1)
    sizes = sizes.at[1:1 + 2 * pairs:2].set(source_of - passed).at[2:2 + 2 * pairs:2].set(taker + passed)
    return sizes[jax.random.permutation(jax.random.fold_in(stream_key, 2), count)]


def routed_block(stream_key, own, number, rows, number_of, top, bound, slope):
    sequence = jax.random.permutation(stream_key, number_of)
    crowded, usual = shares(number_of, rows * top, bound, slope, True), shares(number_of, rows * top, bound, slope, False)
    places = jnp.arange(number_of)

    def named(sizes, turn):
        used = int((sizes > 0).sum())
        fixed = max(1, used // 4)
        shifted = fixed + (places - fixed + turn * (used - fixed)) % max(1, number_of - fixed)
        return jnp.zeros((number_of,), jnp.int32).at[sequence[jnp.where(places < fixed, places, shifted)]].set(jnp.asarray(sizes, jnp.int32))

    sizes = jnp.where(number % 4 == 0, named(crowded, number // 4), named(usual, number - number // 4 - 1))
    mixed = jax.random.permutation(jax.random.fold_in(own, 3), number_of)
    donor, sink = mixed[0:number_of // 2 * 2:2], mixed[1:number_of // 2 * 2:2]
    slack = jnp.minimum(sizes[donor] - 1, bound - sizes[sink]) // 2
    slack = jnp.where((donor == sequence[0]) | (sink == sequence[0]) | (sizes[sink] == 0), 0, jnp.maximum(slack, 0))
    shifted = jax.random.randint(jax.random.fold_in(own, 4), (number_of // 2,), 0, 1 << 20) % (slack + 1)
    sizes = sizes.at[donor].add(-shifted).at[sink].add(shifted)
    items = jnp.searchsorted(jnp.cumsum(sizes), jnp.arange(rows * top), side="right").astype(jnp.int32)
    listing = items.reshape(top, rows).T
    listing = listing[jax.random.permutation(jax.random.fold_in(own, 1), rows)]
    turn = jax.random.randint(jax.random.fold_in(own, 2), (rows, 1), 0, top)
    return jnp.take_along_axis(listing, (jnp.arange(top)[None, :] + turn) % top, axis=1)


def shares(number_of, total, most, slope, full):
    portions = [(1 << 20) // math.isqrt(rank ** slope) + 1 for rank in range(1, number_of + 1)]
    largest = most if full else min(most, max(-(-total // number_of), total * portions[0] // sum(portions)))
    least = 1 if total - largest >= number_of - 1 else 0
    holding, surplus = [largest] + [least] * (number_of - 1), total - largest - least * (number_of - 1)
    while surplus > 0:
        candidates = [i for i in range(1, number_of) if holding[i] < largest] or [i for i in range(1, number_of) if holding[i] < most]
        whole, remaining = sum([portions[i] for i in candidates]), surplus
        for i in candidates:
            extra = min(most - holding[i], max(1, remaining * portions[i] // whole), surplus)
            holding[i] = holding[i] + extra
            surplus = surplus - extra
    return np.array(holding)


def scatter_about(stream_key, shape, deviation, reach, cuts=(), dtype=jnp.bfloat16):
    level = steps_of(stream_key, shape, cuts, -0.22, 0.18) if cuts else 1.0
    result = jax.random.normal(stream_key, shape, jnp.float32) * deviation * level
    return jnp.minimum(jnp.maximum(result, -reach), reach).astype(dtype)


def setup_inputs(seed: int = 0) -> dict:
    streams_of = jax.random.split(jax.random.key(seed), 20)
    tokens = draw_tokens(jax.random.fold_in(streams_of[19], 71), 0)
    attn_gain = jnp.clip(1.0 + 0.15 * jax.random.normal(streams_of[1], (D,), jnp.float32), 0.25, 1.75).astype(jnp.bfloat16)
    w_query = draw_w_query(jax.random.fold_in(streams_of[19], 71), 0)
    w_key = scatter_about(streams_of[3], (D, HEADS * HD), D ** -0.5, 0.125, ((1, 2),))
    w_value = scatter_about(streams_of[4], (D, HEADS * HD), D ** -0.5, 0.125, ((1, 2),))
    w_out = scatter_about(streams_of[5], (HEADS * HD, D), (max(1, HEADS * HD // 16)) ** -0.5, 0.5, ((0, 2),))
    prefix_keys = draw_prefix_keys(jax.random.fold_in(streams_of[19], 71), 0)
    prefix_values = scatter_about(streams_of[7], (N_SEQ * PDEV, HEADS * HD), 1.0, 6.0, ((0, 16), (1, 2)))
    shard_group = draw_shard_group(jax.random.fold_in(streams_of[19], 71), 0)
    request_group = draw_request_group(jax.random.fold_in(streams_of[19], 71), 0)
    lengths = ragged_sizes(streams_of[10], REQS, TOKENS, SPAN * TOK_DEV, 2).astype(jnp.int32)
    moe_gain = jnp.clip(1.0 + 0.15 * jax.random.normal(streams_of[11], (D,), jnp.float32), 0.25, 1.75).astype(jnp.bfloat16)
    w_router = draw_w_router(jax.random.fold_in(streams_of[19], 71), 0)
    w_gate = scatter_about(streams_of[13], (EXPERTS, D, FFE), D ** -0.5, 0.125, ((0, 16), (2, 2)))
    w_up = scatter_about(streams_of[14], (EXPERTS, D, FFE), D ** -0.5, 0.125, ((0, 16), (2, 2)))
    w_down = scatter_about(streams_of[15], (EXPERTS, FFE, D), (max(1, FFE // 256)) ** -0.5, 3.0, ((0, 16), (1, 2)))
    routes_keys = jax.random.split(jax.random.fold_in(streams_of[16], 1), TOKENS // TOK_DEV)
    routes_turns = jax.random.permutation(jax.random.fold_in(streams_of[16], 3), TOKENS // TOK_DEV)
    routes = jax.vmap(lambda own, number: routed_block(jax.random.fold_in(streams_of[16], 2), own, number, TOK_DEV, EXPERTS, TOPK, CAP, 2))(routes_keys, routes_turns).reshape((TOKENS, TOPK))
    final_gain = jnp.clip(1.0 + 0.15 * jax.random.normal(streams_of[17], (D,), jnp.float32), 0.25, 1.75).astype(jnp.bfloat16)
    w_head = draw_w_head(jax.random.fold_in(streams_of[19], 71), 0)
    return {"tokens": tokens, "attn_gain": attn_gain, "w_query": w_query, "w_key": w_key, "w_value": w_value, "w_out": w_out, "prefix_keys": prefix_keys, "prefix_values": prefix_values, "shard_group": shard_group, "request_group": request_group, "lengths": lengths, "moe_gain": moe_gain, "w_router": w_router, "w_gate": w_gate, "w_up": w_up, "w_down": w_down, "routes": routes, "final_gain": final_gain, "w_head": w_head}


EPS = 1e-05

def normalize(rows, gain):
    inv = lax.rsqrt(lax.optimization_barrier(jnp.mean(rows * rows, -1, keepdims=True)) + EPS)
    return rows * inv * gain.astype(jnp.float32)

def rotate(vectors, position):
    half = vectors.shape[-1] // 2
    freq = 10000.0 ** (-jnp.arange(half).astype(jnp.float32) / half)
    angle = position[:, None] * freq[None, :]
    cosine = jnp.cos(angle)[:, None, :]
    sine = jnp.sin(angle)[:, None, :]
    first = vectors[..., :half]
    second = vectors[..., half:]
    return jnp.concatenate([first * cosine - second * sine, second * cosine + first * sine], -1)

def reference(tokens, attn_gain, w_query, w_key, w_value, w_out, prefix_keys, prefix_values, shard_group, request_group, lengths, moe_gain, w_router, w_gate, w_up, w_down, routes, final_gain, w_head):
    f32 = jnp.float32
    bf16 = jnp.bfloat16
    ends = jnp.cumsum(lengths).astype(jnp.int32)
    starts = ends - lengths
    index = jnp.arange(TOKENS).astype(jnp.int32)
    request = lax.optimization_barrier(jnp.sum((index[:, None] >= ends[None, :]).astype(jnp.int32), 1))
    position = (PREFIX + index - starts[request]).astype(f32)
    group = request_group[request]
    cache_group = shard_group[jnp.arange(N_SEQ * PDEV).astype(jnp.int32) // PDEV]
    normed = normalize(tokens.astype(f32), attn_gain).astype(bf16)
    query = rotate(jnp.dot(normed, w_query, preferred_element_type=f32).reshape(TOKENS, HEADS, HD), position).astype(bf16)
    key = rotate(jnp.dot(normed, w_key, preferred_element_type=f32).reshape(TOKENS, HEADS, HD), position).astype(bf16)
    value = jnp.dot(normed, w_value, preferred_element_type=f32).astype(bf16).reshape(TOKENS, HEADS, HD)
    cache_k = prefix_keys.reshape(N_SEQ * PDEV, HEADS, HD)
    cache_v = prefix_values.reshape(N_SEQ * PDEV, HEADS, HD)
    prefix_mask = group[:, None] == cache_group[None, :]
    suffix_mask = (request[:, None] == request[None, :]) & (index[None, :] <= index[:, None])
    allowed = jnp.concatenate([prefix_mask, suffix_mask], 1)

    def one_head(head):
        qh = query[:, head, :].astype(f32)
        kh = jnp.concatenate([cache_k[:, head, :], key[:, head, :]], 0).astype(f32)
        vh = jnp.concatenate([cache_v[:, head, :], value[:, head, :]], 0)
        scores = jnp.dot(qh, kh.T) / jnp.sqrt(f32(HD))
        scores = jnp.where(allowed, scores, -jnp.inf)
        peak = lax.optimization_barrier(jnp.max(scores, -1, keepdims=True))
        weights = jnp.where(allowed, jnp.exp(scores - peak), 0.0)
        total = lax.optimization_barrier(jnp.sum(weights, -1, keepdims=True))
        summed = jnp.dot(weights.astype(bf16).astype(f32), vh.astype(f32))
        return (summed / total).astype(bf16)
    attended = lax.map(one_head, jnp.arange(HEADS))
    attended = jnp.transpose(attended, (1, 0, 2)).reshape(TOKENS, HEADS * HD)
    resid = (tokens.astype(f32) + jnp.dot(attended, w_out, preferred_element_type=f32)).astype(bf16)
    moe_in = normalize(resid.astype(f32), moe_gain).astype(bf16)
    probs = jax.nn.softmax(jnp.dot(moe_in, w_router, preferred_element_type=f32), -1)
    route_weight = jnp.take_along_axis(probs, routes, 1)
    flat = routes.reshape(N_SEQ, TOK_DEV * TOPK)
    hits = (flat[:, :, None] == jnp.arange(EXPERTS).astype(jnp.int32)[None, None, :]).astype(jnp.int32)
    rank = lax.optimization_barrier(jnp.sum((jnp.cumsum(hits, 1) - hits) * hits, -1))
    block = jnp.broadcast_to(jnp.arange(N_SEQ).astype(jnp.int32)[:, None], flat.shape)
    token_id = block * TOK_DEV + jnp.arange(TOK_DEV * TOPK).astype(jnp.int32)[None, :] // TOPK
    table = jnp.zeros((EXPERTS, N_SEQ, CAP), jnp.int32).at[flat, block, rank].set(token_id)

    def one_expert(pack):
        rows_id, gate_w, up_w, down_w = pack
        rows = moe_in[rows_id.reshape(-1)]
        gate = jnp.dot(rows, gate_w, preferred_element_type=f32)
        up = jnp.dot(rows, up_w, preferred_element_type=f32)
        act = (jax.nn.silu(gate) * up).astype(bf16)
        return jnp.dot(act, down_w, preferred_element_type=f32).astype(bf16)
    outputs = lax.map(one_expert, (table, w_gate, w_up, w_down))
    outputs = outputs.reshape(EXPERTS * N_SEQ * CAP, D)
    picked = outputs[((flat * N_SEQ + block) * CAP + rank).reshape(-1)].reshape(TOKENS, TOPK, D)
    moe = lax.optimization_barrier(jnp.sum(picked.astype(f32) * route_weight[:, :, None], 1))
    hidden = (resid.astype(f32) + moe).astype(bf16)
    final = normalize(hidden.astype(f32), final_gain).astype(bf16)
    last = final[ends - 1]
    logits = jnp.dot(last, w_head, preferred_element_type=f32)
    peak = lax.optimization_barrier(jnp.max(logits, -1, keepdims=True))
    log_probs = logits - peak - jnp.log(lax.optimization_barrier(jnp.sum(jnp.exp(logits - peak), -1, keepdims=True)))
    return (hidden, log_probs)
```

```python
import jax
import jax.numpy as jnp
from jax import lax
from jax.experimental import pallas as pl
from jax.experimental.pallas import tpu as pltpu
from jax.sharding import PartitionSpec as P

HD = 128
SPAN = 4
VMEM = pltpu.VMEM


EPS = 1e-05
NEGATIVE = -1e30


def from_behind(value, axis, steps):
    count = lax.axis_size(axis)
    leading, last = (max(0, -steps), min(count, count - steps))
    return lax.ppermute(value, axis, [(source, source + steps) for source in range(leading, last)])


def normalize(rows, gain):
    inv = lax.rsqrt(jnp.mean(rows * rows, -1, keepdims=True) + EPS)
    return rows * inv * gain.astype(jnp.float32)


def rotate(vectors, position):
    half = vectors.shape[-1] // 2
    freq = 10000.0 ** (-jnp.arange(half).astype(jnp.float32) / half)
    angle = position[:, None] * freq[None, :]
    cosine = jnp.cos(angle)[:, None, :]
    sine = jnp.sin(angle)[:, None, :]
    first = vectors[..., :half]
    second = vectors[..., half:]
    return jnp.concatenate([first * cosine - second * sine, second * cosine + first * sine], -1)


def request_of(index, ends):
    return jnp.sum((index[:, None] >= ends[None, :]).astype(jnp.int32), 1)


def lookup(selector, table):
    hit = selector[:, None] == jnp.arange(table.shape[0])[None, :]
    return jnp.sum(jnp.where(hit, table[None, :], 0), 1)


def prefix_sums(values):
    order = jnp.arange(values.shape[0])
    return jnp.sum(jnp.where(order[:, None] >= order[None, :], values[None, :], 0), 1)


def partner(axis, bit):
    index = lax.axis_index(axis)
    span = 1 << bit
    other = index + span - 2 * span * ((index // span) % 2)
    return {axis: other}


def greet(stages):
    barrier = pltpu.get_barrier_semaphore()
    for axis, bit in stages:
        pl.semaphore_signal(barrier, inc=1, device_id=partner(axis, bit))
    pl.semaphore_wait(barrier, len(stages))


def swap(source, target, send_sem, recv_sem, stage):
    copy = pltpu.make_async_remote_copy(
        src_ref=source, dst_ref=target, send_sem=send_sem, recv_sem=recv_sem,
        device_id=partner(*stage),
    )
    copy.start()
    return copy


def bits_of(axis):
    return [(axis, bit) for bit in range(lax.axis_size(axis).bit_length() - 1)]


def last_rows(chosen, gain, width):
    seq_stages, tp_stages = bits_of("seq"), bits_of("tp")
    stages = seq_stages + tp_stages
    rows, part = chosen.shape

    def kernel(chosen_ref, gain_ref, out_ref, held, got, sq_held, sq_got, send_sem, recv_sem):
        greet(stages)
        held[0] = chosen_ref[...]
        count = len(seq_stages)
        for k, stage in enumerate(seq_stages):
            swap(held.at[k], got.at[k], send_sem.at[k], recv_sem.at[k], stage).wait()
            held[k + 1] = held[k] + got[k]
        total = held[count]
        sq_held[0] = jnp.broadcast_to(jnp.sum(total * total, -1, keepdims=True), (rows, 128))
        for k, stage in enumerate(tp_stages):
            n = count + k
            swap(sq_held.at[k], sq_got.at[k], send_sem.at[n], recv_sem.at[n], stage).wait()
            sq_held[k + 1] = sq_held[k] + sq_got[k]
        square = sq_held[len(tp_stages)][:, :1]
        scaled = total * lax.rsqrt(square / width + EPS) * gain_ref[...].astype(jnp.float32)
        out_ref[...] = scaled.astype(jnp.bfloat16)

    ns, nt = len(seq_stages), len(tp_stages)
    return pl.pallas_call(
        kernel,
        out_shape=jax.ShapeDtypeStruct((rows, part), jnp.bfloat16),
        in_specs=[pl.BlockSpec(memory_space=VMEM)] * 2,
        out_specs=pl.BlockSpec(memory_space=VMEM),
        scratch_shapes=[
            VMEM((ns + 1, rows, part), jnp.float32),
            VMEM((ns, rows, part), jnp.float32),
            VMEM((nt + 1, rows, 128), jnp.float32),
            VMEM((nt, rows, 128), jnp.float32),
            pltpu.SemaphoreType.DMA((ns + nt,)),
            pltpu.SemaphoreType.DMA((ns + nt,)),
        ],
        compiler_params=pltpu.CompilerParams(collective_id=1, has_side_effects=True),
        name="last_rows",
    )(chosen, gain.reshape(1, part))


def log_softmax(logits):
    seq_stages, tp_stages = bits_of("seq"), bits_of("tp")
    stages = tp_stages + seq_stages
    rows, part = logits.shape

    def kernel(logits_ref, out_ref, held, got, st_held, st_got, send_sem, recv_sem):
        greet(stages)
        held[0] = logits_ref[...]
        count = len(tp_stages)
        for k, stage in enumerate(tp_stages):
            swap(held.at[k], got.at[k], send_sem.at[k], recv_sem.at[k], stage).wait()
            held[k + 1] = held[k] + got[k]
        total = held[count]
        peak = jnp.max(total, -1, keepdims=True)
        mass = jnp.sum(jnp.exp(total - peak), -1, keepdims=True)
        st_held[0, :, :128] = jnp.broadcast_to(peak, (rows, 128))
        st_held[0, :, 128:] = jnp.broadcast_to(mass, (rows, 128))
        for k, stage in enumerate(seq_stages):
            n = count + k
            swap(st_held.at[k], st_got.at[k], send_sem.at[n], recv_sem.at[n], stage).wait()
            mine, theirs = st_held[k, :, :128], st_got[k, :, :128]
            top = jnp.maximum(mine, theirs)
            st_held[k + 1, :, :128] = top
            st_held[k + 1, :, 128:] = st_held[k, :, 128:] * jnp.exp(mine - top) + st_got[
                k, :, 128:
            ] * jnp.exp(theirs - top)
        last = len(seq_stages)
        out_ref[...] = total - st_held[last, :, :1] - jnp.log(st_held[last, :, 128:129])

    ns, nt = len(seq_stages), len(tp_stages)
    return pl.pallas_call(
        kernel,
        out_shape=jax.ShapeDtypeStruct((rows, part), jnp.float32),
        in_specs=[pl.BlockSpec(memory_space=VMEM)],
        out_specs=pl.BlockSpec(memory_space=VMEM),
        scratch_shapes=[
            VMEM((nt + 1, rows, part), jnp.float32),
            VMEM((nt, rows, part), jnp.float32),
            VMEM((ns + 1, rows, 256), jnp.float32),
            VMEM((ns, rows, 256), jnp.float32),
            pltpu.SemaphoreType.DMA((ns + nt,)),
            pltpu.SemaphoreType.DMA((ns + nt,)),
        ],
        compiler_params=pltpu.CompilerParams(collective_id=2, has_side_effects=True),
        name="log_softmax",
    )(logits)


def gather_columns(block):
    stages = bits_of("tp")
    rows, part = block.shape
    count = lax.axis_size("tp")

    def kernel(block_ref, out_ref, send_sem, recv_sem):
        greet(stages)
        me = lax.axis_index("tp")
        out_ref[:, pl.ds(pl.multiple_of(me * part, part), part)] = block_ref[...]
        for k, stage in enumerate(stages):
            wide = part << k
            start = pl.multiple_of((me // (1 << k)) * wide, wide)
            piece = out_ref.at[:, pl.ds(start, wide)]
            swap(piece, piece, send_sem.at[k], recv_sem.at[k], stage).wait()

    return pl.pallas_call(
        kernel,
        out_shape=jax.ShapeDtypeStruct((rows, part * count), block.dtype),
        in_specs=[pl.BlockSpec(memory_space=VMEM)],
        out_specs=pl.BlockSpec(memory_space=VMEM),
        scratch_shapes=[pltpu.SemaphoreType.DMA((len(stages),))] * 2,
        compiler_params=pltpu.CompilerParams(collective_id=3, has_side_effects=True),
        name="gather_columns",
    )(block)


def sum_over_tp(block):
    stages = bits_of("tp")
    rows, part = block.shape

    def kernel(block_ref, out_ref, held, got, send_sem, recv_sem):
        greet(stages)
        for k, stage in enumerate(stages):
            source = block_ref if k == 0 else held.at[k]
            swap(source, got.at[k], send_sem.at[k], recv_sem.at[k], stage).wait()
            total = source[...].astype(jnp.float32) + got[k].astype(jnp.float32)
            if k + 1 < len(stages):
                held[k + 1] = total.astype(jnp.bfloat16)
            else:
                out_ref[...] = total

    count = len(stages)
    return pl.pallas_call(
        kernel,
        out_shape=jax.ShapeDtypeStruct((rows, part), jnp.float32),
        in_specs=[pl.BlockSpec(memory_space=VMEM)],
        out_specs=pl.BlockSpec(memory_space=VMEM),
        scratch_shapes=[
            VMEM((count, rows, part), jnp.bfloat16),
            VMEM((count, rows, part), jnp.bfloat16),
            pltpu.SemaphoreType.DMA((count,)),
            pltpu.SemaphoreType.DMA((count,)),
        ],
        compiler_params=pltpu.CompilerParams(collective_id=4, has_side_effects=True),
        name="sum_over_tp",
    )(block)


HOPS = 4


def ring_place():
    s = lax.axis_index("seq")
    core = s % 2
    x = (s // 2) % 2
    z = s // 4
    return s, core, z + x * (7 - 2 * z)


def chip_at(place):
    q = (place + 16) % 8
    x = q // 4
    z = q + x * (7 - 2 * q)
    return z * 2 + x


def greet_all(blocks):
    s = lax.axis_index("seq")
    barrier = pltpu.get_barrier_semaphore()
    for d in range(1, blocks):
        pl.semaphore_signal(barrier, inc=1, device_id={"seq": (s + d) % blocks})
    pl.semaphore_signal(barrier, inc=1, device_id={"tp": 1 - lax.axis_index("tp")})
    pl.semaphore_wait(barrier, blocks)


def greet_ring(nxt, prv, sib):
    barrier = pltpu.get_barrier_semaphore()
    for d in ({"seq": nxt}, {"seq": prv}, {"seq": sib}, {"tp": 1 - lax.axis_index("tp")}):
        pl.semaphore_signal(barrier, inc=1, device_id=d)
    pl.semaphore_wait(barrier, 4)


def spread_ring(rows, share):
    tall, wide = rows.shape
    blocks = share.shape[0]
    q = tall // 4

    def kernel(rows_ref, share_ref, out_ref, share_out, send_sem, recv_sem, sh_send, sh_recv):
        s, core, r = ring_place()
        y = lax.axis_index("tp")
        step = 1 - 2 * core
        nxt = {"seq": chip_at(r + step) * 2 + core}
        sib = {"seq": s + step}
        other = {"tp": 1 - y}
        out_ref[pl.ds(pl.multiple_of(s * tall, tall), tall)] = rows_ref[...]
        share_out[s] = share_ref[s]
        greet_all(blocks)
        mine, theirs = core * tall, (1 - core) * tall
        spot = {
            "eo": (mine + 2 * q, 2 * q),
            "ao": (mine + q * ((core + y) % 2), q),
            "as": (theirs + q * ((1 - core + y) % 2), q),
            "es": (theirs + 2 * q, 2 * q),
            "yao": (mine + q * ((core + 1 - y) % 2), q),
            "yas": (theirs + q * ((2 - core - y) % 2), q),
        }
        used = iter(range(64))

        def send(start, size, device):
            piece = out_ref.at[pl.ds(pl.multiple_of(start, q), size)]
            n = next(used)
            copy = pltpu.make_async_remote_copy(
                src_ref=piece, dst_ref=piece, send_sem=send_sem.at[n], recv_sem=recv_sem.at[n],
                device_id=device,
            )
            copy.start()
            return copy

        ring, cross, pair, shares = {}, {}, {}, []
        pair[0] = send(s * tall, tall, sib)
        home = chip_at(r) * 2 * tall

        def put(table, key, base, name, device):
            table[key] = send(base + spot[name][0], spot[name][1], device)

        for p in ("eo", "ao"):
            put(ring, (1, p), home, p, nxt)
        pair[0].wait_recv()
        for p in ("as", "es"):
            put(ring, (1, p), home, p, nxt)
        for d in range(1, blocks):
            dest = (s + d) % blocks
            copy = pltpu.make_async_remote_copy(
                src_ref=share_ref.at[dest], dst_ref=share_out.at[s], send_sem=sh_send.at[d],
                recv_sem=sh_recv.at[d], device_id={"seq": dest},
            )
            copy.start()
            shares.append(copy)
        full, part = ("eo", "ao", "as", "es"), ("eo", "ao")
        late = []
        for t in range(1, HOPS + 1):
            base = chip_at(r - step * t) * 2 * tall
            onward = full if t < HOPS - 1 else part if t == HOPS - 1 else ()
            here = full if t < HOPS else part
            for p in here:
                ring[t, p].wait_recv()
                if p in onward:
                    put(ring, (t + 1, p), base, p, nxt)
                if p in ("ao", "as"):
                    put(cross, (t, p), base, p, other)
                put(pair, (t, p), base, p, sib)
            for act in late:
                act()
            late = []
            for p in here:
                if p in ("ao", "as"):
                    def act(t=t, p=p, base=base):
                        cross[t, p].wait_recv()
                        put(pair, (t, "y" + p), base, "y" + p, sib)
                    late.append(act)
        for act in late:
            act()
        for key, copy in pair.items():
            if key != 0:
                copy.wait_recv()
        for table in (ring, cross, pair):
            for copy in table.values():
                copy.wait_send()
        for copy in shares:
            copy.wait()

    return pl.pallas_call(
        kernel,
        out_shape=(
            jax.ShapeDtypeStruct((blocks * tall, wide), rows.dtype),
            jax.ShapeDtypeStruct((blocks, 1, tall), share.dtype),
        ),
        in_specs=[pl.BlockSpec(memory_space=VMEM)] * 2,
        out_specs=(pl.BlockSpec(memory_space=VMEM), pl.BlockSpec(memory_space=VMEM)),
        scratch_shapes=[pltpu.SemaphoreType.DMA((64,)), pltpu.SemaphoreType.DMA((64,)),
                        pltpu.SemaphoreType.DMA((blocks,)), pltpu.SemaphoreType.DMA((blocks,))],
        compiler_params=pltpu.CompilerParams(
            collective_id=5, has_side_effects=True, vmem_limit_bytes=40 << 20
        ),
        name="spread_ring",
    )(rows, share)


def collect_ring(partial, resid):
    tall, wide = resid.shape
    half = wide // 2
    ty = tall * 5 // 8
    ts = tall - ty
    bf16 = jnp.bfloat16
    G = 16
    units = [(HOPS, "o")] + [(t, b) for t in range(HOPS - 1, 0, -1) for b in ("s", "o")] + [(0, "o")]
    nu = len(units)

    def kernel(part_ref, resid_ref, out_ref, sib_buf, acc_y, acc_s, y_send, y_recv, ring_y, ring_s,
               far_y, far_s, last_recv, send_sem, recv_sem):
        s, core, r = ring_place()
        y = lax.axis_index("tp")
        step = 1 - 2 * core
        nxt = {"seq": chip_at(r + step) * 2 + core}
        sib = {"seq": s + step}
        other = {"tp": 1 - y}
        greet_ring(nxt["seq"], chip_at(r - step) * 2 + core, sib["seq"])
        used = iter(range(64))
        own_cols = pl.ds(pl.multiple_of(y * half, half), half)
        far_cols = pl.ds(pl.multiple_of((1 - y) * half, half), half)

        def send(source, target, device):
            n = next(used)
            copy = pltpu.make_async_remote_copy(
                src_ref=source, dst_ref=target, send_sem=send_sem.at[n], recv_sem=recv_sem.at[n],
                device_id=device,
            )
            copy.start()
            return copy

        def rows_of(t, b, direction, c):
            place = chip_at(r + direction * t) * 2 + (c if b == "o" else 1 - c)
            return place * tall

        pair = []
        for i, (t, b) in enumerate(units):
            start = pl.multiple_of(rows_of(t, b, -step, 1 - core), tall)
            pair.append(send(part_ref.at[pl.ds(start, tall)], sib_buf.at[i], sib))
        cross, ring, sent = {}, {}, list(pair)

        def summed(i):
            t, b = units[i]
            start = rows_of(t, b, step, core)
            pair[i].wait_recv()

            def body_y(g, _):
                rows = pl.ds(pl.multiple_of(g * G, G), G)
                here = pl.ds(pl.multiple_of(start + g * G, G), G)
                y_send[i, rows] = part_ref[here, far_cols] + sib_buf[i, rows, far_cols]
                acc_y[i, rows] = part_ref[here, own_cols] + sib_buf[i, rows, own_cols]
                return 0

            lax.fori_loop(0, ty // G, body_y, 0)
            cross[i] = send(y_send.at[i], y_recv.at[i], other)
            sent.append(cross[i])

            def body_s(g, _):
                rows = pl.ds(pl.multiple_of(g * G, G), G)
                below = pl.ds(pl.multiple_of(ty + g * G, G), G)
                here = pl.ds(pl.multiple_of(start + ty + g * G, G), G)
                acc_s[i, rows] = part_ref[here] + sib_buf[i, below]
                return 0

            lax.fori_loop(0, ts // G, body_s, 0)

        def slot(t, b):
            return 2 * t + (0 if b == "o" else 1)

        def passed(i):
            t, b = units[i]
            cross[i].wait_recv()
            arrived = (t + 1, b) in units and t > 0
            if arrived:
                for copy in ring[t, b]:
                    copy.wait_recv()
            n = slot(t, b)

            def body_y(g, _):
                rows = pl.ds(pl.multiple_of(g * G, G), G)
                total = acc_y[i, rows] + y_recv[i, rows]
                if arrived:
                    total = total + ring_y[n, rows]
                acc_y[i, rows] = total
                return 0

            lax.fori_loop(0, ty // G, body_y, 0)
            if arrived:
                def body_s(g, _):
                    rows = pl.ds(pl.multiple_of(g * G, G), G)
                    acc_s[i, rows] = acc_s[i, rows] + ring_s[n, rows]
                    return 0

                lax.fori_loop(0, ts // G, body_s, 0)
            if t > 0:
                m = slot(t - 1, b)
                ring[t - 1, b] = (
                    send(acc_y.at[i], ring_y.at[m], nxt), send(acc_s.at[i], ring_s.at[m], nxt)
                )
                sent.extend(ring[t - 1, b])

        summed(0)
        for i in range(1, nu):
            summed(i)
            passed(i - 1)
        passed(nu - 1)
        m = slot(0, "s")
        for copy in ring[0, "s"]:
            copy.wait_recv()
        far = (send(ring_y.at[m], far_y, sib), send(ring_s.at[m], far_s, sib))
        sent.extend(far)
        for copy in ring[0, "o"]:
            copy.wait_recv()
        n, i = slot(0, "o"), nu - 1
        far[1].wait_recv()

        def body_s(g, _):
            rows = pl.ds(pl.multiple_of(g * G, G), G)
            acc_s[i, rows] = acc_s[i, rows] + ring_s[n, rows] + far_s[rows]
            return 0

        lax.fori_loop(0, ts // G, body_s, 0)
        last = send(acc_s.at[i, :, far_cols], last_recv, other)
        sent.append(last)
        far[0].wait_recv()
        f32 = jnp.float32

        def body_y(g, _):
            rows = pl.ds(pl.multiple_of(g * G, G), G)
            total = acc_y[i, rows].astype(f32) + ring_y[n, rows].astype(f32) + far_y[rows].astype(f32)
            out_ref[rows] = (total + resid_ref[rows, own_cols].astype(f32)).astype(bf16)
            return 0

        lax.fori_loop(0, ty // G, body_y, 0)
        last.wait_recv()

        def body_l(g, _):
            rows = pl.ds(pl.multiple_of(g * G, G), G)
            here = pl.ds(pl.multiple_of(ty + g * G, G), G)
            total = acc_s[i, rows, own_cols].astype(f32) + last_recv[rows].astype(f32)
            out_ref[here] = (total + resid_ref[here, own_cols].astype(f32)).astype(bf16)
            return 0

        lax.fori_loop(0, ts // G, body_l, 0)
        for copy in sent:
            copy.wait_send()

    return pl.pallas_call(
        kernel,
        out_shape=jax.ShapeDtypeStruct((tall, half), bf16),
        in_specs=[pl.BlockSpec(memory_space=VMEM)] * 2,
        out_specs=pl.BlockSpec(memory_space=VMEM),
        scratch_shapes=[
            VMEM((nu, tall, wide), bf16),
            VMEM((nu, ty, half), bf16), VMEM((nu, ts, wide), bf16),
            VMEM((nu, ty, half), bf16), VMEM((nu, ty, half), bf16),
            VMEM((2 * HOPS, ty, half), bf16), VMEM((2 * HOPS, ts, wide), bf16),
            VMEM((ty, half), bf16), VMEM((ts, wide), bf16), VMEM((ts, half), bf16),
            pltpu.SemaphoreType.DMA((64,)), pltpu.SemaphoreType.DMA((64,)),
        ],
        compiler_params=pltpu.CompilerParams(
            collective_id=6, has_side_effects=True, vmem_limit_bytes=56 << 20
        ),
        name="collect_ring",
    )(partial, resid)


def attention(query, prefix_keys, prefix_values, suffix, bias):
    tall, wide = query.shape
    heads = wide // HD
    cached = prefix_keys.shape[0]
    keys = bias.shape[1]
    many = len(suffix)
    scale = HD ** (-0.5)

    def kernel(query_ref, cached_k, cached_v, bias_ref, *rest):
        suffix_k, suffix_v, out_ref = rest[:many], rest[many : 2 * many], rest[2 * many]
        head = query_ref[...]
        scores = [
            lax.dot_general(
                head, block[...], (((1,), (1,)), ((), ())), preferred_element_type=jnp.float32
            )
            for block in (cached_k, *suffix_k)
        ]
        scores = jnp.concatenate(scores, 1) * scale + bias_ref[...]
        weights = jnp.exp(scores - jnp.max(scores, -1, keepdims=True))
        total = jnp.sum(weights, -1, keepdims=True)
        weights = weights.astype(jnp.bfloat16)
        summed = jnp.dot(weights[:, :cached], cached_v[...], preferred_element_type=jnp.float32)
        for n, block in enumerate(suffix_v):
            start = cached + n * tall
            summed += jnp.dot(
                weights[:, start : start + tall], block[...], preferred_element_type=jnp.float32
            )
        out_ref[...] = (summed / total).astype(jnp.bfloat16)

    def column(rows, offset):
        return pl.BlockSpec((rows, HD), lambda h: (0, h + offset))

    return pl.pallas_call(
        kernel,
        out_shape=jax.ShapeDtypeStruct((tall, wide), jnp.bfloat16),
        grid=(heads,),
        in_specs=[column(tall, 0), column(cached, 0), column(cached, 0)]
        + [pl.BlockSpec((tall, keys), lambda h: (0, 0))]
        + [column(tall, 0)] * many
        + [column(tall, heads)] * many,
        out_specs=column(tall, 0),
        cost_estimate=pl.CostEstimate(
            flops=4 * tall * keys * wide, bytes_accessed=4 * keys * wide, transcendentals=0
        ),
        name="attention",
    )(query, prefix_keys, prefix_values, bias, *suffix, *suffix)


def on_device(
    tokens,
    attn_gain,
    w_query,
    w_key,
    w_value,
    w_out,
    prefix_keys,
    prefix_values,
    shard_group,
    request_group,
    lengths,
    moe_gain,
    w_router,
    w_gate,
    w_up,
    w_down,
    routes,
    final_gain,
    w_head,
):
    f32 = jnp.float32
    bf16 = jnp.bfloat16
    seq_index = lax.axis_index("seq")
    tp_index = lax.axis_index("tp")
    seq_count = lax.axis_size("seq")
    tp_count = lax.axis_size("tp")
    tok_dev = tokens.shape[0]
    width_part = tokens.shape[1]
    shard_rows = prefix_keys.shape[0]
    prefix_length = shard_rows * seq_count // 2
    full_x = gather_columns(tokens)
    width = full_x.shape[1]
    normed = normalize(full_x.astype(f32), attn_gain).astype(bf16)
    heads = w_query.shape[1] // HD
    ends = prefix_sums(lengths)
    starts = ends - lengths
    local_index = seq_index * tok_dev + jnp.arange(tok_dev)
    own_request = request_of(local_index, ends)
    own_start = lookup(own_request, starts)
    own_group = lookup(own_request, request_group)
    position = (prefix_length + local_index - own_start).astype(f32)
    query = rotate(
        jnp.dot(normed, w_query, preferred_element_type=f32).reshape(tok_dev, heads, HD), position
    ).astype(bf16)
    key_rows = rotate(
        jnp.dot(normed, w_key, preferred_element_type=f32).reshape(tok_dev, heads, HD), position
    ).astype(bf16)
    key_rows = key_rows.reshape(tok_dev, heads * HD)
    value_rows = jnp.dot(normed, w_value, preferred_element_type=f32).astype(bf16)
    pieces = (
        lax.all_gather(prefix_keys, "seq", axis=0, tiled=True),
        lax.all_gather(prefix_values, "seq", axis=0, tiled=True),
    )
    count = pieces[0].shape[0]
    shard_ids = jnp.arange(count) // shard_rows
    key_group = lookup(shard_ids, shard_group)
    fold_allowed = own_group[:, None] == key_group[None, :]
    own_allowed = (own_request[:, None] == own_request[None, :]) & (
        local_index[None, :] <= local_index[:, None]
    )
    both_rows = jnp.concatenate([key_rows, value_rows], 1)
    suffix = [both_rows] + [from_behind(both_rows, "seq", step) for step in range(1, SPAN + 1)]
    permitted = [fold_allowed, own_allowed]
    for step in range(1, SPAN + 1):
        key_index = (seq_index - step) * tok_dev + jnp.arange(tok_dev)
        key_request = request_of(key_index, ends)
        permitted.append(
            (key_index >= 0)[None, :] & (own_request[:, None] == key_request[None, :])
        )
    bias = jnp.where(jnp.concatenate(permitted, 1), 0.0, NEGATIVE)
    attended = attention(query.reshape(tok_dev, heads * HD), *pieces, suffix, bias)
    mixed = jnp.dot(attended, w_out, preferred_element_type=f32).astype(bf16)
    resid_full = (full_x.astype(f32) + sum_over_tp(mixed)).astype(bf16)
    moe_in = normalize(resid_full.astype(f32), moe_gain).astype(bf16)
    experts = w_router.shape[1]
    topk = routes.shape[1]
    probs = jax.nn.softmax(jnp.dot(moe_in, w_router, preferred_element_type=f32), -1)
    if seq_count == 16 and tp_count == 2 and experts == seq_count:
        named = routes[:, :, None] == jnp.arange(experts)[None, None, :]
        share = jnp.sum(jnp.where(named, probs[:, None, :], 0.0), 1)
        rows, shares = spread_ring(moe_in, share.T.reshape(experts, 1, tok_dev))
        own_share = shares.reshape(-1, 1)
        gate = jnp.dot(rows, w_gate[0], preferred_element_type=f32)
        up = jnp.dot(rows, w_up[0], preferred_element_type=f32)
        act = (jax.nn.silu(gate) * up).astype(bf16)
        partial_out = (jnp.dot(act, w_down[0], preferred_element_type=f32) * own_share).astype(bf16)
        hidden = collect_ring(partial_out, resid_full)
    else:
        flat = routes.reshape(-1)
        hits = (flat[:, None] == jnp.arange(experts)[None, :]).astype(jnp.int32)
        line = jnp.arange(flat.shape[0])
        before = (line[:, None] > line[None, :]).astype(bf16)
        earlier = jnp.dot(before, hits.astype(bf16), preferred_element_type=f32).astype(jnp.int32)
        rank = jnp.sum(earlier * hits, 1)
        capacity = min(tok_dev, tp_count * max(1, 3 * tok_dev * topk // (2 * experts * tp_count)))
        target = flat * capacity + rank
        route_weight = jnp.sum(hits.reshape(tok_dev, topk, experts).astype(f32) * probs[:, None, :], -1)
        repeated = jnp.repeat(moe_in, topk, axis=0)
        outgoing = (
            jnp.zeros((experts * capacity, width), bf16)
            .at[target]
            .set(repeated)
            .reshape(experts, capacity, width)
        )
        arrived = lax.all_to_all(outgoing, "seq", split_axis=0, concat_axis=0, tiled=True)
        sources = arrived.shape[0]
        count = arrived.shape[1]
        rows = arrived.reshape(sources * count, width)
        gate = jnp.dot(rows, w_gate[0], preferred_element_type=f32)
        up = jnp.dot(rows, w_up[0], preferred_element_type=f32)
        act = (jax.nn.silu(gate) * up).astype(bf16)
        partial_out = jnp.dot(act, w_down[0], preferred_element_type=f32).reshape(sources, count, width)
        summed = lax.psum_scatter(partial_out, "tp", scatter_dimension=2, tiled=True).astype(bf16)
        returned = lax.all_to_all(summed, "seq", split_axis=0, concat_axis=0, tiled=True)
        picked = returned.reshape(experts * capacity, width_part)[target].reshape(
            tok_dev, topk, width_part
        )
        moe_part = jnp.sum(picked.astype(f32) * route_weight[:, :, None], 1)
        resid = lax.dynamic_slice_in_dim(resid_full, tp_index * width_part, width_part, 1)
        hidden = (resid.astype(f32) + moe_part).astype(bf16)
    last_hit = ((ends - 1)[:, None] == local_index[None, :]).astype(bf16)
    chosen = jnp.dot(last_hit, hidden, preferred_element_type=f32)
    final = last_rows(chosen, final_gain, width)
    log_probs = log_softmax(jnp.dot(final, w_head, preferred_element_type=f32))
    return (hidden, log_probs)


def solution(mesh):
    in_specs = (
        P("seq", "tp"),
        P(),
        P(None, "tp"),
        P(None, "tp"),
        P(None, "tp"),
        P("tp", None),
        P("seq", "tp"),
        P("seq", "tp"),
        P(),
        P(),
        P(),
        P(),
        P(),
        P("seq", None, "tp"),
        P("seq", None, "tp"),
        P("seq", "tp", None),
        P("seq", None),
        P("tp"),
        P("tp", "seq"),
    )
    out_specs = (P("seq", "tp"), P(None, "seq"))
    return jax.shard_map(
        on_device, mesh=mesh, in_specs=in_specs, out_specs=out_specs, check_vma=False
    )
```

```python
import jax
import jax.numpy as jnp
from jax import lax
from jax.experimental import pallas as pl
from jax.experimental.pallas import tpu as pltpu
from jax.sharding import PartitionSpec as P

HD = 128
SPAN = 4
VMEM = pltpu.VMEM


EPS = 1e-05
NEGATIVE = -1e30


def from_behind(value, axis, steps):
    count = lax.axis_size(axis)
    leading, last = (max(0, -steps), min(count, count - steps))
    return lax.ppermute(value, axis, [(source, source + steps) for source in range(leading, last)])


def normalize(rows, gain):
    inv = lax.rsqrt(jnp.mean(rows * rows, -1, keepdims=True) + EPS)
    return rows * inv * gain.astype(jnp.float32)


def rotate(vectors, position):
    half = vectors.shape[-1] // 2
    freq = 10000.0 ** (-jnp.arange(half).astype(jnp.float32) / half)
    angle = position[:, None] * freq[None, :]
    cosine = jnp.cos(angle)[:, None, :]
    sine = jnp.sin(angle)[:, None, :]
    first = vectors[..., :half]
    second = vectors[..., half:]
    return jnp.concatenate([first * cosine - second * sine, second * cosine + first * sine], -1)


def request_of(index, ends):
    return jnp.sum((index[:, None] >= ends[None, :]).astype(jnp.int32), 1)


def lookup(selector, table):
    hit = selector[:, None] == jnp.arange(table.shape[0])[None, :]
    return jnp.sum(jnp.where(hit, table[None, :], 0), 1)


def prefix_sums(values):
    order = jnp.arange(values.shape[0])
    return jnp.sum(jnp.where(order[:, None] >= order[None, :], values[None, :], 0), 1)


def partner(axis, bit):
    index = lax.axis_index(axis)
    span = 1 << bit
    other = index + span - 2 * span * ((index // span) % 2)
    return {axis: other}


def greet(stages):
    barrier = pltpu.get_barrier_semaphore()
    for axis, bit in stages:
        pl.semaphore_signal(barrier, inc=1, device_id=partner(axis, bit))
    pl.semaphore_wait(barrier, len(stages))


def swap(source, target, send_sem, recv_sem, stage):
    copy = pltpu.make_async_remote_copy(
        src_ref=source, dst_ref=target, send_sem=send_sem, recv_sem=recv_sem,
        device_id=partner(*stage),
    )
    copy.start()
    return copy


def bits_of(axis):
    return [(axis, bit) for bit in range(lax.axis_size(axis).bit_length() - 1)]


def last_rows(chosen, gain, width):
    seq_stages, tp_stages = bits_of("seq"), bits_of("tp")
    stages = seq_stages + tp_stages
    rows, part = chosen.shape

    def kernel(chosen_ref, gain_ref, out_ref, held, got, sq_held, sq_got, send_sem, recv_sem):
        greet(stages)
        held[0] = chosen_ref[...]
        count = len(seq_stages)
        for k, stage in enumerate(seq_stages):
            swap(held.at[k], got.at[k], send_sem.at[k], recv_sem.at[k], stage).wait()
            held[k + 1] = held[k] + got[k]
        total = held[count]
        sq_held[0] = jnp.broadcast_to(jnp.sum(total * total, -1, keepdims=True), (rows, 128))
        for k, stage in enumerate(tp_stages):
            n = count + k
            swap(sq_held.at[k], sq_got.at[k], send_sem.at[n], recv_sem.at[n], stage).wait()
            sq_held[k + 1] = sq_held[k] + sq_got[k]
        square = sq_held[len(tp_stages)][:, :1]
        scaled = total * lax.rsqrt(square / width + EPS) * gain_ref[...].astype(jnp.float32)
        out_ref[...] = scaled.astype(jnp.bfloat16)

    ns, nt = len(seq_stages), len(tp_stages)
    return pl.pallas_call(
        kernel,
        out_shape=jax.ShapeDtypeStruct((rows, part), jnp.bfloat16),
        in_specs=[pl.BlockSpec(memory_space=VMEM)] * 2,
        out_specs=pl.BlockSpec(memory_space=VMEM),
        scratch_shapes=[
            VMEM((ns + 1, rows, part), jnp.float32),
            VMEM((ns, rows, part), jnp.float32),
            VMEM((nt + 1, rows, 128), jnp.float32),
            VMEM((nt, rows, 128), jnp.float32),
            pltpu.SemaphoreType.DMA((ns + nt,)),
            pltpu.SemaphoreType.DMA((ns + nt,)),
        ],
        compiler_params=pltpu.CompilerParams(collective_id=1, has_side_effects=True),
        name="last_rows",
    )(chosen, gain.reshape(1, part))


def log_softmax(logits):
    seq_stages, tp_stages = bits_of("seq"), bits_of("tp")
    stages = tp_stages + seq_stages
    rows, part = logits.shape

    def kernel(logits_ref, out_ref, held, got, st_held, st_got, send_sem, recv_sem):
        greet(stages)
        held[0] = logits_ref[...]
        count = len(tp_stages)
        for k, stage in enumerate(tp_stages):
            swap(held.at[k], got.at[k], send_sem.at[k], recv_sem.at[k], stage).wait()
            held[k + 1] = held[k] + got[k]
        total = held[count]
        peak = jnp.max(total, -1, keepdims=True)
        mass = jnp.sum(jnp.exp(total - peak), -1, keepdims=True)
        st_held[0, :, :128] = jnp.broadcast_to(peak, (rows, 128))
        st_held[0, :, 128:] = jnp.broadcast_to(mass, (rows, 128))
        for k, stage in enumerate(seq_stages):
            n = count + k
            swap(st_held.at[k], st_got.at[k], send_sem.at[n], recv_sem.at[n], stage).wait()
            mine, theirs = st_held[k, :, :128], st_got[k, :, :128]
            top = jnp.maximum(mine, theirs)
            st_held[k + 1, :, :128] = top
            st_held[k + 1, :, 128:] = st_held[k, :, 128:] * jnp.exp(mine - top) + st_got[
                k, :, 128:
            ] * jnp.exp(theirs - top)
        last = len(seq_stages)
        out_ref[...] = total - st_held[last, :, :1] - jnp.log(st_held[last, :, 128:129])

    ns, nt = len(seq_stages), len(tp_stages)
    return pl.pallas_call(
        kernel,
        out_shape=jax.ShapeDtypeStruct((rows, part), jnp.float32),
        in_specs=[pl.BlockSpec(memory_space=VMEM)],
        out_specs=pl.BlockSpec(memory_space=VMEM),
        scratch_shapes=[
            VMEM((nt + 1, rows, part), jnp.float32),
            VMEM((nt, rows, part), jnp.float32),
            VMEM((ns + 1, rows, 256), jnp.float32),
            VMEM((ns, rows, 256), jnp.float32),
            pltpu.SemaphoreType.DMA((ns + nt,)),
            pltpu.SemaphoreType.DMA((ns + nt,)),
        ],
        compiler_params=pltpu.CompilerParams(collective_id=2, has_side_effects=True),
        name="log_softmax",
    )(logits)


def gather_columns(block):
    stages = bits_of("tp")
    rows, part = block.shape
    count = lax.axis_size("tp")

    def kernel(block_ref, out_ref, send_sem, recv_sem):
        greet(stages)
        me = lax.axis_index("tp")
        out_ref[:, pl.ds(pl.multiple_of(me * part, part), part)] = block_ref[...]
        for k, stage in enumerate(stages):
            wide = part << k
            start = pl.multiple_of((me // (1 << k)) * wide, wide)
            piece = out_ref.at[:, pl.ds(start, wide)]
            swap(piece, piece, send_sem.at[k], recv_sem.at[k], stage).wait()

    return pl.pallas_call(
        kernel,
        out_shape=jax.ShapeDtypeStruct((rows, part * count), block.dtype),
        in_specs=[pl.BlockSpec(memory_space=VMEM)],
        out_specs=pl.BlockSpec(memory_space=VMEM),
        scratch_shapes=[pltpu.SemaphoreType.DMA((len(stages),))] * 2,
        compiler_params=pltpu.CompilerParams(collective_id=3, has_side_effects=True),
        name="gather_columns",
    )(block)


def sum_over_tp(block):
    stages = bits_of("tp")
    rows, part = block.shape

    def kernel(block_ref, out_ref, held, got, send_sem, recv_sem):
        greet(stages)
        for k, stage in enumerate(stages):
            source = block_ref if k == 0 else held.at[k]
            swap(source, got.at[k], send_sem.at[k], recv_sem.at[k], stage).wait()
            total = source[...].astype(jnp.float32) + got[k].astype(jnp.float32)
            if k + 1 < len(stages):
                held[k + 1] = total.astype(jnp.bfloat16)
            else:
                out_ref[...] = total

    count = len(stages)
    return pl.pallas_call(
        kernel,
        out_shape=jax.ShapeDtypeStruct((rows, part), jnp.float32),
        in_specs=[pl.BlockSpec(memory_space=VMEM)],
        out_specs=pl.BlockSpec(memory_space=VMEM),
        scratch_shapes=[
            VMEM((count, rows, part), jnp.bfloat16),
            VMEM((count, rows, part), jnp.bfloat16),
            pltpu.SemaphoreType.DMA((count,)),
            pltpu.SemaphoreType.DMA((count,)),
        ],
        compiler_params=pltpu.CompilerParams(collective_id=4, has_side_effects=True),
        name="sum_over_tp",
    )(block)


HOPS = 4


def ring_place():
    s = lax.axis_index("seq")
    core = s % 2
    x = (s // 2) % 2
    z = s // 4
    return s, core, z + x * (7 - 2 * z)


def chip_at(place):
    q = (place + 16) % 8
    x = q // 4
    z = q + x * (7 - 2 * q)
    return z * 2 + x


def greet_all(blocks):
    s = lax.axis_index("seq")
    barrier = pltpu.get_barrier_semaphore()
    for d in range(1, blocks):
        pl.semaphore_signal(barrier, inc=1, device_id={"seq": (s + d) % blocks})
    pl.semaphore_signal(barrier, inc=1, device_id={"tp": 1 - lax.axis_index("tp")})
    pl.semaphore_wait(barrier, blocks)


def greet_ring(nxt, prv, sib):
    barrier = pltpu.get_barrier_semaphore()
    for d in ({"seq": nxt}, {"seq": prv}, {"seq": sib}, {"tp": 1 - lax.axis_index("tp")}):
        pl.semaphore_signal(barrier, inc=1, device_id=d)
    pl.semaphore_wait(barrier, 4)


def spread_ring(rows, share):
    tall, wide = rows.shape
    blocks = share.shape[0]
    q = tall // 4

    def kernel(rows_ref, share_ref, out_ref, share_out, send_sem, recv_sem, sh_send, sh_recv):
        s, core, r = ring_place()
        y = lax.axis_index("tp")
        step = 1 - 2 * core
        nxt = {"seq": chip_at(r + step) * 2 + core}
        sib = {"seq": s + step}
        other = {"tp": 1 - y}
        out_ref[pl.ds(pl.multiple_of(s * tall, tall), tall)] = rows_ref[...]
        share_out[s] = share_ref[s]
        greet_all(blocks)
        mine, theirs = core * tall, (1 - core) * tall
        spot = {
            "eo": (mine + 2 * q, 2 * q),
            "ao": (mine + q * ((core + y) % 2), q),
            "as": (theirs + q * ((1 - core + y) % 2), q),
            "es": (theirs + 2 * q, 2 * q),
            "yao": (mine + q * ((core + 1 - y) % 2), q),
            "yas": (theirs + q * ((2 - core - y) % 2), q),
        }
        used = iter(range(64))

        def send(start, size, device):
            piece = out_ref.at[pl.ds(pl.multiple_of(start, q), size)]
            n = next(used)
            copy = pltpu.make_async_remote_copy(
                src_ref=piece, dst_ref=piece, send_sem=send_sem.at[n], recv_sem=recv_sem.at[n],
                device_id=device,
            )
            copy.start()
            return copy

        ring, cross, pair, shares = {}, {}, {}, []
        pair[0] = send(s * tall, tall, sib)
        home = chip_at(r) * 2 * tall

        def put(table, key, base, name, device):
            table[key] = send(base + spot[name][0], spot[name][1], device)

        for p in ("eo", "ao"):
            put(ring, (1, p), home, p, nxt)
        pair[0].wait_recv()
        for p in ("as", "es"):
            put(ring, (1, p), home, p, nxt)
        for d in range(1, blocks):
            dest = (s + d) % blocks
            copy = pltpu.make_async_remote_copy(
                src_ref=share_ref.at[dest], dst_ref=share_out.at[s], send_sem=sh_send.at[d],
                recv_sem=sh_recv.at[d], device_id={"seq": dest},
            )
            copy.start()
            shares.append(copy)
        full, part = ("eo", "ao", "as", "es"), ("eo", "ao")
        late = []
        for t in range(1, HOPS + 1):
            base = chip_at(r - step * t) * 2 * tall
            onward = full if t < HOPS - 1 else part if t == HOPS - 1 else ()
            here = full if t < HOPS else part
            for p in here:
                ring[t, p].wait_recv()
                if p in onward:
                    put(ring, (t + 1, p), base, p, nxt)
                if p in ("ao", "as"):
                    put(cross, (t, p), base, p, other)
                put(pair, (t, p), base, p, sib)
            for act in late:
                act()
            late = []
            for p in here:
                if p in ("ao", "as"):
                    def act(t=t, p=p, base=base):
                        cross[t, p].wait_recv()
                        put(pair, (t, "y" + p), base, "y" + p, sib)
                    late.append(act)
        for act in late:
            act()
        for key, copy in pair.items():
            if key != 0:
                copy.wait_recv()
        for table in (ring, cross, pair):
            for copy in table.values():
                copy.wait_send()
        for copy in shares:
            copy.wait()

    return pl.pallas_call(
        kernel,
        out_shape=(
            jax.ShapeDtypeStruct((blocks * tall, wide), rows.dtype),
            jax.ShapeDtypeStruct((blocks, 1, tall), share.dtype),
        ),
        in_specs=[pl.BlockSpec(memory_space=VMEM)] * 2,
        out_specs=(pl.BlockSpec(memory_space=VMEM), pl.BlockSpec(memory_space=VMEM)),
        scratch_shapes=[pltpu.SemaphoreType.DMA((64,)), pltpu.SemaphoreType.DMA((64,)),
                        pltpu.SemaphoreType.DMA((blocks,)), pltpu.SemaphoreType.DMA((blocks,))],
        compiler_params=pltpu.CompilerParams(
            collective_id=5, has_side_effects=True, vmem_limit_bytes=40 << 20
        ),
        name="spread_ring",
    )(rows, share)


def collect_ring(partial, resid):
    tall, wide = resid.shape
    half = wide // 2
    ty = tall * 5 // 8
    ts = tall - ty
    bf16 = jnp.bfloat16
    G = 16
    units = [(HOPS, "o")] + [(t, b) for t in range(HOPS - 1, 0, -1) for b in ("s", "o")] + [(0, "o")]
    nu = len(units)

    def kernel(part_ref, resid_ref, out_ref, sib_buf, acc_y, acc_s, y_send, y_recv, ring_y, ring_s,
               far_y, far_s, last_recv, send_sem, recv_sem):
        s, core, r = ring_place()
        y = lax.axis_index("tp")
        step = 1 - 2 * core
        nxt = {"seq": chip_at(r + step) * 2 + core}
        sib = {"seq": s + step}
        other = {"tp": 1 - y}
        greet_ring(nxt["seq"], chip_at(r - step) * 2 + core, sib["seq"])
        used = iter(range(64))
        own_cols = pl.ds(pl.multiple_of(y * half, half), half)
        far_cols = pl.ds(pl.multiple_of((1 - y) * half, half), half)

        def send(source, target, device):
            n = next(used)
            copy = pltpu.make_async_remote_copy(
                src_ref=source, dst_ref=target, send_sem=send_sem.at[n], recv_sem=recv_sem.at[n],
                device_id=device,
            )
            copy.start()
            return copy

        def rows_of(t, b, direction, c):
            place = chip_at(r + direction * t) * 2 + (c if b == "o" else 1 - c)
            return place * tall

        pair = []
        for i, (t, b) in enumerate(units):
            start = pl.multiple_of(rows_of(t, b, -step, 1 - core), tall)
            pair.append(send(part_ref.at[pl.ds(start, tall)], sib_buf.at[i], sib))
        cross, ring, sent = {}, {}, list(pair)

        def summed(i):
            t, b = units[i]
            start = rows_of(t, b, step, core)
            pair[i].wait_recv()

            def body_y(g, _):
                rows = pl.ds(pl.multiple_of(g * G, G), G)
                here = pl.ds(pl.multiple_of(start + g * G, G), G)
                y_send[i, rows] = part_ref[here, far_cols] + sib_buf[i, rows, far_cols]
                acc_y[i, rows] = part_ref[here, own_cols] + sib_buf[i, rows, own_cols]
                return 0

            lax.fori_loop(0, ty // G, body_y, 0)
            cross[i] = send(y_send.at[i], y_recv.at[i], other)
            sent.append(cross[i])

            def body_s(g, _):
                rows = pl.ds(pl.multiple_of(g * G, G), G)
                below = pl.ds(pl.multiple_of(ty + g * G, G), G)
                here = pl.ds(pl.multiple_of(start + ty + g * G, G), G)
                acc_s[i, rows] = part_ref[here] + sib_buf[i, below]
                return 0

            lax.fori_loop(0, ts // G, body_s, 0)

        def slot(t, b):
            return 2 * t + (0 if b == "o" else 1)

        def passed(i):
            t, b = units[i]
            cross[i].wait_recv()
            arrived = (t + 1, b) in units and t > 0
            if arrived:
                for copy in ring[t, b]:
                    copy.wait_recv()
            n = slot(t, b)

            def body_y(g, _):
                rows = pl.ds(pl.multiple_of(g * G, G), G)
                total = acc_y[i, rows] + y_recv[i, rows]
                if arrived:
                    total = total + ring_y[n, rows]
                acc_y[i, rows] = total
                return 0

            lax.fori_loop(0, ty // G, body_y, 0)
            if arrived:
                def body_s(g, _):
                    rows = pl.ds(pl.multiple_of(g * G, G), G)
                    acc_s[i, rows] = acc_s[i, rows] + ring_s[n, rows]
                    return 0

                lax.fori_loop(0, ts // G, body_s, 0)
            if t > 0:
                m = slot(t - 1, b)
                ring[t - 1, b] = (
                    send(acc_y.at[i], ring_y.at[m], nxt), send(acc_s.at[i], ring_s.at[m], nxt)
                )
                sent.extend(ring[t - 1, b])

        summed(0)
        for i in range(1, nu):
            summed(i)
            passed(i - 1)
        passed(nu - 1)
        m = slot(0, "s")
        for copy in ring[0, "s"]:
            copy.wait_recv()
        far = (send(ring_y.at[m], far_y, sib), send(ring_s.at[m], far_s, sib))
        sent.extend(far)
        for copy in ring[0, "o"]:
            copy.wait_recv()
        n, i = slot(0, "o"), nu - 1
        far[1].wait_recv()

        def body_s(g, _):
            rows = pl.ds(pl.multiple_of(g * G, G), G)
            acc_s[i, rows] = acc_s[i, rows] + ring_s[n, rows] + far_s[rows]
            return 0

        lax.fori_loop(0, ts // G, body_s, 0)
        last = send(acc_s.at[i, :, far_cols], last_recv, other)
        sent.append(last)
        far[0].wait_recv()
        f32 = jnp.float32

        def body_y(g, _):
            rows = pl.ds(pl.multiple_of(g * G, G), G)
            total = acc_y[i, rows].astype(f32) + ring_y[n, rows].astype(f32) + far_y[rows].astype(f32)
            out_ref[rows] = (total + resid_ref[rows, own_cols].astype(f32)).astype(bf16)
            return 0

        lax.fori_loop(0, ty // G, body_y, 0)
        last.wait_recv()

        def body_l(g, _):
            rows = pl.ds(pl.multiple_of(g * G, G), G)
            here = pl.ds(pl.multiple_of(ty + g * G, G), G)
            total = acc_s[i, rows, own_cols].astype(f32) + last_recv[rows].astype(f32)
            out_ref[here] = (total + resid_ref[here, own_cols].astype(f32)).astype(bf16)
            return 0

        lax.fori_loop(0, ts // G, body_l, 0)
        for copy in sent:
            copy.wait_send()

    return pl.pallas_call(
        kernel,
        out_shape=jax.ShapeDtypeStruct((tall, half), bf16),
        in_specs=[pl.BlockSpec(memory_space=VMEM)] * 2,
        out_specs=pl.BlockSpec(memory_space=VMEM),
        scratch_shapes=[
            VMEM((nu, tall, wide), bf16),
            VMEM((nu, ty, half), bf16), VMEM((nu, ts, wide), bf16),
            VMEM((nu, ty, half), bf16), VMEM((nu, ty, half), bf16),
            VMEM((2 * HOPS, ty, half), bf16), VMEM((2 * HOPS, ts, wide), bf16),
            VMEM((ty, half), bf16), VMEM((ts, wide), bf16), VMEM((ts, half), bf16),
            pltpu.SemaphoreType.DMA((64,)), pltpu.SemaphoreType.DMA((64,)),
        ],
        compiler_params=pltpu.CompilerParams(
            collective_id=6, has_side_effects=True, vmem_limit_bytes=56 << 20
        ),
        name="collect_ring",
    )(partial, resid)


def head_tail(hidden, lengths, gain, w_head):
    tall, part = hidden.shape
    reqs = lengths.shape[0]
    cols = w_head.shape[1]
    width = 2 * part
    wide = -(-cols // 128) * 128
    bf16, f32 = jnp.bfloat16, jnp.float32
    cuts = 4
    high = -(-reqs // 16) * 16
    per = -(-cols // (16 * cuts)) * 16
    spans = [(k * per, min(per, cols - k * per)) for k in range(cuts)]

    def kernel(len_ref, hid_ref, gain_ref, w_ref, out_ref, w_buf, near, far, logit, got, stat, stats,
               w_sem, send_sem, recv_sem):
        load = pltpu.make_async_copy(w_ref, w_buf, w_sem)
        load.start()
        s = lax.axis_index("seq")
        y = lax.axis_index("tp")
        count = 16
        barrier = pltpu.get_barrier_semaphore()
        for d in range(1, count):
            pl.semaphore_signal(barrier, inc=1, device_id={"seq": (s + d) % count})
        pl.semaphore_signal(barrier, inc=1, device_id={"tp": 1 - y})
        row = lax.broadcasted_iota(jnp.int32, (high, tall), 0)
        place = lax.broadcasted_iota(jnp.int32, (high, tall), 1) + s * tall
        last = jnp.full((high, tall), -1, jnp.int32)
        end = 0
        for j in range(reqs):
            end = end + len_ref[j]
            last = jnp.where(row == j, end - 1, last)
        hit = (last == place).astype(f32).astype(bf16)
        near[0] = jnp.dot(hit, hid_ref[...], preferred_element_type=f32).astype(bf16)
        pl.semaphore_wait(barrier, count)
        used = iter(range(32))
        sent = []

        def send(source, target, device):
            n = next(used)
            copy = pltpu.make_async_remote_copy(
                src_ref=source, dst_ref=target, send_sem=send_sem.at[n], recv_sem=recv_sem.at[n],
                device_id=device,
            )
            copy.start()
            sent.append(copy)
            return copy

        first = [
            send(near.at[0], near.at[d], {"seq": (s // 4) * 4 + (s + d) % 4}) for d in range(1, 4)
        ]
        for copy in first:
            copy.wait_recv()
        far[0] = (near[0] + near[1]) + (near[2] + near[3])
        second = [send(far.at[0], far.at[d], {"seq": (s + 4 * d) % count}) for d in range(1, 4)]
        for copy in second:
            copy.wait_recv()
        total = ((far[0] + far[1]) + (far[2] + far[3])).astype(f32)
        square = jnp.sum(total * total, -1, keepdims=True)
        scaled = (total * gain_ref[...].astype(f32)).astype(bf16)
        logit[:, wide:] = jnp.broadcast_to(square[:reqs], (reqs, 128))
        load.wait()
        for k, (start, size) in enumerate(spans):
            product = lax.dot_general(
                scaled, w_buf[start : start + size], (((1,), (1,)), ((), ())), preferred_element_type=f32
            )
            logit[:, start : start + size] = product[:reqs]
        send(logit, got, {"tp": 1 - y}).wait_recv()
        square = logit[:, wide : wide + 1] + got[:, wide : wide + 1]
        inv = lax.rsqrt(square / width + EPS)
        both = (logit[:, :cols] + got[:, :cols]) * inv
        peak = jnp.max(both, -1, keepdims=True)
        mass = jnp.sum(jnp.exp(both - peak), -1, keepdims=True)
        lane = lax.broadcasted_iota(jnp.int32, (reqs, 128), 1)
        stat[...] = jnp.where(lane < 64, peak, mass)
        stats[0] = stat[...]
        third = [send(stat, stats.at[d], {"seq": (s + d) % count}) for d in range(1, count)]
        for copy in third:
            copy.wait_recv()
        everyone = stats[...]
        peaks, masses = everyone[:, :, :1], everyone[:, :, 64:65]
        top = jnp.max(peaks, 0)
        whole = jnp.sum(masses * jnp.exp(peaks - top[None]), 0)
        out_ref[...] = both - top - jnp.log(whole)
        for copy in sent:
            copy.wait_send()

    return pl.pallas_call(
        kernel,
        out_shape=jax.ShapeDtypeStruct((reqs, cols), f32),
        in_specs=[pl.BlockSpec(memory_space=pltpu.SMEM)]
        + [pl.BlockSpec(memory_space=VMEM)] * 2
        + [pl.BlockSpec(memory_space=pl.ANY)],
        out_specs=pl.BlockSpec(memory_space=VMEM),
        scratch_shapes=[
            VMEM((cols, part), bf16),
            VMEM((4, high, part), bf16),
            VMEM((4, high, part), bf16),
            VMEM((reqs, wide + 128), f32),
            VMEM((reqs, wide + 128), f32),
            VMEM((reqs, 128), f32),
            VMEM((16, reqs, 128), f32),
            pltpu.SemaphoreType.DMA,
            pltpu.SemaphoreType.DMA((32,)),
            pltpu.SemaphoreType.DMA((32,)),
        ],
        compiler_params=pltpu.CompilerParams(
            collective_id=7, has_side_effects=True, vmem_limit_bytes=24 << 20
        ),
        name="head_tail",
    )(lengths, hidden, gain.reshape(1, part), w_head.T)


def front(tokens, gain, w_query, w_key, w_value, w_out, prefix_keys, prefix_values, lengths,
          request_group, shard_group, cosine, sine, moe_gain, w_router, routes):
    tall, part = tokens.shape
    width = 2 * part
    local = w_query.shape[1]
    shard = prefix_keys.shape[0]
    shards = shard_group.shape[0]
    reqs = lengths.shape[0]
    cached = shard * shards
    experts = w_router.shape[1]
    topk = routes.shape[1]
    bf16, f32 = jnp.bfloat16, jnp.float32
    pair = 2 * HD
    groups = local // pair
    slots = SPAN + 1
    near = slots * tall
    cuts = 4
    piece = width // cuts
    scale = HD ** (-0.5)
    nt = (((1,), (1,)), ((), ()))

    def kernel(len_ref, rg_ref, sg_ref, tok_ref, gain_ref, cos_ref, sin_ref, pk_ref, pv_ref, mg_ref,
               wr_ref, routes_ref, wq_ref, wk_ref, wv_ref, wo_ref, resid_ref, moe_ref, share_ref,
               wq, wk, wv, wo, x, normed, cache, kv, query, attended, bias, mix, mix_got, w_sem, send_sem,
               recv_sem):
        loads = {}
        for n, (source, target) in enumerate(((wk_ref, wk), (wv_ref, wv), (wq_ref, wq), (wo_ref, wo))):
            loads[n] = pltpu.make_async_copy(source, target, w_sem.at[n])
            loads[n].start()
        s, core, r = ring_place()
        y = lax.axis_index("tp")
        count = 16
        step = 1 - 2 * core
        ahead = 1 - 2 * ((s // 2) % 2)
        nxt = {"seq": chip_at(r + step) * 2 + core}
        sib = {"seq": s + step}
        side = {"seq": s + 2 * ahead}
        above = {"seq": (s + 4) % count}
        other = {"tp": 1 - y}
        own_cols = pl.ds(pl.multiple_of(y * part, part), part)
        x[:, own_cols] = tok_ref[...]
        own_rows = pl.ds(pl.multiple_of(s * shard, shard), shard)
        cache[0, own_rows] = pk_ref[...]
        cache[1, own_rows] = pv_ref[...]
        greet_all(count)
        used = iter(range(128))
        sent = []

        def send(source, target, device):
            n = next(used)
            copy = pltpu.make_async_remote_copy(
                src_ref=source, dst_ref=target, send_sem=send_sem.at[n], recv_sem=recv_sem.at[n],
                device_id=device,
            )
            copy.start()
            sent.append(copy)
            return copy

        def move(chip, name, device):
            which, owner = name
            shift = core if owner == "o" else 1 - core
            rows = pl.ds(pl.multiple_of((chip * 2 + shift) * shard, shard), shard)
            view = cache.at[which, rows]
            return send(view, view, device)

        home = chip_at(r)
        swapped = [move(home, (which, "o"), sib) for which in range(2)]
        ring, twin = {}, {}
        for which in range(2):
            ring[1, (which, "o")] = move(home, (which, "o"), nxt)
        crossing = send(tok_ref, x.at[:, own_cols], other)
        for which in range(2):
            swapped[which].wait_recv()
            ring[1, (which, "s")] = move(home, (which, "s"), nxt)

        def hop(t):
            chip = chip_at(r - step * t)
            owners = ("o", "s") if t < HOPS else ("o",)
            for owner in owners:
                for which in range(2):
                    name = (which, owner)
                    ring[t, name].wait_recv()
                    if t < HOPS - 1 or (t == HOPS - 1 and owner == "o"):
                        ring[t + 1, name] = move(chip, name, nxt)
                    twin[t, name] = move(chip, name, sib)

        lane = lax.broadcasted_iota(jnp.int32, (tall, 128), 0) + s * tall
        mine = jnp.zeros((tall, 128), jnp.int32)
        ends, end = [], 0
        for j in range(reqs):
            end = end + len_ref[j]
            ends.append(end)
        for j in range(reqs):
            mine = mine + (lane >= ends[j]).astype(jnp.int32)
        group = jnp.zeros((tall, 128), jnp.int32)
        for j in range(reqs):
            group = jnp.where(mine == j, rg_ref[j], group)
        own_index, own_request, own_group = lane[:, :1], mine[:, :1], group[:, :1]
        column = lax.broadcasted_iota(jnp.int32, (8, cached), 1)
        key_group = jnp.zeros((8, cached), jnp.int32)
        for j in range(shards):
            inside = (column >= j * shard) & (column < (j + 1) * shard)
            key_group = jnp.where(inside, sg_ref[j], key_group)
        bias[:, :cached] = jnp.where(own_group == key_group[:1], 0.0, NEGATIVE)
        chip = s // 2
        bases = (
            s * tall, (chip - 1) * 2 * tall, (chip - 1) * 2 * tall + tall, (chip - 2) * 2 * tall + tall,
            (chip - 2 + 2 * core) * 2 * tall,
        )
        for n in range(slots):
            place = lax.broadcasted_iota(jnp.int32, (8, tall), 1) + bases[n]
            theirs = jnp.zeros((8, tall), jnp.int32)
            for j in range(reqs):
                theirs = theirs + (place >= ends[j]).astype(jnp.int32)
            seen = (own_request == theirs[:1]) & (place[:1] <= own_index) & (place[:1] >= 0)
            start = cached + n * tall
            bias[:, start : start + tall] = jnp.where(seen, 0.0, NEGATIVE)
        hop(1)
        crossing.wait_recv()
        rows = x[...].astype(f32)
        inv = lax.rsqrt(jnp.mean(rows * rows, -1, keepdims=True) + EPS)
        normed[...] = (rows * inv * gain_ref[...].astype(f32)).astype(bf16)

        def turned(value):
            heads = []
            for n in range(pair // HD):
                head = value[:, n * HD : (n + 1) * HD]
                heads.append(head * cos_ref[...] + pltpu.roll(head, HD // 2, 1) * sin_ref[...])
            return jnp.concatenate(heads, 1).astype(bf16)

        back = 4 - core
        side_slot = 1 + core

        def slot_of(g, n):
            return kv.at[g, pl.ds(pl.multiple_of(n * tall, tall), tall)]

        up = {}

        def keys_of(g):
            cols = slice(g * pair, (g + 1) * pair)
            key = jnp.dot(normed[...], wk[:, cols], preferred_element_type=f32)
            kv[g, :tall, :pair] = turned(key)
            value = jnp.dot(normed[...], wv[:, cols], preferred_element_type=f32)
            kv[g, :tall, pair:] = value.astype(bf16)
            up[g] = send(slot_of(g, 0), slot_of(g, back), above)

        loads[0].wait()
        loads[1].wait()
        keys_of(0)
        hop(2)
        keys_of(1)
        hop(3)
        for g in range(2, groups):
            keys_of(g)
        loads[2].wait()
        for g in range(groups):
            cols = slice(g * pair, (g + 1) * pair)
            query[:, cols] = turned(jnp.dot(normed[...], wq[:, cols], preferred_element_type=f32))
        hop(4)
        across, down, inner = {}, {}, {}
        for g in range(groups):
            up[g].wait_recv()
            across[g] = send(slot_of(g, (1 - ahead) // 2 * back), slot_of(g, side_slot), side)
            inner[g] = send(slot_of(g, 3 * core), slot_of(g, back), sib)
        for copy in twin.values():
            copy.wait_recv()
        for g in range(groups):
            across[g].wait_recv()
            down[g] = send(slot_of(g, side_slot), slot_of(g, side_slot), sib)
        for g in range(groups):
            inner[g].wait_recv()
            down[g].wait_recv()
            for n in range(pair // HD):
                cols = slice(g * pair + n * HD, g * pair + (n + 1) * HD)
                k_cols = slice(n * HD, (n + 1) * HD)
                v_cols = slice(pair + n * HD, pair + (n + 1) * HD)
                head = query[:, cols]
                scores = jnp.concatenate(
                    [
                        lax.dot_general(head, cache[0, :, cols], nt, preferred_element_type=f32),
                        lax.dot_general(head, kv[g, :, k_cols], nt, preferred_element_type=f32),
                    ],
                    1,
                )
                scores = scores * scale + bias[...]
                weights = jnp.exp(scores - jnp.max(scores, -1, keepdims=True))
                total = jnp.sum(weights, -1, keepdims=True)
                weights = weights.astype(bf16)
                summed = jnp.dot(weights[:, :cached], cache[1, :, cols], preferred_element_type=f32)
                summed += jnp.dot(weights[:, cached:], kv[g, :, v_cols], preferred_element_type=f32)
                attended[:, cols] = (summed / total).astype(bf16)
        loads[3].wait()
        mixed = []
        for n in range(cuts):
            cols = slice(n * piece, (n + 1) * piece)
            mix[n] = jnp.dot(attended[...], wo[:, cols], preferred_element_type=f32).astype(bf16)
            mixed.append(send(mix.at[n], mix_got.at[n], other))
        square = jnp.zeros((tall, 1), f32)
        for n in range(cuts):
            cols = slice(n * piece, (n + 1) * piece)
            mixed[n].wait_recv()
            total = x[:, cols].astype(f32) + (mix[n].astype(f32) + mix_got[n].astype(f32))
            total = total.astype(bf16)
            resid_ref[:, cols] = total
            wide = total.astype(f32)
            square += jnp.sum(wide * wide, -1, keepdims=True)
        inv = lax.rsqrt(square / width + EPS)
        logits = jnp.zeros((experts, tall), f32)
        for n in range(cuts):
            cols = slice(n * piece, (n + 1) * piece)
            rows = resid_ref[:, cols].astype(f32) * inv * mg_ref[:, cols].astype(f32)
            moe_ref[:, cols] = rows.astype(bf16)
            logits += lax.dot_general(
                wr_ref[:, cols], moe_ref[:, cols], nt, preferred_element_type=f32
            )
        odds = jnp.exp(logits - jnp.max(logits, 0, keepdims=True))
        probs = odds / jnp.sum(odds, 0, keepdims=True)
        expert = lax.broadcasted_iota(jnp.int32, (experts, tall), 0)
        named = jnp.zeros((experts, tall), f32)
        for n in range(topk):
            named = jnp.where(routes_ref[n : n + 1] == expert, 1.0, named)
        share_ref[...] = probs * named
        for copy in sent:
            copy.wait_send()

    vmem, smem = pl.BlockSpec(memory_space=VMEM), pl.BlockSpec(memory_space=pltpu.SMEM)
    return pl.pallas_call(
        kernel,
        out_shape=(
            jax.ShapeDtypeStruct((tall, width), bf16),
            jax.ShapeDtypeStruct((tall, width), bf16),
            jax.ShapeDtypeStruct((experts, tall), f32),
        ),
        in_specs=[smem] * 3 + [vmem] * 9 + [pl.BlockSpec(memory_space=pl.ANY)] * 4,
        out_specs=(vmem, vmem, vmem),
        scratch_shapes=[
            VMEM((width, local), bf16),
            VMEM((width, local), bf16),
            VMEM((width, local), bf16),
            VMEM((local, width), bf16),
            VMEM((tall, width), bf16),
            VMEM((tall, width), bf16),
            VMEM((2, cached, local), bf16),
            VMEM((groups, near, 2 * pair), bf16),
            VMEM((tall, local), bf16),
            VMEM((tall, local), bf16),
            VMEM((tall, cached + near), f32),
            VMEM((cuts, tall, piece), bf16),
            VMEM((cuts, tall, piece), bf16),
            pltpu.SemaphoreType.DMA((4,)),
            pltpu.SemaphoreType.DMA((128,)),
            pltpu.SemaphoreType.DMA((128,)),
        ],
        compiler_params=pltpu.CompilerParams(
            collective_id=8, has_side_effects=True, vmem_limit_bytes=40 << 20
        ),
        name="front",
    )(lengths, request_group, shard_group, tokens, gain.reshape(1, width), cosine, sine, prefix_keys,
      prefix_values, moe_gain.reshape(1, width), w_router.T, routes.T, w_query, w_key, w_value, w_out)


def attention(query, prefix_keys, prefix_values, suffix, bias):
    tall, wide = query.shape
    heads = wide // HD
    cached = prefix_keys.shape[0]
    keys = bias.shape[1]
    many = len(suffix)
    scale = HD ** (-0.5)

    def kernel(query_ref, cached_k, cached_v, bias_ref, *rest):
        suffix_k, suffix_v, out_ref = rest[:many], rest[many : 2 * many], rest[2 * many]
        head = query_ref[...]
        scores = [
            lax.dot_general(
                head, block[...], (((1,), (1,)), ((), ())), preferred_element_type=jnp.float32
            )
            for block in (cached_k, *suffix_k)
        ]
        scores = jnp.concatenate(scores, 1) * scale + bias_ref[...]
        weights = jnp.exp(scores - jnp.max(scores, -1, keepdims=True))
        total = jnp.sum(weights, -1, keepdims=True)
        weights = weights.astype(jnp.bfloat16)
        summed = jnp.dot(weights[:, :cached], cached_v[...], preferred_element_type=jnp.float32)
        for n, block in enumerate(suffix_v):
            start = cached + n * tall
            summed += jnp.dot(
                weights[:, start : start + tall], block[...], preferred_element_type=jnp.float32
            )
        out_ref[...] = (summed / total).astype(jnp.bfloat16)

    def column(rows, offset):
        return pl.BlockSpec((rows, HD), lambda h: (0, h + offset))

    return pl.pallas_call(
        kernel,
        out_shape=jax.ShapeDtypeStruct((tall, wide), jnp.bfloat16),
        grid=(heads,),
        in_specs=[column(tall, 0), column(cached, 0), column(cached, 0)]
        + [pl.BlockSpec((tall, keys), lambda h: (0, 0))]
        + [column(tall, 0)] * many
        + [column(tall, heads)] * many,
        out_specs=column(tall, 0),
        cost_estimate=pl.CostEstimate(
            flops=4 * tall * keys * wide, bytes_accessed=4 * keys * wide, transcendentals=0
        ),
        name="attention",
    )(query, prefix_keys, prefix_values, bias, *suffix, *suffix)


def on_device(
    tokens,
    attn_gain,
    w_query,
    w_key,
    w_value,
    w_out,
    prefix_keys,
    prefix_values,
    shard_group,
    request_group,
    lengths,
    moe_gain,
    w_router,
    w_gate,
    w_up,
    w_down,
    routes,
    final_gain,
    w_head,
):
    f32 = jnp.float32
    bf16 = jnp.bfloat16
    seq_index = lax.axis_index("seq")
    tp_index = lax.axis_index("tp")
    seq_count = lax.axis_size("seq")
    tp_count = lax.axis_size("tp")
    tok_dev = tokens.shape[0]
    width_part = tokens.shape[1]
    shard_rows = prefix_keys.shape[0]
    prefix_length = shard_rows * seq_count // 2
    ends = prefix_sums(lengths)
    experts = w_router.shape[1]
    topk = routes.shape[1]
    local_index = seq_index * tok_dev + jnp.arange(tok_dev)
    if seq_count == 16 and tp_count == 2 and experts == seq_count:
        begun = jnp.max(jnp.where(local_index[:, None] >= ends[None, :], ends[None, :], 0), 1)
        half = HD // 2
        freq = 10000.0 ** (-jnp.arange(half).astype(f32) / half)
        angle = (prefix_length + local_index - begun).astype(f32)[:, None] * freq[None, :]
        cosine, sine = jnp.cos(angle), jnp.sin(angle)
        resid_full, moe_in, share = front(
            tokens, attn_gain, w_query, w_key, w_value, w_out, prefix_keys, prefix_values, lengths,
            request_group, shard_group, jnp.concatenate([cosine, cosine], 1),
            jnp.concatenate([-sine, sine], 1), moe_gain, w_router, routes,
        )
        rows, shares = spread_ring(moe_in, share.reshape(experts, 1, tok_dev))
        own_share = shares.reshape(-1, 1)
        gate = jnp.dot(rows, w_gate[0], preferred_element_type=f32)
        up = jnp.dot(rows, w_up[0], preferred_element_type=f32)
        act = (jax.nn.silu(gate) * up).astype(bf16)
        partial_out = (jnp.dot(act, w_down[0], preferred_element_type=f32) * own_share).astype(bf16)
        hidden = collect_ring(partial_out, resid_full)
        return (hidden, head_tail(hidden, lengths, final_gain, w_head))
    full_x = gather_columns(tokens)
    width = full_x.shape[1]
    normed = normalize(full_x.astype(f32), attn_gain).astype(bf16)
    heads = w_query.shape[1] // HD
    starts = ends - lengths
    own_request = request_of(local_index, ends)
    own_start = lookup(own_request, starts)
    own_group = lookup(own_request, request_group)
    position = (prefix_length + local_index - own_start).astype(f32)
    query = rotate(
        jnp.dot(normed, w_query, preferred_element_type=f32).reshape(tok_dev, heads, HD), position
    ).astype(bf16)
    key_rows = rotate(
        jnp.dot(normed, w_key, preferred_element_type=f32).reshape(tok_dev, heads, HD), position
    ).astype(bf16)
    key_rows = key_rows.reshape(tok_dev, heads * HD)
    value_rows = jnp.dot(normed, w_value, preferred_element_type=f32).astype(bf16)
    pieces = (
        lax.all_gather(prefix_keys, "seq", axis=0, tiled=True),
        lax.all_gather(prefix_values, "seq", axis=0, tiled=True),
    )
    count = pieces[0].shape[0]
    shard_ids = jnp.arange(count) // shard_rows
    key_group = lookup(shard_ids, shard_group)
    fold_allowed = own_group[:, None] == key_group[None, :]
    own_allowed = (own_request[:, None] == own_request[None, :]) & (
        local_index[None, :] <= local_index[:, None]
    )
    both_rows = jnp.concatenate([key_rows, value_rows], 1)
    suffix = [both_rows] + [from_behind(both_rows, "seq", step) for step in range(1, SPAN + 1)]
    permitted = [fold_allowed, own_allowed]
    for step in range(1, SPAN + 1):
        key_index = (seq_index - step) * tok_dev + jnp.arange(tok_dev)
        key_request = request_of(key_index, ends)
        permitted.append(
            (key_index >= 0)[None, :] & (own_request[:, None] == key_request[None, :])
        )
    bias = jnp.where(jnp.concatenate(permitted, 1), 0.0, NEGATIVE)
    attended = attention(query.reshape(tok_dev, heads * HD), *pieces, suffix, bias)
    mixed = jnp.dot(attended, w_out, preferred_element_type=f32).astype(bf16)
    resid_full = (full_x.astype(f32) + sum_over_tp(mixed)).astype(bf16)
    moe_in = normalize(resid_full.astype(f32), moe_gain).astype(bf16)
    probs = jax.nn.softmax(jnp.dot(moe_in, w_router, preferred_element_type=f32), -1)
    flat = routes.reshape(-1)
    hits = (flat[:, None] == jnp.arange(experts)[None, :]).astype(jnp.int32)
    line = jnp.arange(flat.shape[0])
    before = (line[:, None] > line[None, :]).astype(bf16)
    earlier = jnp.dot(before, hits.astype(bf16), preferred_element_type=f32).astype(jnp.int32)
    rank = jnp.sum(earlier * hits, 1)
    capacity = min(tok_dev, tp_count * max(1, 3 * tok_dev * topk // (2 * experts * tp_count)))
    target = flat * capacity + rank
    route_weight = jnp.sum(hits.reshape(tok_dev, topk, experts).astype(f32) * probs[:, None, :], -1)
    repeated = jnp.repeat(moe_in, topk, axis=0)
    outgoing = (
        jnp.zeros((experts * capacity, width), bf16)
        .at[target]
        .set(repeated)
        .reshape(experts, capacity, width)
    )
    arrived = lax.all_to_all(outgoing, "seq", split_axis=0, concat_axis=0, tiled=True)
    sources = arrived.shape[0]
    count = arrived.shape[1]
    rows = arrived.reshape(sources * count, width)
    gate = jnp.dot(rows, w_gate[0], preferred_element_type=f32)
    up = jnp.dot(rows, w_up[0], preferred_element_type=f32)
    act = (jax.nn.silu(gate) * up).astype(bf16)
    partial_out = jnp.dot(act, w_down[0], preferred_element_type=f32).reshape(sources, count, width)
    summed = lax.psum_scatter(partial_out, "tp", scatter_dimension=2, tiled=True).astype(bf16)
    returned = lax.all_to_all(summed, "seq", split_axis=0, concat_axis=0, tiled=True)
    picked = returned.reshape(experts * capacity, width_part)[target].reshape(
        tok_dev, topk, width_part
    )
    moe_part = jnp.sum(picked.astype(f32) * route_weight[:, :, None], 1)
    resid = lax.dynamic_slice_in_dim(resid_full, tp_index * width_part, width_part, 1)
    hidden = (resid.astype(f32) + moe_part).astype(bf16)
    last_hit = ((ends - 1)[:, None] == local_index[None, :]).astype(bf16)
    chosen = jnp.dot(last_hit, hidden, preferred_element_type=f32)
    final = last_rows(chosen, final_gain, width)
    log_probs = log_softmax(jnp.dot(final, w_head, preferred_element_type=f32))
    return (hidden, log_probs)


def solution(mesh):
    in_specs = (
        P("seq", "tp"),
        P(),
        P(None, "tp"),
        P(None, "tp"),
        P(None, "tp"),
        P("tp", None),
        P("seq", "tp"),
        P("seq", "tp"),
        P(),
        P(),
        P(),
        P(),
        P(),
        P("seq", None, "tp"),
        P("seq", None, "tp"),
        P("seq", "tp", None),
        P("seq", None),
        P("tp"),
        P("tp", "seq"),
    )
    out_specs = (P("seq", "tp"), P(None, "seq"))
    return jax.shard_map(
        on_device, mesh=mesh, in_specs=in_specs, out_specs=out_specs, check_vma=False
    )
```

```python
import jax
import jax.numpy as jnp
from jax import lax
from jax.experimental import pallas as pl
from jax.experimental.pallas import tpu as pltpu
from jax.sharding import PartitionSpec as P

HD = 128
SPAN = 4
VMEM = pltpu.VMEM


EPS = 1e-05
NEGATIVE = -1e30


def from_behind(value, axis, steps):
    count = lax.axis_size(axis)
    leading, last = (max(0, -steps), min(count, count - steps))
    return lax.ppermute(value, axis, [(source, source + steps) for source in range(leading, last)])


def normalize(rows, gain):
    inv = lax.rsqrt(jnp.mean(rows * rows, -1, keepdims=True) + EPS)
    return rows * inv * gain.astype(jnp.float32)


def rotate(vectors, position):
    half = vectors.shape[-1] // 2
    freq = 10000.0 ** (-jnp.arange(half).astype(jnp.float32) / half)
    angle = position[:, None] * freq[None, :]
    cosine = jnp.cos(angle)[:, None, :]
    sine = jnp.sin(angle)[:, None, :]
    first = vectors[..., :half]
    second = vectors[..., half:]
    return jnp.concatenate([first * cosine - second * sine, second * cosine + first * sine], -1)


def request_of(index, ends):
    return jnp.sum((index[:, None] >= ends[None, :]).astype(jnp.int32), 1)


def lookup(selector, table):
    hit = selector[:, None] == jnp.arange(table.shape[0])[None, :]
    return jnp.sum(jnp.where(hit, table[None, :], 0), 1)


def prefix_sums(values):
    order = jnp.arange(values.shape[0])
    return jnp.sum(jnp.where(order[:, None] >= order[None, :], values[None, :], 0), 1)


def partner(axis, bit):
    index = lax.axis_index(axis)
    span = 1 << bit
    other = index + span - 2 * span * ((index // span) % 2)
    return {axis: other}


def greet(stages):
    barrier = pltpu.get_barrier_semaphore()
    for axis, bit in stages:
        pl.semaphore_signal(barrier, inc=1, device_id=partner(axis, bit))
    pl.semaphore_wait(barrier, len(stages))


def swap(source, target, send_sem, recv_sem, stage):
    copy = pltpu.make_async_remote_copy(
        src_ref=source, dst_ref=target, send_sem=send_sem, recv_sem=recv_sem,
        device_id=partner(*stage),
    )
    copy.start()
    return copy


def bits_of(axis):
    return [(axis, bit) for bit in range(lax.axis_size(axis).bit_length() - 1)]


def last_rows(chosen, gain, width):
    seq_stages, tp_stages = bits_of("seq"), bits_of("tp")
    stages = seq_stages + tp_stages
    rows, part = chosen.shape

    def kernel(chosen_ref, gain_ref, out_ref, held, got, sq_held, sq_got, send_sem, recv_sem):
        greet(stages)
        held[0] = chosen_ref[...]
        count = len(seq_stages)
        for k, stage in enumerate(seq_stages):
            swap(held.at[k], got.at[k], send_sem.at[k], recv_sem.at[k], stage).wait()
            held[k + 1] = held[k] + got[k]
        total = held[count]
        sq_held[0] = jnp.broadcast_to(jnp.sum(total * total, -1, keepdims=True), (rows, 128))
        for k, stage in enumerate(tp_stages):
            n = count + k
            swap(sq_held.at[k], sq_got.at[k], send_sem.at[n], recv_sem.at[n], stage).wait()
            sq_held[k + 1] = sq_held[k] + sq_got[k]
        square = sq_held[len(tp_stages)][:, :1]
        scaled = total * lax.rsqrt(square / width + EPS) * gain_ref[...].astype(jnp.float32)
        out_ref[...] = scaled.astype(jnp.bfloat16)

    ns, nt = len(seq_stages), len(tp_stages)
    return pl.pallas_call(
        kernel,
        out_shape=jax.ShapeDtypeStruct((rows, part), jnp.bfloat16),
        in_specs=[pl.BlockSpec(memory_space=VMEM)] * 2,
        out_specs=pl.BlockSpec(memory_space=VMEM),
        scratch_shapes=[
            VMEM((ns + 1, rows, part), jnp.float32),
            VMEM((ns, rows, part), jnp.float32),
            VMEM((nt + 1, rows, 128), jnp.float32),
            VMEM((nt, rows, 128), jnp.float32),
            pltpu.SemaphoreType.DMA((ns + nt,)),
            pltpu.SemaphoreType.DMA((ns + nt,)),
        ],
        compiler_params=pltpu.CompilerParams(collective_id=1, has_side_effects=True),
        name="last_rows",
    )(chosen, gain.reshape(1, part))


def log_softmax(logits):
    seq_stages, tp_stages = bits_of("seq"), bits_of("tp")
    stages = tp_stages + seq_stages
    rows, part = logits.shape

    def kernel(logits_ref, out_ref, held, got, st_held, st_got, send_sem, recv_sem):
        greet(stages)
        held[0] = logits_ref[...]
        count = len(tp_stages)
        for k, stage in enumerate(tp_stages):
            swap(held.at[k], got.at[k], send_sem.at[k], recv_sem.at[k], stage).wait()
            held[k + 1] = held[k] + got[k]
        total = held[count]
        peak = jnp.max(total, -1, keepdims=True)
        mass = jnp.sum(jnp.exp(total - peak), -1, keepdims=True)
        st_held[0, :, :128] = jnp.broadcast_to(peak, (rows, 128))
        st_held[0, :, 128:] = jnp.broadcast_to(mass, (rows, 128))
        for k, stage in enumerate(seq_stages):
            n = count + k
            swap(st_held.at[k], st_got.at[k], send_sem.at[n], recv_sem.at[n], stage).wait()
            mine, theirs = st_held[k, :, :128], st_got[k, :, :128]
            top = jnp.maximum(mine, theirs)
            st_held[k + 1, :, :128] = top
            st_held[k + 1, :, 128:] = st_held[k, :, 128:] * jnp.exp(mine - top) + st_got[
                k, :, 128:
            ] * jnp.exp(theirs - top)
        last = len(seq_stages)
        out_ref[...] = total - st_held[last, :, :1] - jnp.log(st_held[last, :, 128:129])

    ns, nt = len(seq_stages), len(tp_stages)
    return pl.pallas_call(
        kernel,
        out_shape=jax.ShapeDtypeStruct((rows, part), jnp.float32),
        in_specs=[pl.BlockSpec(memory_space=VMEM)],
        out_specs=pl.BlockSpec(memory_space=VMEM),
        scratch_shapes=[
            VMEM((nt + 1, rows, part), jnp.float32),
            VMEM((nt, rows, part), jnp.float32),
            VMEM((ns + 1, rows, 256), jnp.float32),
            VMEM((ns, rows, 256), jnp.float32),
            pltpu.SemaphoreType.DMA((ns + nt,)),
            pltpu.SemaphoreType.DMA((ns + nt,)),
        ],
        compiler_params=pltpu.CompilerParams(collective_id=2, has_side_effects=True),
        name="log_softmax",
    )(logits)


def gather_columns(block):
    stages = bits_of("tp")
    rows, part = block.shape
    count = lax.axis_size("tp")

    def kernel(block_ref, out_ref, send_sem, recv_sem):
        greet(stages)
        me = lax.axis_index("tp")
        out_ref[:, pl.ds(pl.multiple_of(me * part, part), part)] = block_ref[...]
        for k, stage in enumerate(stages):
            wide = part << k
            start = pl.multiple_of((me // (1 << k)) * wide, wide)
            piece = out_ref.at[:, pl.ds(start, wide)]
            swap(piece, piece, send_sem.at[k], recv_sem.at[k], stage).wait()

    return pl.pallas_call(
        kernel,
        out_shape=jax.ShapeDtypeStruct((rows, part * count), block.dtype),
        in_specs=[pl.BlockSpec(memory_space=VMEM)],
        out_specs=pl.BlockSpec(memory_space=VMEM),
        scratch_shapes=[pltpu.SemaphoreType.DMA((len(stages),))] * 2,
        compiler_params=pltpu.CompilerParams(collective_id=3, has_side_effects=True),
        name="gather_columns",
    )(block)


def sum_over_tp(block):
    stages = bits_of("tp")
    rows, part = block.shape

    def kernel(block_ref, out_ref, held, got, send_sem, recv_sem):
        greet(stages)
        for k, stage in enumerate(stages):
            source = block_ref if k == 0 else held.at[k]
            swap(source, got.at[k], send_sem.at[k], recv_sem.at[k], stage).wait()
            total = source[...].astype(jnp.float32) + got[k].astype(jnp.float32)
            if k + 1 < len(stages):
                held[k + 1] = total.astype(jnp.bfloat16)
            else:
                out_ref[...] = total

    count = len(stages)
    return pl.pallas_call(
        kernel,
        out_shape=jax.ShapeDtypeStruct((rows, part), jnp.float32),
        in_specs=[pl.BlockSpec(memory_space=VMEM)],
        out_specs=pl.BlockSpec(memory_space=VMEM),
        scratch_shapes=[
            VMEM((count, rows, part), jnp.bfloat16),
            VMEM((count, rows, part), jnp.bfloat16),
            pltpu.SemaphoreType.DMA((count,)),
            pltpu.SemaphoreType.DMA((count,)),
        ],
        compiler_params=pltpu.CompilerParams(collective_id=4, has_side_effects=True),
        name="sum_over_tp",
    )(block)


HOPS = 4


def ring_place():
    s = lax.axis_index("seq")
    core = s % 2
    x = (s // 2) % 2
    z = s // 4
    return s, core, z + x * (7 - 2 * z)


def chip_at(place):
    q = (place + 16) % 8
    x = q // 4
    z = q + x * (7 - 2 * q)
    return z * 2 + x


def greet_all(blocks):
    s = lax.axis_index("seq")
    barrier = pltpu.get_barrier_semaphore()
    for d in range(1, blocks):
        pl.semaphore_signal(barrier, inc=1, device_id={"seq": (s + d) % blocks})
    pl.semaphore_signal(barrier, inc=1, device_id={"tp": 1 - lax.axis_index("tp")})
    pl.semaphore_wait(barrier, blocks)


def greet_ring(nxt, prv, sib):
    barrier = pltpu.get_barrier_semaphore()
    for d in ({"seq": nxt}, {"seq": prv}, {"seq": sib}, {"tp": 1 - lax.axis_index("tp")}):
        pl.semaphore_signal(barrier, inc=1, device_id=d)
    pl.semaphore_wait(barrier, 4)


def collect_ring(partial, resid):
    tall, wide = resid.shape
    half = wide // 2
    ty = tall * 5 // 8
    ts = tall - ty
    bf16 = jnp.bfloat16
    G = 16
    units = [(HOPS, "o")] + [(t, b) for t in range(HOPS - 1, 0, -1) for b in ("s", "o")] + [(0, "o")]
    nu = len(units)

    def kernel(part_ref, resid_ref, out_ref, sib_buf, acc_y, acc_s, y_send, y_recv, ring_y, ring_s,
               far_y, far_s, last_recv, send_sem, recv_sem):
        s, core, r = ring_place()
        y = lax.axis_index("tp")
        step = 1 - 2 * core
        nxt = {"seq": chip_at(r + step) * 2 + core}
        sib = {"seq": s + step}
        other = {"tp": 1 - y}
        greet_ring(nxt["seq"], chip_at(r - step) * 2 + core, sib["seq"])
        used = iter(range(64))
        own_cols = pl.ds(pl.multiple_of(y * half, half), half)
        far_cols = pl.ds(pl.multiple_of((1 - y) * half, half), half)

        def send(source, target, device):
            n = next(used)
            copy = pltpu.make_async_remote_copy(
                src_ref=source, dst_ref=target, send_sem=send_sem.at[n], recv_sem=recv_sem.at[n],
                device_id=device,
            )
            copy.start()
            return copy

        def rows_of(t, b, direction, c):
            place = chip_at(r + direction * t) * 2 + (c if b == "o" else 1 - c)
            return place * tall

        pair, cross, ring, sent = {}, {}, {}, []

        def lend(i):
            if i < nu:
                start = pl.multiple_of(rows_of(*units[i], -step, 1 - core), tall)
                pair[i] = send(part_ref.at[pl.ds(start, tall)], sib_buf.at[i], sib)
                sent.append(pair[i])

        lend(0)
        lend(1)

        def summed(i):
            t, b = units[i]
            start = rows_of(t, b, step, core)
            pair[i].wait_recv()
            lend(i + 2)

            def body_y(g, _):
                rows = pl.ds(pl.multiple_of(g * G, G), G)
                here = pl.ds(pl.multiple_of(start + g * G, G), G)
                y_send[i, rows] = part_ref[here, far_cols] + sib_buf[i, rows, far_cols]
                acc_y[i, rows] = part_ref[here, own_cols] + sib_buf[i, rows, own_cols]
                return 0

            lax.fori_loop(0, ty // G, body_y, 0)
            cross[i] = send(y_send.at[i], y_recv.at[i], other)
            sent.append(cross[i])

            def body_s(g, _):
                rows = pl.ds(pl.multiple_of(g * G, G), G)
                below = pl.ds(pl.multiple_of(ty + g * G, G), G)
                here = pl.ds(pl.multiple_of(start + ty + g * G, G), G)
                acc_s[i, rows] = part_ref[here] + sib_buf[i, below]
                return 0

            lax.fori_loop(0, ts // G, body_s, 0)
            if not arriving(t, b) and t > 0:
                pass_s(i)

        def slot(t, b):
            return 2 * t + (0 if b == "o" else 1)

        def arriving(t, b):
            return (t + 1, b) in units and t > 0

        def pass_s(i):
            t, b = units[i]
            m = slot(t - 1, b)
            ring[t - 1, b, "s"] = send(acc_s.at[i], ring_s.at[m], nxt)
            sent.append(ring[t - 1, b, "s"])

        def passed(i):
            t, b = units[i]
            arrived = arriving(t, b)
            n = slot(t, b)
            if arrived:
                ring[t, b, "s"].wait_recv()

                def body_s(g, _):
                    rows = pl.ds(pl.multiple_of(g * G, G), G)
                    acc_s[i, rows] = acc_s[i, rows] + ring_s[n, rows]
                    return 0

                lax.fori_loop(0, ts // G, body_s, 0)
                pass_s(i)
                ring[t, b, "y"].wait_recv()
            cross[i].wait_recv()

            def body_y(g, _):
                rows = pl.ds(pl.multiple_of(g * G, G), G)
                total = acc_y[i, rows] + y_recv[i, rows]
                if arrived:
                    total = total + ring_y[n, rows]
                acc_y[i, rows] = total
                return 0

            lax.fori_loop(0, ty // G, body_y, 0)
            if t > 0:
                m = slot(t - 1, b)
                ring[t - 1, b, "y"] = send(acc_y.at[i], ring_y.at[m], nxt)
                sent.append(ring[t - 1, b, "y"])

        summed(0)
        for i in range(1, nu):
            summed(i)
            passed(i - 1)
        passed(nu - 1)
        m, n, i = slot(0, "s"), slot(0, "o"), nu - 1
        ring[0, "s", "s"].wait_recv()
        far_copy_s = send(ring_s.at[m], far_s, sib)
        ring[0, "s", "y"].wait_recv()
        far_copy_y = send(ring_y.at[m], far_y, sib)
        sent.extend((far_copy_s, far_copy_y))
        ring[0, "o", "s"].wait_recv()
        far_copy_s.wait_recv()

        def body_s(g, _):
            rows = pl.ds(pl.multiple_of(g * G, G), G)
            acc_s[i, rows] = acc_s[i, rows] + ring_s[n, rows] + far_s[rows]
            return 0

        lax.fori_loop(0, ts // G, body_s, 0)
        last = send(acc_s.at[i, :, far_cols], last_recv, other)
        sent.append(last)
        ring[0, "o", "y"].wait_recv()
        far_copy_y.wait_recv()
        f32 = jnp.float32

        def body_y(g, _):
            rows = pl.ds(pl.multiple_of(g * G, G), G)
            total = acc_y[i, rows].astype(f32) + ring_y[n, rows].astype(f32) + far_y[rows].astype(f32)
            out_ref[rows] = (total + resid_ref[rows, own_cols].astype(f32)).astype(bf16)
            return 0

        lax.fori_loop(0, ty // G, body_y, 0)
        last.wait_recv()

        def body_l(g, _):
            rows = pl.ds(pl.multiple_of(g * G, G), G)
            here = pl.ds(pl.multiple_of(ty + g * G, G), G)
            total = acc_s[i, rows, own_cols].astype(f32) + last_recv[rows].astype(f32)
            out_ref[here] = (total + resid_ref[here, own_cols].astype(f32)).astype(bf16)
            return 0

        lax.fori_loop(0, ts // G, body_l, 0)
        for copy in sent:
            copy.wait_send()

    return pl.pallas_call(
        kernel,
        out_shape=jax.ShapeDtypeStruct((tall, half), bf16),
        in_specs=[pl.BlockSpec(memory_space=VMEM)] * 2,
        out_specs=pl.BlockSpec(memory_space=VMEM),
        scratch_shapes=[
            VMEM((nu, tall, wide), bf16),
            VMEM((nu, ty, half), bf16), VMEM((nu, ts, wide), bf16),
            VMEM((nu, ty, half), bf16), VMEM((nu, ty, half), bf16),
            VMEM((2 * HOPS, ty, half), bf16), VMEM((2 * HOPS, ts, wide), bf16),
            VMEM((ty, half), bf16), VMEM((ts, wide), bf16), VMEM((ts, half), bf16),
            pltpu.SemaphoreType.DMA((64,)), pltpu.SemaphoreType.DMA((64,)),
        ],
        compiler_params=pltpu.CompilerParams(
            collective_id=6, has_side_effects=True, vmem_limit_bytes=56 << 20
        ),
        name="collect_ring",
    )(partial, resid)


def head_tail(hidden, lengths, gain, w_head):
    tall, part = hidden.shape
    reqs = lengths.shape[0]
    cols = w_head.shape[1]
    width = 2 * part
    wide = -(-cols // 128) * 128
    bf16, f32 = jnp.bfloat16, jnp.float32
    cuts = 4
    high = -(-reqs // 16) * 16
    per = -(-cols // (16 * cuts)) * 16
    spans = [(k * per, min(per, cols - k * per)) for k in range(cuts)]

    def kernel(len_ref, hid_ref, gain_ref, w_ref, out_ref, w_buf, near, far, logit, got, stat, stats,
               w_sem, send_sem, recv_sem):
        load = pltpu.make_async_copy(w_ref, w_buf, w_sem)
        load.start()
        s = lax.axis_index("seq")
        y = lax.axis_index("tp")
        count = 16
        barrier = pltpu.get_barrier_semaphore()
        for d in range(1, count):
            pl.semaphore_signal(barrier, inc=1, device_id={"seq": (s + d) % count})
        pl.semaphore_signal(barrier, inc=1, device_id={"tp": 1 - y})
        row = lax.broadcasted_iota(jnp.int32, (high, tall), 0)
        place = lax.broadcasted_iota(jnp.int32, (high, tall), 1) + s * tall
        last = jnp.full((high, tall), -1, jnp.int32)
        end = 0
        for j in range(reqs):
            end = end + len_ref[j]
            last = jnp.where(row == j, end - 1, last)
        hit = (last == place).astype(f32).astype(bf16)
        near[0] = jnp.dot(hit, hid_ref[...], preferred_element_type=f32).astype(bf16)
        pl.semaphore_wait(barrier, count)
        used = iter(range(32))
        sent = []

        def send(source, target, device):
            n = next(used)
            copy = pltpu.make_async_remote_copy(
                src_ref=source, dst_ref=target, send_sem=send_sem.at[n], recv_sem=recv_sem.at[n],
                device_id=device,
            )
            copy.start()
            sent.append(copy)
            return copy

        first = [
            send(near.at[0], near.at[d], {"seq": (s // 4) * 4 + (s + d) % 4}) for d in range(1, 4)
        ]
        for copy in first:
            copy.wait_recv()
        far[0] = (near[0] + near[1]) + (near[2] + near[3])
        second = [send(far.at[0], far.at[d], {"seq": (s + 4 * d) % count}) for d in range(1, 4)]
        for copy in second:
            copy.wait_recv()
        total = ((far[0] + far[1]) + (far[2] + far[3])).astype(f32)
        square = jnp.sum(total * total, -1, keepdims=True)
        scaled = (total * gain_ref[...].astype(f32)).astype(bf16)
        logit[:, wide:] = jnp.broadcast_to(square[:reqs], (reqs, 128))
        load.wait()
        for k, (start, size) in enumerate(spans):
            product = lax.dot_general(
                scaled, w_buf[start : start + size], (((1,), (1,)), ((), ())), preferred_element_type=f32
            )
            logit[:, start : start + size] = product[:reqs]
        send(logit, got, {"tp": 1 - y}).wait_recv()
        square = logit[:, wide : wide + 1] + got[:, wide : wide + 1]
        inv = lax.rsqrt(square / width + EPS)
        both = (logit[:, :cols] + got[:, :cols]) * inv
        peak = jnp.max(both, -1, keepdims=True)
        mass = jnp.sum(jnp.exp(both - peak), -1, keepdims=True)
        lane = lax.broadcasted_iota(jnp.int32, (reqs, 128), 1)
        stat[...] = jnp.where(lane < 64, peak, mass)
        stats[0] = stat[...]
        third = [send(stat, stats.at[d], {"seq": (s + d) % count}) for d in range(1, count)]
        for copy in third:
            copy.wait_recv()
        everyone = stats[...]
        peaks, masses = everyone[:, :, :1], everyone[:, :, 64:65]
        top = jnp.max(peaks, 0)
        whole = jnp.sum(masses * jnp.exp(peaks - top[None]), 0)
        out_ref[...] = both - top - jnp.log(whole)
        for copy in sent:
            copy.wait_send()

    return pl.pallas_call(
        kernel,
        out_shape=jax.ShapeDtypeStruct((reqs, cols), f32),
        in_specs=[pl.BlockSpec(memory_space=pltpu.SMEM)]
        + [pl.BlockSpec(memory_space=VMEM)] * 2
        + [pl.BlockSpec(memory_space=pl.ANY)],
        out_specs=pl.BlockSpec(memory_space=VMEM),
        scratch_shapes=[
            VMEM((cols, part), bf16),
            VMEM((4, high, part), bf16),
            VMEM((4, high, part), bf16),
            VMEM((reqs, wide + 128), f32),
            VMEM((reqs, wide + 128), f32),
            VMEM((reqs, 128), f32),
            VMEM((16, reqs, 128), f32),
            pltpu.SemaphoreType.DMA,
            pltpu.SemaphoreType.DMA((32,)),
            pltpu.SemaphoreType.DMA((32,)),
        ],
        compiler_params=pltpu.CompilerParams(
            collective_id=7, has_side_effects=True, vmem_limit_bytes=60 << 20
        ),
        name="head_tail",
    )(lengths, hidden, gain.reshape(1, part), w_head.T)


def front(tokens, gain, w_query, w_key, w_value, w_out, prefix_keys, prefix_values, lengths,
          request_group, shard_group, cosine, sine, moe_gain, w_router, routes, w_gate, w_up):
    tall, part = tokens.shape
    width = 2 * part
    local = w_query.shape[1]
    shard = prefix_keys.shape[0]
    shards = shard_group.shape[0]
    reqs = lengths.shape[0]
    cached = shard * shards
    experts = w_router.shape[1]
    topk = routes.shape[1]
    bf16, f32 = jnp.bfloat16, jnp.float32
    pair = 2 * HD
    groups = local // pair
    slots = SPAN + 1
    near = slots * tall
    hidden = w_gate.shape[1]
    blocks = 16
    q = tall // 4
    sems = 136
    scale = HD ** (-0.5)
    nt = (((1,), (1,)), ((), ()))

    def kernel(len_ref, rg_ref, sg_ref, tok_ref, gain_ref, cos_ref, sin_ref, pk_ref, pv_ref, mg_ref,
               wr_ref, routes_ref, wq_ref, wk_ref, wv_ref, wo_ref, wg_ref, wu_ref, resid_ref, act_ref,
               share_out, wq, wk, wv, wo, wg, wu, x, normed, cache, kv, query, attended, bias, mix, mix_got,
               all_rows, share_own, w_sem, send_sem, recv_sem):
        loads = {}
        for n, (source, target) in enumerate((
            (wk_ref, wk), (wv_ref, wv), (wq_ref, wq), (wo_ref, wo), (wg_ref, wg), (wu_ref, wu)
        )):
            loads[n] = pltpu.make_async_copy(source, target, w_sem.at[n])
            loads[n].start()
        s, core, r = ring_place()
        y = lax.axis_index("tp")
        count = 16
        step = 1 - 2 * core
        ahead = 1 - 2 * ((s // 2) % 2)
        nxt = {"seq": chip_at(r + step) * 2 + core}
        sib = {"seq": s + step}
        side = {"seq": s + 2 * ahead}
        above = {"seq": (s + 4) % count}
        other = {"tp": 1 - y}
        own_cols = pl.ds(pl.multiple_of(y * part, part), part)
        x[:, own_cols] = tok_ref[...]
        own_rows = pl.ds(pl.multiple_of(s * shard, shard), shard)
        cache[0, own_rows] = pk_ref[...]
        cache[1, own_rows] = pv_ref[...]
        greet_all(count)
        used = iter(range(sems))
        sent = []

        def send(source, target, device):
            n = next(used)
            copy = pltpu.make_async_remote_copy(
                src_ref=source, dst_ref=target, send_sem=send_sem.at[n], recv_sem=recv_sem.at[n],
                device_id=device,
            )
            copy.start()
            sent.append(copy)
            return copy

        def move(chip, name, device):
            which, owner = name
            shift = core if owner == "o" else 1 - core
            rows = pl.ds(pl.multiple_of((chip * 2 + shift) * shard, shard), shard)
            view = cache.at[which, rows]
            return send(view, view, device)

        home = chip_at(r)
        swapped = [move(home, (which, "o"), sib) for which in range(2)]
        ring, twin = {}, {}
        for which in range(2):
            ring[1, (which, "o")] = move(home, (which, "o"), nxt)
        crossing = send(tok_ref, x.at[:, own_cols], other)
        for which in range(2):
            swapped[which].wait_recv()
            ring[1, (which, "s")] = move(home, (which, "s"), nxt)

        def hop(t):
            chip = chip_at(r - step * t)
            owners = ("o", "s") if t < HOPS else ("o",)
            for owner in owners:
                for which in range(2):
                    name = (which, owner)
                    ring[t, name].wait_recv()
                    if t < HOPS - 1 or (t == HOPS - 1 and owner == "o"):
                        ring[t + 1, name] = move(chip, name, nxt)
                    twin[t, name] = move(chip, name, sib)

        lane = lax.broadcasted_iota(jnp.int32, (tall, 128), 0) + s * tall
        mine = jnp.zeros((tall, 128), jnp.int32)
        ends, end = [], 0
        for j in range(reqs):
            end = end + len_ref[j]
            ends.append(end)
        for j in range(reqs):
            mine = mine + (lane >= ends[j]).astype(jnp.int32)
        group = jnp.zeros((tall, 128), jnp.int32)
        for j in range(reqs):
            group = jnp.where(mine == j, rg_ref[j], group)
        own_index, own_request, own_group = lane[:, :1], mine[:, :1], group[:, :1]
        column = lax.broadcasted_iota(jnp.int32, (8, cached), 1)
        key_group = jnp.zeros((8, cached), jnp.int32)
        for j in range(shards):
            inside = (column >= j * shard) & (column < (j + 1) * shard)
            key_group = jnp.where(inside, sg_ref[j], key_group)
        bias[:, :cached] = jnp.where(own_group == key_group[:1], 0.0, NEGATIVE)
        chip = s // 2
        bases = (
            s * tall, (chip - 1) * 2 * tall, (chip - 1) * 2 * tall + tall, (chip - 2) * 2 * tall + tall,
            (chip - 2 + 2 * core) * 2 * tall,
        )
        for n in range(slots):
            place = lax.broadcasted_iota(jnp.int32, (8, tall), 1) + bases[n]
            theirs = jnp.zeros((8, tall), jnp.int32)
            for j in range(reqs):
                theirs = theirs + (place >= ends[j]).astype(jnp.int32)
            seen = (own_request == theirs[:1]) & (place[:1] <= own_index) & (place[:1] >= 0)
            start = cached + n * tall
            bias[:, start : start + tall] = jnp.where(seen, 0.0, NEGATIVE)
        hop(1)
        crossing.wait_recv()
        rows = x[...].astype(f32)
        inv = lax.rsqrt(jnp.mean(rows * rows, -1, keepdims=True) + EPS)
        normed[...] = (rows * inv * gain_ref[...].astype(f32)).astype(bf16)

        def turned(value):
            heads = []
            for n in range(pair // HD):
                head = value[:, n * HD : (n + 1) * HD]
                heads.append(head * cos_ref[...] + pltpu.roll(head, HD // 2, 1) * sin_ref[...])
            return jnp.concatenate(heads, 1).astype(bf16)

        back = 4 - core
        side_slot = 1 + core

        def slot_of(g, n):
            return kv.at[g, pl.ds(pl.multiple_of(n * tall, tall), tall)]

        up = {}

        def keys_of(g):
            cols = slice(g * pair, (g + 1) * pair)
            key = jnp.dot(normed[...], wk[:, cols], preferred_element_type=f32)
            kv[g, :tall, :pair] = turned(key)
            value = jnp.dot(normed[...], wv[:, cols], preferred_element_type=f32)
            kv[g, :tall, pair:] = value.astype(bf16)
            up[g] = send(slot_of(g, 0), slot_of(g, back), above)

        loads[0].wait()
        loads[1].wait()
        keys_of(0)
        hop(2)
        keys_of(1)
        hop(3)
        for g in range(2, groups):
            keys_of(g)
        loads[2].wait()
        for g in range(groups):
            cols = slice(g * pair, (g + 1) * pair)
            query[:, cols] = turned(jnp.dot(normed[...], wq[:, cols], preferred_element_type=f32))
        hop(4)
        across, down, inner = {}, {}, {}
        for g in range(groups):
            up[g].wait_recv()
            across[g] = send(slot_of(g, (1 - ahead) // 2 * back), slot_of(g, side_slot), side)
            inner[g] = send(slot_of(g, 3 * core), slot_of(g, back), sib)
        for copy in twin.values():
            copy.wait_recv()
        for g in range(groups):
            across[g].wait_recv()
            down[g] = send(slot_of(g, side_slot), slot_of(g, side_slot), sib)
        for g in range(groups):
            inner[g].wait_recv()
            down[g].wait_recv()
            for n in range(pair // HD):
                cols = slice(g * pair + n * HD, g * pair + (n + 1) * HD)
                k_cols = slice(n * HD, (n + 1) * HD)
                v_cols = slice(pair + n * HD, pair + (n + 1) * HD)
                head = query[:, cols]
                scores = jnp.concatenate(
                    [
                        lax.dot_general(head, cache[0, :, cols], nt, preferred_element_type=f32),
                        lax.dot_general(head, kv[g, :, k_cols], nt, preferred_element_type=f32),
                    ],
                    1,
                )
                scores = scores * scale + bias[...]
                weights = jnp.exp(scores - jnp.max(scores, -1, keepdims=True))
                total = jnp.sum(weights, -1, keepdims=True)
                weights = weights.astype(bf16)
                summed = jnp.dot(weights[:, :cached], cache[1, :, cols], preferred_element_type=f32)
                summed += jnp.dot(weights[:, cached:], kv[g, :, v_cols], preferred_element_type=f32)
                attended[:, cols] = (summed / total).astype(bf16)
        loads[3].wait()
        mine, theirs = core * tall, (1 - core) * tall
        odd = (core + y) % 2
        spot = {
            "ao": mine + q * odd,
            "as": theirs + q * (1 - odd),
            "e1o": mine + 2 * q,
            "e1s": theirs + 2 * q,
            "e2o": mine + 3 * q,
            "e2s": theirs + 3 * q,
            "yo": mine + q * (1 - odd),
            "ys": theirs + q * odd,
        }
        inside = {"ao": q * odd, "e1o": 2 * q, "e2o": 3 * q, "yo": q * (1 - odd)}
        circle, cross, twins = {}, {}, {}

        def put(table, key, hops, name, device):
            start = chip_at(r + hops) * 2 * tall + spot[name]
            view = all_rows.at[pl.ds(pl.multiple_of(start, q), q)]
            table[key] = send(view, view, device)

        mixed = {}
        for n, (away, name) in enumerate((("yo", "ao"), ("e1o", "e1o"), ("e2o", "e2o"), ("ao", "yo"))):
            part_rows = pl.ds(pl.multiple_of(inside[away], q), q)
            product = jnp.dot(attended[part_rows], wo[...], preferred_element_type=f32)
            mix[part_rows] = product.astype(bf16)
            mixed[name] = send(mix.at[part_rows], mix_got.at[part_rows], other)

        def settle(name):
            mixed[name].wait_recv()
            rows = pl.ds(pl.multiple_of(inside[name], q), q)
            total = x[rows].astype(f32) + (mix[rows].astype(f32) + mix_got[rows].astype(f32))
            total = total.astype(bf16)
            resid_ref[rows] = total
            total = total.astype(f32)
            inv = lax.rsqrt(jnp.mean(total * total, -1, keepdims=True) + EPS)
            here = pl.ds(pl.multiple_of(home * 2 * tall + spot[name], q), q)
            all_rows[here] = (total * inv * mg_ref[...].astype(f32)).astype(bf16)
            put(twins, (0, name), 0, name, sib)

        pieces = ("ao", "as", "e1o", "e1s", "e2o", "e2s")
        some = ("ao", "e1o", "e2o")
        order = [(t, p) for t in range(1, HOPS) for p in pieces] + [(HOPS, p) for p in some]

        def onward(t, p):
            if t < HOPS - 1 or (t == HOPS - 1 and p in some):
                put(circle, (t + 1, p), -step * t, p, nxt)

        for name in some:
            settle(name)
            onward(0, name)
            twins[0, name].wait_recv()
            onward(0, name[:-1] + "s")
        settle("yo")

        def experts_of(place):
            rows = pl.ds(pl.multiple_of(place * tall, tall), tall)
            gate = jnp.dot(all_rows[rows], wg[...], preferred_element_type=f32)
            raised = jnp.dot(all_rows[rows], wu[...], preferred_element_type=f32)
            act_ref[rows] = (gate / (1.0 + jnp.exp(-gate)) * raised).astype(bf16)

        def route():
            own = all_rows[pl.ds(pl.multiple_of(s * tall, tall), tall)]
            logits = lax.dot_general(wr_ref[...], own, nt, preferred_element_type=f32)
            odds = jnp.exp(logits - jnp.max(logits, 0, keepdims=True))
            probs = odds / jnp.sum(odds, 0, keepdims=True)
            expert = lax.broadcasted_iota(jnp.int32, (experts, tall), 0)
            named = jnp.zeros((experts, tall), f32)
            for n in range(topk):
                named = jnp.where(routes_ref[n : n + 1] == expert, 1.0, named)
            share = probs * named
            for n in range(experts):
                share_own[n] = share[n : n + 1]
            share_out[s] = share_own[s]
            for d in range(1, blocks):
                dest = (s + d) % blocks
                shares.append(send(share_own.at[dest], share_out.at[s], {"seq": dest}))

        shares = []

        def job(t, along, owner):
            def act():
                if owner == "first":
                    names = pieces if t < HOPS else some
                    if along < 0:
                        for p in names:
                            twins[t, p].wait_recv()
                        for p in ("ao", "as") if t < HOPS else ("ao",):
                            twins[t, "y" + p].wait_recv()
                experts_of(chip_at(r - step * t * along) * 2 + (0 if owner == "first" else 1))
            return act

        def own_job():
            experts_of(s)

        def sibling_job():
            twins[0, "yo"].wait_recv()
            experts_of(s + step)

        jobs = {0: [route], 1: [own_job], 3: [sibling_job]}
        for t in range(1, HOPS):
            at = 6 * t + (1 if t < HOPS - 1 else 0)
            for k, (along, owner) in enumerate(((1, "first"), (1, "second"), (-1, "first"), (-1, "second"))):
                jobs.setdefault(at + k, []).append(job(t, along, owner))
        late = []

        def drain(limit):
            while late and late[0][0] <= limit:
                _, t, p = late.pop(0)
                cross[t, p].wait_recv()
                put(twins, (t, "y" + p), -step * t, "y" + p[1], sib)

        loads[4].wait()
        loads[5].wait()
        for n, (t, p) in enumerate(order):
            circle[t, p].wait_recv()
            onward(t, p)
            if p in ("ao", "as"):
                put(cross, (t, p), -step * t, p, other)
                late.append((n, t, p))
            put(twins, (t, p), -step * t, p, sib)
            drain(n - 4)
            for act in jobs.pop(n, ()):
                act()
        drain(len(order))
        for n in sorted(jobs):
            for act in jobs[n]:
                act()
        for p in some + ("yao",):
            twins[HOPS, p].wait_recv()
        last = chip_at(r + HOPS) * 2
        experts_of(last)
        experts_of(last + 1)
        for copy in shares:
            copy.wait_recv()
        for copy in sent:
            copy.wait_send()

    vmem, smem = pl.BlockSpec(memory_space=VMEM), pl.BlockSpec(memory_space=pltpu.SMEM)
    return pl.pallas_call(
        kernel,
        out_shape=(
            jax.ShapeDtypeStruct((tall, width), bf16),
            jax.ShapeDtypeStruct((blocks * tall, hidden), bf16),
            jax.ShapeDtypeStruct((blocks, 1, tall), f32),
        ),
        in_specs=[smem] * 3 + [vmem] * 9 + [pl.BlockSpec(memory_space=pl.ANY)] * 6,
        out_specs=(vmem, vmem, vmem),
        scratch_shapes=[
            VMEM((width, local), bf16),
            VMEM((width, local), bf16),
            VMEM((width, local), bf16),
            VMEM((local, width), bf16),
            VMEM((width, hidden), bf16),
            VMEM((width, hidden), bf16),
            VMEM((tall, width), bf16),
            VMEM((tall, width), bf16),
            VMEM((2, cached, local), bf16),
            VMEM((groups, near, 2 * pair), bf16),
            VMEM((tall, local), bf16),
            VMEM((tall, local), bf16),
            VMEM((tall, cached + near), f32),
            VMEM((tall, width), bf16),
            VMEM((tall, width), bf16),
            VMEM((blocks * tall, width), bf16),
            VMEM((experts, 1, tall), f32),
            pltpu.SemaphoreType.DMA((6,)),
            pltpu.SemaphoreType.DMA((sems,)),
            pltpu.SemaphoreType.DMA((sems,)),
        ],
        compiler_params=pltpu.CompilerParams(
            collective_id=8, has_side_effects=True, vmem_limit_bytes=60 << 20
        ),
        name="front",
    )(lengths, request_group, shard_group, tokens, gain.reshape(1, width), cosine, sine, prefix_keys,
      prefix_values, moe_gain.reshape(1, width), w_router.T, routes.T, w_query, w_key, w_value, w_out,
      w_gate, w_up)


def attention(query, prefix_keys, prefix_values, suffix, bias):
    tall, wide = query.shape
    heads = wide // HD
    cached = prefix_keys.shape[0]
    keys = bias.shape[1]
    many = len(suffix)
    scale = HD ** (-0.5)

    def kernel(query_ref, cached_k, cached_v, bias_ref, *rest):
        suffix_k, suffix_v, out_ref = rest[:many], rest[many : 2 * many], rest[2 * many]
        head = query_ref[...]
        scores = [
            lax.dot_general(
                head, block[...], (((1,), (1,)), ((), ())), preferred_element_type=jnp.float32
            )
            for block in (cached_k, *suffix_k)
        ]
        scores = jnp.concatenate(scores, 1) * scale + bias_ref[...]
        weights = jnp.exp(scores - jnp.max(scores, -1, keepdims=True))
        total = jnp.sum(weights, -1, keepdims=True)
        weights = weights.astype(jnp.bfloat16)
        summed = jnp.dot(weights[:, :cached], cached_v[...], preferred_element_type=jnp.float32)
        for n, block in enumerate(suffix_v):
            start = cached + n * tall
            summed += jnp.dot(
                weights[:, start : start + tall], block[...], preferred_element_type=jnp.float32
            )
        out_ref[...] = (summed / total).astype(jnp.bfloat16)

    def column(rows, offset):
        return pl.BlockSpec((rows, HD), lambda h: (0, h + offset))

    return pl.pallas_call(
        kernel,
        out_shape=jax.ShapeDtypeStruct((tall, wide), jnp.bfloat16),
        grid=(heads,),
        in_specs=[column(tall, 0), column(cached, 0), column(cached, 0)]
        + [pl.BlockSpec((tall, keys), lambda h: (0, 0))]
        + [column(tall, 0)] * many
        + [column(tall, heads)] * many,
        out_specs=column(tall, 0),
        cost_estimate=pl.CostEstimate(
            flops=4 * tall * keys * wide, bytes_accessed=4 * keys * wide, transcendentals=0
        ),
        name="attention",
    )(query, prefix_keys, prefix_values, bias, *suffix, *suffix)


def on_device(
    tokens,
    attn_gain,
    w_query,
    w_key,
    w_value,
    w_out,
    prefix_keys,
    prefix_values,
    shard_group,
    request_group,
    lengths,
    moe_gain,
    w_router,
    w_gate,
    w_up,
    w_down,
    routes,
    final_gain,
    w_head,
):
    f32 = jnp.float32
    bf16 = jnp.bfloat16
    seq_index = lax.axis_index("seq")
    tp_index = lax.axis_index("tp")
    seq_count = lax.axis_size("seq")
    tp_count = lax.axis_size("tp")
    tok_dev = tokens.shape[0]
    width_part = tokens.shape[1]
    shard_rows = prefix_keys.shape[0]
    prefix_length = shard_rows * seq_count // 2
    ends = prefix_sums(lengths)
    experts = w_router.shape[1]
    topk = routes.shape[1]
    local_index = seq_index * tok_dev + jnp.arange(tok_dev)
    if seq_count == 16 and tp_count == 2 and experts == seq_count:
        begun = jnp.max(jnp.where(local_index[:, None] >= ends[None, :], ends[None, :], 0), 1)
        half = HD // 2
        freq = 10000.0 ** (-jnp.arange(half).astype(f32) / half)
        angle = (prefix_length + local_index - begun).astype(f32)[:, None] * freq[None, :]
        cosine, sine = jnp.cos(angle), jnp.sin(angle)
        resid_full, act, shares = front(
            tokens, attn_gain, w_query, w_key, w_value, w_out, prefix_keys, prefix_values, lengths,
            request_group, shard_group, jnp.concatenate([cosine, cosine], 1),
            jnp.concatenate([-sine, sine], 1), moe_gain, w_router, routes,
            w_gate[0], w_up[0],
        )
        own_share = shares.reshape(-1, 1)
        partial_out = (jnp.dot(act, w_down[0], preferred_element_type=f32) * own_share).astype(bf16)
        hidden = collect_ring(partial_out, resid_full)
        return (hidden, head_tail(hidden, lengths, final_gain, w_head))
    full_x = gather_columns(tokens)
    width = full_x.shape[1]
    normed = normalize(full_x.astype(f32), attn_gain).astype(bf16)
    heads = w_query.shape[1] // HD
    starts = ends - lengths
    own_request = request_of(local_index, ends)
    own_start = lookup(own_request, starts)
    own_group = lookup(own_request, request_group)
    position = (prefix_length + local_index - own_start).astype(f32)
    query = rotate(
        jnp.dot(normed, w_query, preferred_element_type=f32).reshape(tok_dev, heads, HD), position
    ).astype(bf16)
    key_rows = rotate(
        jnp.dot(normed, w_key, preferred_element_type=f32).reshape(tok_dev, heads, HD), position
    ).astype(bf16)
    key_rows = key_rows.reshape(tok_dev, heads * HD)
    value_rows = jnp.dot(normed, w_value, preferred_element_type=f32).astype(bf16)
    pieces = (
        lax.all_gather(prefix_keys, "seq", axis=0, tiled=True),
        lax.all_gather(prefix_values, "seq", axis=0, tiled=True),
    )
    count = pieces[0].shape[0]
    shard_ids = jnp.arange(count) // shard_rows
    key_group = lookup(shard_ids, shard_group)
    fold_allowed = own_group[:, None] == key_group[None, :]
    own_allowed = (own_request[:, None] == own_request[None, :]) & (
        local_index[None, :] <= local_index[:, None]
    )
    both_rows = jnp.concatenate([key_rows, value_rows], 1)
    suffix = [both_rows] + [from_behind(both_rows, "seq", step) for step in range(1, SPAN + 1)]
    permitted = [fold_allowed, own_allowed]
    for step in range(1, SPAN + 1):
        key_index = (seq_index - step) * tok_dev + jnp.arange(tok_dev)
        key_request = request_of(key_index, ends)
        permitted.append(
            (key_index >= 0)[None, :] & (own_request[:, None] == key_request[None, :])
        )
    bias = jnp.where(jnp.concatenate(permitted, 1), 0.0, NEGATIVE)
    attended = attention(query.reshape(tok_dev, heads * HD), *pieces, suffix, bias)
    mixed = jnp.dot(attended, w_out, preferred_element_type=f32).astype(bf16)
    resid_full = (full_x.astype(f32) + sum_over_tp(mixed)).astype(bf16)
    moe_in = normalize(resid_full.astype(f32), moe_gain).astype(bf16)
    probs = jax.nn.softmax(jnp.dot(moe_in, w_router, preferred_element_type=f32), -1)
    flat = routes.reshape(-1)
    hits = (flat[:, None] == jnp.arange(experts)[None, :]).astype(jnp.int32)
    line = jnp.arange(flat.shape[0])
    before = (line[:, None] > line[None, :]).astype(bf16)
    earlier = jnp.dot(before, hits.astype(bf16), preferred_element_type=f32).astype(jnp.int32)
    rank = jnp.sum(earlier * hits, 1)
    capacity = min(tok_dev, tp_count * max(1, 3 * tok_dev * topk // (2 * experts * tp_count)))
    target = flat * capacity + rank
    route_weight = jnp.sum(hits.reshape(tok_dev, topk, experts).astype(f32) * probs[:, None, :], -1)
    repeated = jnp.repeat(moe_in, topk, axis=0)
    outgoing = (
        jnp.zeros((experts * capacity, width), bf16)
        .at[target]
        .set(repeated)
        .reshape(experts, capacity, width)
    )
    arrived = lax.all_to_all(outgoing, "seq", split_axis=0, concat_axis=0, tiled=True)
    sources = arrived.shape[0]
    count = arrived.shape[1]
    rows = arrived.reshape(sources * count, width)
    gate = jnp.dot(rows, w_gate[0], preferred_element_type=f32)
    up = jnp.dot(rows, w_up[0], preferred_element_type=f32)
    act = (jax.nn.silu(gate) * up).astype(bf16)
    partial_out = jnp.dot(act, w_down[0], preferred_element_type=f32).reshape(sources, count, width)
    summed = lax.psum_scatter(partial_out, "tp", scatter_dimension=2, tiled=True).astype(bf16)
    returned = lax.all_to_all(summed, "seq", split_axis=0, concat_axis=0, tiled=True)
    picked = returned.reshape(experts * capacity, width_part)[target].reshape(
        tok_dev, topk, width_part
    )
    moe_part = jnp.sum(picked.astype(f32) * route_weight[:, :, None], 1)
    resid = lax.dynamic_slice_in_dim(resid_full, tp_index * width_part, width_part, 1)
    hidden = (resid.astype(f32) + moe_part).astype(bf16)
    last_hit = ((ends - 1)[:, None] == local_index[None, :]).astype(bf16)
    chosen = jnp.dot(last_hit, hidden, preferred_element_type=f32)
    final = last_rows(chosen, final_gain, width)
    log_probs = log_softmax(jnp.dot(final, w_head, preferred_element_type=f32))
    return (hidden, log_probs)


def solution(mesh):
    in_specs = (
        P("seq", "tp"),
        P(),
        P(None, "tp"),
        P(None, "tp"),
        P(None, "tp"),
        P("tp", None),
        P("seq", "tp"),
        P("seq", "tp"),
        P(),
        P(),
        P(),
        P(),
        P(),
        P("seq", None, "tp"),
        P("seq", None, "tp"),
        P("seq", "tp", None),
        P("seq", None),
        P("tp"),
        P("tp", "seq"),
    )
    out_specs = (P("seq", "tp"), P(None, "seq"))
    return jax.shard_map(
        on_device, mesh=mesh, in_specs=in_specs, out_specs=out_specs, check_vma=False
    )
```

```python
import jax
import jax.numpy as jnp
from jax import lax
from jax.experimental import pallas as pl
from jax.experimental.pallas import tpu as pltpu
from jax.sharding import PartitionSpec as P

HD = 128
SPAN = 4
VMEM = pltpu.VMEM


EPS = 1e-05
NEGATIVE = -1e30


def from_behind(value, axis, steps):
    count = lax.axis_size(axis)
    leading, last = (max(0, -steps), min(count, count - steps))
    return lax.ppermute(value, axis, [(source, source + steps) for source in range(leading, last)])


def normalize(rows, gain):
    inv = lax.rsqrt(jnp.mean(rows * rows, -1, keepdims=True) + EPS)
    return rows * inv * gain.astype(jnp.float32)


def rotate(vectors, position):
    half = vectors.shape[-1] // 2
    freq = 10000.0 ** (-jnp.arange(half).astype(jnp.float32) / half)
    angle = position[:, None] * freq[None, :]
    cosine = jnp.cos(angle)[:, None, :]
    sine = jnp.sin(angle)[:, None, :]
    first = vectors[..., :half]
    second = vectors[..., half:]
    return jnp.concatenate([first * cosine - second * sine, second * cosine + first * sine], -1)


def request_of(index, ends):
    return jnp.sum((index[:, None] >= ends[None, :]).astype(jnp.int32), 1)


def lookup(selector, table):
    hit = selector[:, None] == jnp.arange(table.shape[0])[None, :]
    return jnp.sum(jnp.where(hit, table[None, :], 0), 1)


def prefix_sums(values):
    order = jnp.arange(values.shape[0])
    return jnp.sum(jnp.where(order[:, None] >= order[None, :], values[None, :], 0), 1)


def partner(axis, bit):
    index = lax.axis_index(axis)
    span = 1 << bit
    other = index + span - 2 * span * ((index // span) % 2)
    return {axis: other}


def greet(stages):
    barrier = pltpu.get_barrier_semaphore()
    for axis, bit in stages:
        pl.semaphore_signal(barrier, inc=1, device_id=partner(axis, bit))
    pl.semaphore_wait(barrier, len(stages))


def swap(source, target, send_sem, recv_sem, stage):
    copy = pltpu.make_async_remote_copy(
        src_ref=source, dst_ref=target, send_sem=send_sem, recv_sem=recv_sem,
        device_id=partner(*stage),
    )
    copy.start()
    return copy


def bits_of(axis):
    return [(axis, bit) for bit in range(lax.axis_size(axis).bit_length() - 1)]


def last_rows(chosen, gain, width):
    seq_stages, tp_stages = bits_of("seq"), bits_of("tp")
    stages = seq_stages + tp_stages
    rows, part = chosen.shape

    def kernel(chosen_ref, gain_ref, out_ref, held, got, sq_held, sq_got, send_sem, recv_sem):
        greet(stages)
        held[0] = chosen_ref[...]
        count = len(seq_stages)
        for k, stage in enumerate(seq_stages):
            swap(held.at[k], got.at[k], send_sem.at[k], recv_sem.at[k], stage).wait()
            held[k + 1] = held[k] + got[k]
        total = held[count]
        sq_held[0] = jnp.broadcast_to(jnp.sum(total * total, -1, keepdims=True), (rows, 128))
        for k, stage in enumerate(tp_stages):
            n = count + k
            swap(sq_held.at[k], sq_got.at[k], send_sem.at[n], recv_sem.at[n], stage).wait()
            sq_held[k + 1] = sq_held[k] + sq_got[k]
        square = sq_held[len(tp_stages)][:, :1]
        scaled = total * lax.rsqrt(square / width + EPS) * gain_ref[...].astype(jnp.float32)
        out_ref[...] = scaled.astype(jnp.bfloat16)

    ns, nt = len(seq_stages), len(tp_stages)
    return pl.pallas_call(
        kernel,
        out_shape=jax.ShapeDtypeStruct((rows, part), jnp.bfloat16),
        in_specs=[pl.BlockSpec(memory_space=VMEM)] * 2,
        out_specs=pl.BlockSpec(memory_space=VMEM),
        scratch_shapes=[
            VMEM((ns + 1, rows, part), jnp.float32),
            VMEM((ns, rows, part), jnp.float32),
            VMEM((nt + 1, rows, 128), jnp.float32),
            VMEM((nt, rows, 128), jnp.float32),
            pltpu.SemaphoreType.DMA((ns + nt,)),
            pltpu.SemaphoreType.DMA((ns + nt,)),
        ],
        compiler_params=pltpu.CompilerParams(collective_id=1, has_side_effects=True),
        name="last_rows",
    )(chosen, gain.reshape(1, part))


def log_softmax(logits):
    seq_stages, tp_stages = bits_of("seq"), bits_of("tp")
    stages = tp_stages + seq_stages
    rows, part = logits.shape

    def kernel(logits_ref, out_ref, held, got, st_held, st_got, send_sem, recv_sem):
        greet(stages)
        held[0] = logits_ref[...]
        count = len(tp_stages)
        for k, stage in enumerate(tp_stages):
            swap(held.at[k], got.at[k], send_sem.at[k], recv_sem.at[k], stage).wait()
            held[k + 1] = held[k] + got[k]
        total = held[count]
        peak = jnp.max(total, -1, keepdims=True)
        mass = jnp.sum(jnp.exp(total - peak), -1, keepdims=True)
        st_held[0, :, :128] = jnp.broadcast_to(peak, (rows, 128))
        st_held[0, :, 128:] = jnp.broadcast_to(mass, (rows, 128))
        for k, stage in enumerate(seq_stages):
            n = count + k
            swap(st_held.at[k], st_got.at[k], send_sem.at[n], recv_sem.at[n], stage).wait()
            mine, theirs = st_held[k, :, :128], st_got[k, :, :128]
            top = jnp.maximum(mine, theirs)
            st_held[k + 1, :, :128] = top
            st_held[k + 1, :, 128:] = st_held[k, :, 128:] * jnp.exp(mine - top) + st_got[
                k, :, 128:
            ] * jnp.exp(theirs - top)
        last = len(seq_stages)
        out_ref[...] = total - st_held[last, :, :1] - jnp.log(st_held[last, :, 128:129])

    ns, nt = len(seq_stages), len(tp_stages)
    return pl.pallas_call(
        kernel,
        out_shape=jax.ShapeDtypeStruct((rows, part), jnp.float32),
        in_specs=[pl.BlockSpec(memory_space=VMEM)],
        out_specs=pl.BlockSpec(memory_space=VMEM),
        scratch_shapes=[
            VMEM((nt + 1, rows, part), jnp.float32),
            VMEM((nt, rows, part), jnp.float32),
            VMEM((ns + 1, rows, 256), jnp.float32),
            VMEM((ns, rows, 256), jnp.float32),
            pltpu.SemaphoreType.DMA((ns + nt,)),
            pltpu.SemaphoreType.DMA((ns + nt,)),
        ],
        compiler_params=pltpu.CompilerParams(collective_id=2, has_side_effects=True),
        name="log_softmax",
    )(logits)


def gather_columns(block):
    stages = bits_of("tp")
    rows, part = block.shape
    count = lax.axis_size("tp")

    def kernel(block_ref, out_ref, send_sem, recv_sem):
        greet(stages)
        me = lax.axis_index("tp")
        out_ref[:, pl.ds(pl.multiple_of(me * part, part), part)] = block_ref[...]
        for k, stage in enumerate(stages):
            wide = part << k
            start = pl.multiple_of((me // (1 << k)) * wide, wide)
            piece = out_ref.at[:, pl.ds(start, wide)]
            swap(piece, piece, send_sem.at[k], recv_sem.at[k], stage).wait()

    return pl.pallas_call(
        kernel,
        out_shape=jax.ShapeDtypeStruct((rows, part * count), block.dtype),
        in_specs=[pl.BlockSpec(memory_space=VMEM)],
        out_specs=pl.BlockSpec(memory_space=VMEM),
        scratch_shapes=[pltpu.SemaphoreType.DMA((len(stages),))] * 2,
        compiler_params=pltpu.CompilerParams(collective_id=3, has_side_effects=True),
        name="gather_columns",
    )(block)


def sum_over_tp(block):
    stages = bits_of("tp")
    rows, part = block.shape

    def kernel(block_ref, out_ref, held, got, send_sem, recv_sem):
        greet(stages)
        for k, stage in enumerate(stages):
            source = block_ref if k == 0 else held.at[k]
            swap(source, got.at[k], send_sem.at[k], recv_sem.at[k], stage).wait()
            total = source[...].astype(jnp.float32) + got[k].astype(jnp.float32)
            if k + 1 < len(stages):
                held[k + 1] = total.astype(jnp.bfloat16)
            else:
                out_ref[...] = total

    count = len(stages)
    return pl.pallas_call(
        kernel,
        out_shape=jax.ShapeDtypeStruct((rows, part), jnp.float32),
        in_specs=[pl.BlockSpec(memory_space=VMEM)],
        out_specs=pl.BlockSpec(memory_space=VMEM),
        scratch_shapes=[
            VMEM((count, rows, part), jnp.bfloat16),
            VMEM((count, rows, part), jnp.bfloat16),
            pltpu.SemaphoreType.DMA((count,)),
            pltpu.SemaphoreType.DMA((count,)),
        ],
        compiler_params=pltpu.CompilerParams(collective_id=4, has_side_effects=True),
        name="sum_over_tp",
    )(block)


HOPS = 4


def ring_place():
    s = lax.axis_index("seq")
    core = s % 2
    x = (s // 2) % 2
    z = s // 4
    return s, core, z + x * (7 - 2 * z)


def chip_at(place):
    q = (place + 16) % 8
    x = q // 4
    z = q + x * (7 - 2 * q)
    return z * 2 + x


def greet_all(blocks):
    s = lax.axis_index("seq")
    barrier = pltpu.get_barrier_semaphore()
    for d in range(1, blocks):
        pl.semaphore_signal(barrier, inc=1, device_id={"seq": (s + d) % blocks})
    pl.semaphore_signal(barrier, inc=1, device_id={"tp": 1 - lax.axis_index("tp")})
    pl.semaphore_wait(barrier, blocks)


def back(act, shares, w_down, resid, lengths, gain, w_head):
    tall, wide = resid.shape
    half = wide // 2
    hidden = act.shape[1]
    count = shares.shape[0]
    reqs = lengths.shape[0]
    cols = w_head.shape[1]
    padded = -(-cols // 128) * 128
    high = -(-reqs // 16) * 16
    cuts = 4
    per = -(-cols // (128 * cuts)) * 128
    spans = [(k * per, min(per, cols - k * per)) for k in range(cuts)]
    f32 = jnp.float32
    ty = tall // 2
    ts = tall - ty
    sems = 80
    bf16 = jnp.bfloat16
    G = 16
    units = [(HOPS, "o")] + [(t, b) for t in range(HOPS - 1, 0, -1) for b in ("s", "o")] + [(0, "o")]
    nu = len(units)

    def kernel(len_ref, act_ref, share_ref, resid_ref, gain_ref, wd_ref, wh_ref, out_ref, logs_ref, wd,
               wh, part_ref, sib_buf, acc_y, acc_s, y_send, y_recv, ring_y, ring_s, far_y, far_s, last_recv,
               near, far, logit, got, stats, w_sem, send_sem, recv_sem):
        loads = []
        for n, (source, target) in enumerate(((wd_ref, wd), (wh_ref, wh))):
            loads.append(pltpu.make_async_copy(source, target, w_sem.at[n]))
            loads[n].start()
        s, core, r = ring_place()
        y = lax.axis_index("tp")
        step = 1 - 2 * core
        nxt = {"seq": chip_at(r + step) * 2 + core}
        sib = {"seq": s + step}
        other = {"tp": 1 - y}
        eye = lax.broadcasted_iota(jnp.int32, (tall, tall), 0) == lax.broadcasted_iota(
            jnp.int32, (tall, tall), 1
        )

        def project(place):
            rows = pl.ds(pl.multiple_of(place * tall, tall), tall)
            weight = jnp.sum(jnp.where(eye, share_ref[place], 0.0), -1, keepdims=True)
            product = jnp.dot(act_ref[rows], wd[...], preferred_element_type=f32)
            part_ref[rows] = (product * weight).astype(bf16)

        greet_all(count)
        loads[0].wait()
        used = iter(range(sems))
        own_cols = pl.ds(pl.multiple_of(y * half, half), half)
        far_cols = pl.ds(pl.multiple_of((1 - y) * half, half), half)

        def send(source, target, device):
            n = next(used)
            copy = pltpu.make_async_remote_copy(
                src_ref=source, dst_ref=target, send_sem=send_sem.at[n], recv_sem=recv_sem.at[n],
                device_id=device,
            )
            copy.start()
            return copy

        def rows_of(t, b, direction, c):
            return chip_at(r + direction * t) * 2 + (c if b == "o" else 1 - c)

        pair, cross, ring, sent = {}, {}, {}, []

        def lend(i):
            if i < nu:
                place = rows_of(*units[i], -step, 1 - core)
                project(place)
                start = pl.multiple_of(place * tall, tall)
                pair[i] = send(part_ref.at[pl.ds(start, tall)], sib_buf.at[i], sib)
                sent.append(pair[i])

        lend(0)
        lend(1)

        def summed(i):
            t, b = units[i]
            place = rows_of(t, b, step, core)
            project(place)
            start = place * tall
            pair[i].wait_recv()

            def body_y(g, _):
                rows = pl.ds(pl.multiple_of(g * G, G), G)
                here = pl.ds(pl.multiple_of(start + g * G, G), G)
                y_send[i, rows] = part_ref[here, far_cols] + sib_buf[i, rows, far_cols]
                acc_y[i, rows] = part_ref[here, own_cols] + sib_buf[i, rows, own_cols]
                return 0

            lax.fori_loop(0, ty // G, body_y, 0)
            cross[i] = send(y_send.at[i], y_recv.at[i], other)
            sent.append(cross[i])

            def body_s(g, _):
                rows = pl.ds(pl.multiple_of(g * G, G), G)
                below = pl.ds(pl.multiple_of(ty + g * G, G), G)
                here = pl.ds(pl.multiple_of(start + ty + g * G, G), G)
                acc_s[i, rows] = part_ref[here] + sib_buf[i, below]
                return 0

            lax.fori_loop(0, ts // G, body_s, 0)
            if not arriving(t, b) and t > 0:
                pass_s(i)
            lend(i + 2)

        def slot(t, b):
            return 2 * t + (0 if b == "o" else 1)

        def arriving(t, b):
            return (t + 1, b) in units and t > 0

        def pass_s(i):
            t, b = units[i]
            m = slot(t - 1, b)
            ring[t - 1, b, "s"] = send(acc_s.at[i], ring_s.at[m], nxt)
            sent.append(ring[t - 1, b, "s"])

        def passed(i):
            t, b = units[i]
            arrived = arriving(t, b)
            n = slot(t, b)
            if arrived:
                ring[t, b, "s"].wait_recv()

                def body_s(g, _):
                    rows = pl.ds(pl.multiple_of(g * G, G), G)
                    acc_s[i, rows] = acc_s[i, rows] + ring_s[n, rows]
                    return 0

                lax.fori_loop(0, ts // G, body_s, 0)
                pass_s(i)
                ring[t, b, "y"].wait_recv()
            cross[i].wait_recv()

            def body_y(g, _):
                rows = pl.ds(pl.multiple_of(g * G, G), G)
                total = acc_y[i, rows] + y_recv[i, rows]
                if arrived:
                    total = total + ring_y[n, rows]
                acc_y[i, rows] = total
                return 0

            lax.fori_loop(0, ty // G, body_y, 0)
            if t > 0:
                m = slot(t - 1, b)
                ring[t - 1, b, "y"] = send(acc_y.at[i], ring_y.at[m], nxt)
                sent.append(ring[t - 1, b, "y"])

        summed(0)
        for i in range(1, nu):
            summed(i)
            passed(i - 1)
        passed(nu - 1)
        m, n, i = slot(0, "s"), slot(0, "o"), nu - 1
        ring[0, "s", "s"].wait_recv()
        far_copy_s = send(ring_s.at[m], far_s, sib)
        ring[0, "s", "y"].wait_recv()
        far_copy_y = send(ring_y.at[m], far_y, sib)
        sent.extend((far_copy_s, far_copy_y))
        ring[0, "o", "s"].wait_recv()
        far_copy_s.wait_recv()

        def body_s(g, _):
            rows = pl.ds(pl.multiple_of(g * G, G), G)
            acc_s[i, rows] = acc_s[i, rows] + ring_s[n, rows] + far_s[rows]
            return 0

        lax.fori_loop(0, ts // G, body_s, 0)
        last = send(acc_s.at[i, :, far_cols], last_recv, other)
        sent.append(last)
        ring[0, "o", "y"].wait_recv()
        far_copy_y.wait_recv()

        def body_y(g, _):
            rows = pl.ds(pl.multiple_of(g * G, G), G)
            total = acc_y[i, rows].astype(f32) + ring_y[n, rows].astype(f32) + far_y[rows].astype(f32)
            out_ref[rows] = (total + resid_ref[rows, own_cols].astype(f32)).astype(bf16)
            return 0

        lax.fori_loop(0, ty // G, body_y, 0)
        last.wait_recv()

        def body_l(g, _):
            rows = pl.ds(pl.multiple_of(g * G, G), G)
            here = pl.ds(pl.multiple_of(ty + g * G, G), G)
            total = acc_s[i, rows, own_cols].astype(f32) + last_recv[rows].astype(f32)
            out_ref[here] = (total + resid_ref[here, own_cols].astype(f32)).astype(bf16)
            return 0

        lax.fori_loop(0, ts // G, body_l, 0)
        row = lax.broadcasted_iota(jnp.int32, (high, tall), 0)
        place = lax.broadcasted_iota(jnp.int32, (high, tall), 1) + s * tall
        last = jnp.full((high, tall), -1, jnp.int32)
        end = 0
        for j in range(reqs):
            end = end + len_ref[j]
            last = jnp.where(row == j, end - 1, last)
        hit = (last == place).astype(f32).astype(bf16)
        near[0] = jnp.dot(hit, out_ref[...], preferred_element_type=f32).astype(bf16)

        def note(source, target, device):
            sent.append(send(source, target, device))
            return sent[-1]

        first = [
            note(near.at[0], near.at[d], {"seq": (s // 4) * 4 + (s + d) % 4}) for d in range(1, 4)
        ]
        for copy in first:
            copy.wait_recv()
        far[0] = (near[0] + near[1]) + (near[2] + near[3])
        second = [note(far.at[0], far.at[d], {"seq": (s + 4 * d) % count}) for d in range(1, 4)]
        for copy in second:
            copy.wait_recv()
        total = ((far[0] + far[1]) + (far[2] + far[3])).astype(f32)
        square = jnp.sum(total * total, -1, keepdims=True)
        scaled = (total * gain_ref[...].astype(f32)).astype(bf16)
        logit[:, padded:] = jnp.broadcast_to(square[:reqs], (reqs, 128))
        loads[1].wait()
        swapped = [note(logit.at[:, padded:], got.at[:, padded:], other)]
        for k, (start, size) in enumerate(spans):
            product = lax.dot_general(
                scaled, wh[start : start + size], (((1,), (1,)), ((), ())), preferred_element_type=f32
            )
            logit[:, start : start + size] = product[:reqs]
            full = per if k < cuts - 1 else padded - start
            swapped.append(note(logit.at[:, start : start + full], got.at[:, start : start + full], other))
        for copy in swapped:
            copy.wait_recv()
        square = logit[:, padded : padded + 1] + got[:, padded : padded + 1]
        inv = lax.rsqrt(square / wide + EPS)
        both = (logit[:, :cols] + got[:, :cols]) * inv
        peak = jnp.max(both, -1, keepdims=True)
        mass = jnp.sum(jnp.exp(both - peak), -1, keepdims=True)
        lane = lax.broadcasted_iota(jnp.int32, (reqs, 128), 1)
        stats[0] = jnp.where(lane < 64, peak, mass)
        third = [note(stats.at[0], stats.at[d], {"seq": (s + d) % count}) for d in range(1, count)]
        for copy in third:
            copy.wait_recv()
        everyone = stats[...]
        peaks, masses = everyone[:, :, :1], everyone[:, :, 64:65]
        top = jnp.max(peaks, 0)
        whole = jnp.sum(masses * jnp.exp(peaks - top[None]), 0)
        logs_ref[...] = both - top - jnp.log(whole)
        for copy in sent:
            copy.wait_send()

    vmem, hbm = pl.BlockSpec(memory_space=VMEM), pl.BlockSpec(memory_space=pl.ANY)
    return pl.pallas_call(
        kernel,
        out_shape=(
            jax.ShapeDtypeStruct((tall, half), bf16),
            jax.ShapeDtypeStruct((reqs, cols), f32),
        ),
        in_specs=[pl.BlockSpec(memory_space=pltpu.SMEM)] + [vmem] * 4 + [hbm] * 2,
        out_specs=(vmem, vmem),
        scratch_shapes=[
            VMEM((hidden, wide), bf16),
            VMEM((cols, half), bf16),
            VMEM((count * tall, wide), bf16),
            VMEM((nu, tall, wide), bf16),
            VMEM((nu, ty, half), bf16), VMEM((nu, ts, wide), bf16),
            VMEM((nu, ty, half), bf16), VMEM((nu, ty, half), bf16),
            VMEM((2 * HOPS, ty, half), bf16), VMEM((2 * HOPS, ts, wide), bf16),
            VMEM((ty, half), bf16), VMEM((ts, wide), bf16), VMEM((ts, half), bf16),
            VMEM((4, high, half), bf16), VMEM((4, high, half), bf16),
            VMEM((reqs, padded + 128), f32), VMEM((reqs, padded + 128), f32),
            VMEM((count, reqs, 128), f32),
            pltpu.SemaphoreType.DMA((2,)),
            pltpu.SemaphoreType.DMA((sems,)),
            pltpu.SemaphoreType.DMA((sems,)),
        ],
        compiler_params=pltpu.CompilerParams(
            collective_id=6, has_side_effects=True, vmem_limit_bytes=60 << 20
        ),
        name="back",
    )(lengths, act, shares, resid, gain.reshape(1, half), w_down, w_head.T)


def front(tokens, gain, w_query, w_key, w_value, w_out, prefix_keys, prefix_values, lengths,
          request_group, shard_group, cosine, sine, moe_gain, w_router, routes, w_gate, w_up):
    tall, part = tokens.shape
    width = 2 * part
    local = w_query.shape[1]
    shard = prefix_keys.shape[0]
    shards = shard_group.shape[0]
    reqs = lengths.shape[0]
    cached = shard * shards
    experts = w_router.shape[1]
    topk = routes.shape[1]
    bf16, f32 = jnp.bfloat16, jnp.float32
    pair = 2 * HD
    groups = local // pair
    slots = SPAN + 1
    near = slots * tall
    hidden = w_gate.shape[1]
    blocks = 16
    q = tall // 4
    sems = 136
    scale = HD ** (-0.5)
    nt = (((1,), (1,)), ((), ()))

    def kernel(len_ref, rg_ref, sg_ref, tok_ref, gain_ref, cos_ref, sin_ref, pk_ref, pv_ref, mg_ref,
               wr_ref, routes_ref, wq_ref, wk_ref, wv_ref, wo_ref, wg_ref, wu_ref, resid_ref, act_ref,
               share_out, wq, wk, wv, wo, wg, wu, x, normed, cache, kv, query, attended, bias, mix, mix_got,
               all_rows, share_own, w_sem, send_sem, recv_sem):
        loads = {}
        for n, (source, target) in enumerate((
            (wk_ref, wk), (wv_ref, wv), (wq_ref, wq), (wo_ref, wo), (wg_ref, wg), (wu_ref, wu)
        )):
            loads[n] = pltpu.make_async_copy(source, target, w_sem.at[n])
            loads[n].start()
        s, core, r = ring_place()
        y = lax.axis_index("tp")
        count = 16
        step = 1 - 2 * core
        ahead = 1 - 2 * ((s // 2) % 2)
        nxt = {"seq": chip_at(r + step) * 2 + core}
        sib = {"seq": s + step}
        side = {"seq": s + 2 * ahead}
        above = {"seq": (s + 4) % count}
        other = {"tp": 1 - y}
        own_cols = pl.ds(pl.multiple_of(y * part, part), part)
        x[:, own_cols] = tok_ref[...]
        own_rows = pl.ds(pl.multiple_of(s * shard, shard), shard)
        cache[0, own_rows] = pk_ref[...]
        cache[1, own_rows] = pv_ref[...]
        greet_all(count)
        used = iter(range(sems))
        sent = []

        def send(source, target, device):
            n = next(used)
            copy = pltpu.make_async_remote_copy(
                src_ref=source, dst_ref=target, send_sem=send_sem.at[n], recv_sem=recv_sem.at[n],
                device_id=device,
            )
            copy.start()
            sent.append(copy)
            return copy

        def move(chip, name, device):
            which, owner = name
            shift = core if owner == "o" else 1 - core
            rows = pl.ds(pl.multiple_of((chip * 2 + shift) * shard, shard), shard)
            view = cache.at[which, rows]
            return send(view, view, device)

        home = chip_at(r)
        swapped = [move(home, (which, "o"), sib) for which in range(2)]
        ring, twin = {}, {}
        for which in range(2):
            ring[1, (which, "o")] = move(home, (which, "o"), nxt)
        crossing = send(tok_ref, x.at[:, own_cols], other)
        for which in range(2):
            swapped[which].wait_recv()
            ring[1, (which, "s")] = move(home, (which, "s"), nxt)

        def hop(t):
            chip = chip_at(r - step * t)
            owners = ("o", "s") if t < HOPS else ("o",)
            for owner in owners:
                for which in range(2):
                    name = (which, owner)
                    ring[t, name].wait_recv()
                    if t < HOPS - 1 or (t == HOPS - 1 and owner == "o"):
                        ring[t + 1, name] = move(chip, name, nxt)
                    twin[t, name] = move(chip, name, sib)

        lane = lax.broadcasted_iota(jnp.int32, (tall, 128), 0) + s * tall
        mine = jnp.zeros((tall, 128), jnp.int32)
        ends, end = [], 0
        for j in range(reqs):
            end = end + len_ref[j]
            ends.append(end)
        for j in range(reqs):
            mine = mine + (lane >= ends[j]).astype(jnp.int32)
        group = jnp.zeros((tall, 128), jnp.int32)
        for j in range(reqs):
            group = jnp.where(mine == j, rg_ref[j], group)
        own_index, own_request, own_group = lane[:, :1], mine[:, :1], group[:, :1]
        column = lax.broadcasted_iota(jnp.int32, (8, cached), 1)
        key_group = jnp.zeros((8, cached), jnp.int32)
        for j in range(shards):
            inside = (column >= j * shard) & (column < (j + 1) * shard)
            key_group = jnp.where(inside, sg_ref[j], key_group)
        bias[:, :cached] = jnp.where(own_group == key_group[:1], 0.0, NEGATIVE)
        chip = s // 2
        bases = (
            s * tall, (chip - 1) * 2 * tall, (chip - 1) * 2 * tall + tall, (chip - 2) * 2 * tall + tall,
            (chip - 2 + 2 * core) * 2 * tall,
        )
        for n in range(slots):
            place = lax.broadcasted_iota(jnp.int32, (8, tall), 1) + bases[n]
            theirs = jnp.zeros((8, tall), jnp.int32)
            for j in range(reqs):
                theirs = theirs + (place >= ends[j]).astype(jnp.int32)
            seen = (own_request == theirs[:1]) & (place[:1] <= own_index) & (place[:1] >= 0)
            start = cached + n * tall
            bias[:, start : start + tall] = jnp.where(seen, 0.0, NEGATIVE)
        hop(1)
        crossing.wait_recv()
        rows = x[...].astype(f32)
        inv = lax.rsqrt(jnp.mean(rows * rows, -1, keepdims=True) + EPS)
        normed[...] = (rows * inv * gain_ref[...].astype(f32)).astype(bf16)

        def turned(value):
            heads = []
            for n in range(pair // HD):
                head = value[:, n * HD : (n + 1) * HD]
                heads.append(head * cos_ref[...] + pltpu.roll(head, HD // 2, 1) * sin_ref[...])
            return jnp.concatenate(heads, 1).astype(bf16)

        back = 4 - core
        side_slot = 1 + core

        def slot_of(g, n):
            return kv.at[g, pl.ds(pl.multiple_of(n * tall, tall), tall)]

        up = {}

        def keys_of(g):
            cols = slice(g * pair, (g + 1) * pair)
            key = jnp.dot(normed[...], wk[:, cols], preferred_element_type=f32)
            kv[g, :tall, :pair] = turned(key)
            value = jnp.dot(normed[...], wv[:, cols], preferred_element_type=f32)
            kv[g, :tall, pair:] = value.astype(bf16)
            up[g] = send(slot_of(g, 0), slot_of(g, back), above)

        loads[0].wait()
        loads[1].wait()
        keys_of(0)
        hop(2)
        keys_of(1)
        hop(3)
        for g in range(2, groups):
            keys_of(g)
        loads[2].wait()
        for g in range(groups):
            cols = slice(g * pair, (g + 1) * pair)
            query[:, cols] = turned(jnp.dot(normed[...], wq[:, cols], preferred_element_type=f32))
        hop(4)
        across, down, inner = {}, {}, {}
        for g in range(groups):
            up[g].wait_recv()
            across[g] = send(slot_of(g, (1 - ahead) // 2 * back), slot_of(g, side_slot), side)
            inner[g] = send(slot_of(g, 3 * core), slot_of(g, back), sib)
        for copy in twin.values():
            copy.wait_recv()
        for g in range(groups):
            across[g].wait_recv()
            down[g] = send(slot_of(g, side_slot), slot_of(g, side_slot), sib)
        for g in range(groups):
            inner[g].wait_recv()
            down[g].wait_recv()
            for n in range(pair // HD):
                cols = slice(g * pair + n * HD, g * pair + (n + 1) * HD)
                k_cols = slice(n * HD, (n + 1) * HD)
                v_cols = slice(pair + n * HD, pair + (n + 1) * HD)
                head = query[:, cols]
                scores = jnp.concatenate(
                    [
                        lax.dot_general(head, cache[0, :, cols], nt, preferred_element_type=f32),
                        lax.dot_general(head, kv[g, :, k_cols], nt, preferred_element_type=f32),
                    ],
                    1,
                )
                scores = scores * scale + bias[...]
                weights = jnp.exp(scores - jnp.max(scores, -1, keepdims=True))
                total = jnp.sum(weights, -1, keepdims=True)
                weights = weights.astype(bf16)
                summed = jnp.dot(weights[:, :cached], cache[1, :, cols], preferred_element_type=f32)
                summed += jnp.dot(weights[:, cached:], kv[g, :, v_cols], preferred_element_type=f32)
                attended[:, cols] = (summed / total).astype(bf16)
        loads[3].wait()
        mine, theirs = core * tall, (1 - core) * tall
        odd = (core + y) % 2
        spot = {
            "ao": mine + q * odd,
            "as": theirs + q * (1 - odd),
            "e1o": mine + 2 * q,
            "e1s": theirs + 2 * q,
            "e2o": mine + 3 * q,
            "e2s": theirs + 3 * q,
            "yo": mine + q * (1 - odd),
            "ys": theirs + q * odd,
        }
        inside = {"ao": q * odd, "e1o": 2 * q, "e2o": 3 * q, "yo": q * (1 - odd)}
        circle, cross, twins = {}, {}, {}

        def put(table, key, hops, name, device):
            start = chip_at(r + hops) * 2 * tall + spot[name]
            view = all_rows.at[pl.ds(pl.multiple_of(start, q), q)]
            table[key] = send(view, view, device)

        mixed = {}
        for n, (away, name) in enumerate((("yo", "ao"), ("e1o", "e1o"), ("e2o", "e2o"), ("ao", "yo"))):
            part_rows = pl.ds(pl.multiple_of(inside[away], q), q)
            product = jnp.dot(attended[part_rows], wo[...], preferred_element_type=f32)
            mix[part_rows] = product.astype(bf16)
            mixed[name] = send(mix.at[part_rows], mix_got.at[part_rows], other)

        def settle(name):
            mixed[name].wait_recv()
            rows = pl.ds(pl.multiple_of(inside[name], q), q)
            total = x[rows].astype(f32) + (mix[rows].astype(f32) + mix_got[rows].astype(f32))
            total = total.astype(bf16)
            resid_ref[rows] = total
            total = total.astype(f32)
            inv = lax.rsqrt(jnp.mean(total * total, -1, keepdims=True) + EPS)
            here = pl.ds(pl.multiple_of(home * 2 * tall + spot[name], q), q)
            all_rows[here] = (total * inv * mg_ref[...].astype(f32)).astype(bf16)
            put(twins, (0, name), 0, name, sib)

        pieces = ("ao", "as", "e1o", "e1s", "e2o", "e2s")
        some = ("ao", "e1o", "e2o")
        order = [(t, p) for t in range(1, HOPS) for p in pieces] + [(HOPS, p) for p in some]

        def onward(t, p):
            if t < HOPS - 1 or (t == HOPS - 1 and p in some):
                put(circle, (t + 1, p), -step * t, p, nxt)

        for name in some:
            settle(name)
            onward(0, name)
            twins[0, name].wait_recv()
            onward(0, name[:-1] + "s")
        settle("yo")

        def experts_of(place):
            rows = pl.ds(pl.multiple_of(place * tall, tall), tall)
            gate = jnp.dot(all_rows[rows], wg[...], preferred_element_type=f32)
            raised = jnp.dot(all_rows[rows], wu[...], preferred_element_type=f32)
            act_ref[rows] = (gate / (1.0 + jnp.exp(-gate)) * raised).astype(bf16)

        def route():
            own = all_rows[pl.ds(pl.multiple_of(s * tall, tall), tall)]
            logits = lax.dot_general(wr_ref[...], own, nt, preferred_element_type=f32)
            odds = jnp.exp(logits - jnp.max(logits, 0, keepdims=True))
            probs = odds / jnp.sum(odds, 0, keepdims=True)
            expert = lax.broadcasted_iota(jnp.int32, (experts, tall), 0)
            named = jnp.zeros((experts, tall), f32)
            for n in range(topk):
                named = jnp.where(routes_ref[n : n + 1] == expert, 1.0, named)
            share = probs * named
            for n in range(experts):
                share_own[n] = share[n : n + 1]
            share_out[s] = share_own[s]
            for d in range(1, blocks):
                dest = (s + d) % blocks
                shares.append(send(share_own.at[dest], share_out.at[s], {"seq": dest}))

        shares = []

        def job(t, along, owner):
            def act():
                if owner == "first":
                    names = pieces if t < HOPS else some
                    if along < 0:
                        for p in names:
                            twins[t, p].wait_recv()
                        for p in ("ao", "as") if t < HOPS else ("ao",):
                            twins[t, "y" + p].wait_recv()
                experts_of(chip_at(r - step * t * along) * 2 + (0 if owner == "first" else 1))
            return act

        def own_job():
            experts_of(s)

        def sibling_job():
            twins[0, "yo"].wait_recv()
            experts_of(s + step)

        jobs = {0: [route], 1: [own_job], 3: [sibling_job]}
        for t in range(1, HOPS):
            at = 6 * t + (1 if t < HOPS - 1 else 0)
            for k, (along, owner) in enumerate(((1, "first"), (1, "second"), (-1, "first"), (-1, "second"))):
                jobs.setdefault(at + k, []).append(job(t, along, owner))
        late = []

        def drain(limit):
            while late and late[0][0] <= limit:
                _, t, p = late.pop(0)
                cross[t, p].wait_recv()
                put(twins, (t, "y" + p), -step * t, "y" + p[1], sib)

        loads[4].wait()
        loads[5].wait()
        for n, (t, p) in enumerate(order):
            circle[t, p].wait_recv()
            onward(t, p)
            if p in ("ao", "as"):
                put(cross, (t, p), -step * t, p, other)
                late.append((n, t, p))
            put(twins, (t, p), -step * t, p, sib)
            drain(n - 4)
            for act in jobs.pop(n, ()):
                act()
        drain(len(order))
        for n in sorted(jobs):
            for act in jobs[n]:
                act()
        for p in some + ("yao",):
            twins[HOPS, p].wait_recv()
        last = chip_at(r + HOPS) * 2
        experts_of(last)
        experts_of(last + 1)
        for copy in shares:
            copy.wait_recv()
        for copy in sent:
            copy.wait_send()

    vmem, smem = pl.BlockSpec(memory_space=VMEM), pl.BlockSpec(memory_space=pltpu.SMEM)
    return pl.pallas_call(
        kernel,
        out_shape=(
            jax.ShapeDtypeStruct((tall, width), bf16),
            jax.ShapeDtypeStruct((blocks * tall, hidden), bf16),
            jax.ShapeDtypeStruct((blocks, 1, tall), f32),
        ),
        in_specs=[smem] * 3 + [vmem] * 9 + [pl.BlockSpec(memory_space=pl.ANY)] * 6,
        out_specs=(vmem, vmem, vmem),
        scratch_shapes=[
            VMEM((width, local), bf16),
            VMEM((width, local), bf16),
            VMEM((width, local), bf16),
            VMEM((local, width), bf16),
            VMEM((width, hidden), bf16),
            VMEM((width, hidden), bf16),
            VMEM((tall, width), bf16),
            VMEM((tall, width), bf16),
            VMEM((2, cached, local), bf16),
            VMEM((groups, near, 2 * pair), bf16),
            VMEM((tall, local), bf16),
            VMEM((tall, local), bf16),
            VMEM((tall, cached + near), f32),
            VMEM((tall, width), bf16),
            VMEM((tall, width), bf16),
            VMEM((blocks * tall, width), bf16),
            VMEM((experts, 1, tall), f32),
            pltpu.SemaphoreType.DMA((6,)),
            pltpu.SemaphoreType.DMA((sems,)),
            pltpu.SemaphoreType.DMA((sems,)),
        ],
        compiler_params=pltpu.CompilerParams(
            collective_id=8, has_side_effects=True, vmem_limit_bytes=60 << 20
        ),
        name="front",
    )(lengths, request_group, shard_group, tokens, gain.reshape(1, width), cosine, sine, prefix_keys,
      prefix_values, moe_gain.reshape(1, width), w_router.T, routes.T, w_query, w_key, w_value, w_out,
      w_gate, w_up)


def attention(query, prefix_keys, prefix_values, suffix, bias):
    tall, wide = query.shape
    heads = wide // HD
    cached = prefix_keys.shape[0]
    keys = bias.shape[1]
    many = len(suffix)
    scale = HD ** (-0.5)

    def kernel(query_ref, cached_k, cached_v, bias_ref, *rest):
        suffix_k, suffix_v, out_ref = rest[:many], rest[many : 2 * many], rest[2 * many]
        head = query_ref[...]
        scores = [
            lax.dot_general(
                head, block[...], (((1,), (1,)), ((), ())), preferred_element_type=jnp.float32
            )
            for block in (cached_k, *suffix_k)
        ]
        scores = jnp.concatenate(scores, 1) * scale + bias_ref[...]
        weights = jnp.exp(scores - jnp.max(scores, -1, keepdims=True))
        total = jnp.sum(weights, -1, keepdims=True)
        weights = weights.astype(jnp.bfloat16)
        summed = jnp.dot(weights[:, :cached], cached_v[...], preferred_element_type=jnp.float32)
        for n, block in enumerate(suffix_v):
            start = cached + n * tall
            summed += jnp.dot(
                weights[:, start : start + tall], block[...], preferred_element_type=jnp.float32
            )
        out_ref[...] = (summed / total).astype(jnp.bfloat16)

    def column(rows, offset):
        return pl.BlockSpec((rows, HD), lambda h: (0, h + offset))

    return pl.pallas_call(
        kernel,
        out_shape=jax.ShapeDtypeStruct((tall, wide), jnp.bfloat16),
        grid=(heads,),
        in_specs=[column(tall, 0), column(cached, 0), column(cached, 0)]
        + [pl.BlockSpec((tall, keys), lambda h: (0, 0))]
        + [column(tall, 0)] * many
        + [column(tall, heads)] * many,
        out_specs=column(tall, 0),
        cost_estimate=pl.CostEstimate(
            flops=4 * tall * keys * wide, bytes_accessed=4 * keys * wide, transcendentals=0
        ),
        name="attention",
    )(query, prefix_keys, prefix_values, bias, *suffix, *suffix)


def on_device(
    tokens,
    attn_gain,
    w_query,
    w_key,
    w_value,
    w_out,
    prefix_keys,
    prefix_values,
    shard_group,
    request_group,
    lengths,
    moe_gain,
    w_router,
    w_gate,
    w_up,
    w_down,
    routes,
    final_gain,
    w_head,
):
    f32 = jnp.float32
    bf16 = jnp.bfloat16
    seq_index = lax.axis_index("seq")
    tp_index = lax.axis_index("tp")
    seq_count = lax.axis_size("seq")
    tp_count = lax.axis_size("tp")
    tok_dev = tokens.shape[0]
    width_part = tokens.shape[1]
    shard_rows = prefix_keys.shape[0]
    prefix_length = shard_rows * seq_count // 2
    ends = prefix_sums(lengths)
    experts = w_router.shape[1]
    topk = routes.shape[1]
    local_index = seq_index * tok_dev + jnp.arange(tok_dev)
    if seq_count == 16 and tp_count == 2 and experts == seq_count:
        begun = jnp.max(jnp.where(local_index[:, None] >= ends[None, :], ends[None, :], 0), 1)
        half = HD // 2
        freq = 10000.0 ** (-jnp.arange(half).astype(f32) / half)
        angle = (prefix_length + local_index - begun).astype(f32)[:, None] * freq[None, :]
        cosine, sine = jnp.cos(angle), jnp.sin(angle)
        resid_full, act, shares = front(
            tokens, attn_gain, w_query, w_key, w_value, w_out, prefix_keys, prefix_values, lengths,
            request_group, shard_group, jnp.concatenate([cosine, cosine], 1),
            jnp.concatenate([-sine, sine], 1), moe_gain, w_router, routes,
            w_gate[0], w_up[0],
        )
        return back(act, shares, w_down[0], resid_full, lengths, final_gain, w_head)
    full_x = gather_columns(tokens)
    width = full_x.shape[1]
    normed = normalize(full_x.astype(f32), attn_gain).astype(bf16)
    heads = w_query.shape[1] // HD
    starts = ends - lengths
    own_request = request_of(local_index, ends)
    own_start = lookup(own_request, starts)
    own_group = lookup(own_request, request_group)
    position = (prefix_length + local_index - own_start).astype(f32)
    query = rotate(
        jnp.dot(normed, w_query, preferred_element_type=f32).reshape(tok_dev, heads, HD), position
    ).astype(bf16)
    key_rows = rotate(
        jnp.dot(normed, w_key, preferred_element_type=f32).reshape(tok_dev, heads, HD), position
    ).astype(bf16)
    key_rows = key_rows.reshape(tok_dev, heads * HD)
    value_rows = jnp.dot(normed, w_value, preferred_element_type=f32).astype(bf16)
    pieces = (
        lax.all_gather(prefix_keys, "seq", axis=0, tiled=True),
        lax.all_gather(prefix_values, "seq", axis=0, tiled=True),
    )
    count = pieces[0].shape[0]
    shard_ids = jnp.arange(count) // shard_rows
    key_group = lookup(shard_ids, shard_group)
    fold_allowed = own_group[:, None] == key_group[None, :]
    own_allowed = (own_request[:, None] == own_request[None, :]) & (
        local_index[None, :] <= local_index[:, None]
    )
    both_rows = jnp.concatenate([key_rows, value_rows], 1)
    suffix = [both_rows] + [from_behind(both_rows, "seq", step) for step in range(1, SPAN + 1)]
    permitted = [fold_allowed, own_allowed]
    for step in range(1, SPAN + 1):
        key_index = (seq_index - step) * tok_dev + jnp.arange(tok_dev)
        key_request = request_of(key_index, ends)
        permitted.append(
            (key_index >= 0)[None, :] & (own_request[:, None] == key_request[None, :])
        )
    bias = jnp.where(jnp.concatenate(permitted, 1), 0.0, NEGATIVE)
    attended = attention(query.reshape(tok_dev, heads * HD), *pieces, suffix, bias)
    mixed = jnp.dot(attended, w_out, preferred_element_type=f32).astype(bf16)
    resid_full = (full_x.astype(f32) + sum_over_tp(mixed)).astype(bf16)
    moe_in = normalize(resid_full.astype(f32), moe_gain).astype(bf16)
    probs = jax.nn.softmax(jnp.dot(moe_in, w_router, preferred_element_type=f32), -1)
    flat = routes.reshape(-1)
    hits = (flat[:, None] == jnp.arange(experts)[None, :]).astype(jnp.int32)
    line = jnp.arange(flat.shape[0])
    before = (line[:, None] > line[None, :]).astype(bf16)
    earlier = jnp.dot(before, hits.astype(bf16), preferred_element_type=f32).astype(jnp.int32)
    rank = jnp.sum(earlier * hits, 1)
    capacity = min(tok_dev, tp_count * max(1, 3 * tok_dev * topk // (2 * experts * tp_count)))
    target = flat * capacity + rank
    route_weight = jnp.sum(hits.reshape(tok_dev, topk, experts).astype(f32) * probs[:, None, :], -1)
    repeated = jnp.repeat(moe_in, topk, axis=0)
    outgoing = (
        jnp.zeros((experts * capacity, width), bf16)
        .at[target]
        .set(repeated)
        .reshape(experts, capacity, width)
    )
    arrived = lax.all_to_all(outgoing, "seq", split_axis=0, concat_axis=0, tiled=True)
    sources = arrived.shape[0]
    count = arrived.shape[1]
    rows = arrived.reshape(sources * count, width)
    gate = jnp.dot(rows, w_gate[0], preferred_element_type=f32)
    up = jnp.dot(rows, w_up[0], preferred_element_type=f32)
    act = (jax.nn.silu(gate) * up).astype(bf16)
    partial_out = jnp.dot(act, w_down[0], preferred_element_type=f32).reshape(sources, count, width)
    summed = lax.psum_scatter(partial_out, "tp", scatter_dimension=2, tiled=True).astype(bf16)
    returned = lax.all_to_all(summed, "seq", split_axis=0, concat_axis=0, tiled=True)
    picked = returned.reshape(experts * capacity, width_part)[target].reshape(
        tok_dev, topk, width_part
    )
    moe_part = jnp.sum(picked.astype(f32) * route_weight[:, :, None], 1)
    resid = lax.dynamic_slice_in_dim(resid_full, tp_index * width_part, width_part, 1)
    hidden = (resid.astype(f32) + moe_part).astype(bf16)
    last_hit = ((ends - 1)[:, None] == local_index[None, :]).astype(bf16)
    chosen = jnp.dot(last_hit, hidden, preferred_element_type=f32)
    final = last_rows(chosen, final_gain, width)
    log_probs = log_softmax(jnp.dot(final, w_head, preferred_element_type=f32))
    return (hidden, log_probs)


def solution(mesh):
    in_specs = (
        P("seq", "tp"),
        P(),
        P(None, "tp"),
        P(None, "tp"),
        P(None, "tp"),
        P("tp", None),
        P("seq", "tp"),
        P("seq", "tp"),
        P(),
        P(),
        P(),
        P(),
        P(),
        P("seq", None, "tp"),
        P("seq", None, "tp"),
        P("seq", "tp", None),
        P("seq", None),
        P("tp"),
        P("tp", "seq"),
    )
    out_specs = (P("seq", "tp"), P(None, "seq"))
    return jax.shard_map(
        on_device, mesh=mesh, in_specs=in_specs, out_specs=out_specs, check_vma=False
    )
```

```python
import jax
import jax.numpy as jnp
import numpy as np
from jax import lax
from jax.experimental import pallas as pl
from jax.experimental.pallas import tpu as pltpu
from jax.sharding import PartitionSpec as P

HD = 128
SPAN = 4
VMEM = pltpu.VMEM


EPS = 1e-05
NEGATIVE = -1e30


def from_behind(value, axis, steps):
    count = lax.axis_size(axis)
    leading, last = (max(0, -steps), min(count, count - steps))
    return lax.ppermute(value, axis, [(source, source + steps) for source in range(leading, last)])


def normalize(rows, gain):
    inv = lax.rsqrt(jnp.mean(rows * rows, -1, keepdims=True) + EPS)
    return rows * inv * gain.astype(jnp.float32)


def rotate(vectors, position):
    half = vectors.shape[-1] // 2
    freq = 10000.0 ** (-jnp.arange(half).astype(jnp.float32) / half)
    angle = position[:, None] * freq[None, :]
    cosine = jnp.cos(angle)[:, None, :]
    sine = jnp.sin(angle)[:, None, :]
    first = vectors[..., :half]
    second = vectors[..., half:]
    return jnp.concatenate([first * cosine - second * sine, second * cosine + first * sine], -1)


def request_of(index, ends):
    return jnp.sum((index[:, None] >= ends[None, :]).astype(jnp.int32), 1)


def lookup(selector, table):
    hit = selector[:, None] == jnp.arange(table.shape[0])[None, :]
    return jnp.sum(jnp.where(hit, table[None, :], 0), 1)


def prefix_sums(values):
    order = jnp.arange(values.shape[0])
    return jnp.sum(jnp.where(order[:, None] >= order[None, :], values[None, :], 0), 1)


def partner(axis, bit):
    index = lax.axis_index(axis)
    span = 1 << bit
    other = index + span - 2 * span * ((index // span) % 2)
    return {axis: other}


def greet(stages):
    barrier = pltpu.get_barrier_semaphore()
    for axis, bit in stages:
        pl.semaphore_signal(barrier, inc=1, device_id=partner(axis, bit))
    pl.semaphore_wait(barrier, len(stages))


def swap(source, target, send_sem, recv_sem, stage):
    copy = pltpu.make_async_remote_copy(
        src_ref=source, dst_ref=target, send_sem=send_sem, recv_sem=recv_sem,
        device_id=partner(*stage),
    )
    copy.start()
    return copy


def bits_of(axis):
    return [(axis, bit) for bit in range(lax.axis_size(axis).bit_length() - 1)]


def last_rows(chosen, gain, width):
    seq_stages, tp_stages = bits_of("seq"), bits_of("tp")
    stages = seq_stages + tp_stages
    rows, part = chosen.shape

    def kernel(chosen_ref, gain_ref, out_ref, held, got, sq_held, sq_got, send_sem, recv_sem):
        greet(stages)
        held[0] = chosen_ref[...]
        count = len(seq_stages)
        for k, stage in enumerate(seq_stages):
            swap(held.at[k], got.at[k], send_sem.at[k], recv_sem.at[k], stage).wait()
            held[k + 1] = held[k] + got[k]
        total = held[count]
        sq_held[0] = jnp.broadcast_to(jnp.sum(total * total, -1, keepdims=True), (rows, 128))
        for k, stage in enumerate(tp_stages):
            n = count + k
            swap(sq_held.at[k], sq_got.at[k], send_sem.at[n], recv_sem.at[n], stage).wait()
            sq_held[k + 1] = sq_held[k] + sq_got[k]
        square = sq_held[len(tp_stages)][:, :1]
        scaled = total * lax.rsqrt(square / width + EPS) * gain_ref[...].astype(jnp.float32)
        out_ref[...] = scaled.astype(jnp.bfloat16)

    ns, nt = len(seq_stages), len(tp_stages)
    return pl.pallas_call(
        kernel,
        out_shape=jax.ShapeDtypeStruct((rows, part), jnp.bfloat16),
        in_specs=[pl.BlockSpec(memory_space=VMEM)] * 2,
        out_specs=pl.BlockSpec(memory_space=VMEM),
        scratch_shapes=[
            VMEM((ns + 1, rows, part), jnp.float32),
            VMEM((ns, rows, part), jnp.float32),
            VMEM((nt + 1, rows, 128), jnp.float32),
            VMEM((nt, rows, 128), jnp.float32),
            pltpu.SemaphoreType.DMA((ns + nt,)),
            pltpu.SemaphoreType.DMA((ns + nt,)),
        ],
        compiler_params=pltpu.CompilerParams(collective_id=1, has_side_effects=True),
        name="last_rows",
    )(chosen, gain.reshape(1, part))


def log_softmax(logits):
    seq_stages, tp_stages = bits_of("seq"), bits_of("tp")
    stages = tp_stages + seq_stages
    rows, part = logits.shape

    def kernel(logits_ref, out_ref, held, got, st_held, st_got, send_sem, recv_sem):
        greet(stages)
        held[0] = logits_ref[...]
        count = len(tp_stages)
        for k, stage in enumerate(tp_stages):
            swap(held.at[k], got.at[k], send_sem.at[k], recv_sem.at[k], stage).wait()
            held[k + 1] = held[k] + got[k]
        total = held[count]
        peak = jnp.max(total, -1, keepdims=True)
        mass = jnp.sum(jnp.exp(total - peak), -1, keepdims=True)
        st_held[0, :, :128] = jnp.broadcast_to(peak, (rows, 128))
        st_held[0, :, 128:] = jnp.broadcast_to(mass, (rows, 128))
        for k, stage in enumerate(seq_stages):
            n = count + k
            swap(st_held.at[k], st_got.at[k], send_sem.at[n], recv_sem.at[n], stage).wait()
            mine, theirs = st_held[k, :, :128], st_got[k, :, :128]
            top = jnp.maximum(mine, theirs)
            st_held[k + 1, :, :128] = top
            st_held[k + 1, :, 128:] = st_held[k, :, 128:] * jnp.exp(mine - top) + st_got[
                k, :, 128:
            ] * jnp.exp(theirs - top)
        last = len(seq_stages)
        out_ref[...] = total - st_held[last, :, :1] - jnp.log(st_held[last, :, 128:129])

    ns, nt = len(seq_stages), len(tp_stages)
    return pl.pallas_call(
        kernel,
        out_shape=jax.ShapeDtypeStruct((rows, part), jnp.float32),
        in_specs=[pl.BlockSpec(memory_space=VMEM)],
        out_specs=pl.BlockSpec(memory_space=VMEM),
        scratch_shapes=[
            VMEM((nt + 1, rows, part), jnp.float32),
            VMEM((nt, rows, part), jnp.float32),
            VMEM((ns + 1, rows, 256), jnp.float32),
            VMEM((ns, rows, 256), jnp.float32),
            pltpu.SemaphoreType.DMA((ns + nt,)),
            pltpu.SemaphoreType.DMA((ns + nt,)),
        ],
        compiler_params=pltpu.CompilerParams(collective_id=2, has_side_effects=True),
        name="log_softmax",
    )(logits)


def gather_columns(block):
    stages = bits_of("tp")
    rows, part = block.shape
    count = lax.axis_size("tp")

    def kernel(block_ref, out_ref, send_sem, recv_sem):
        greet(stages)
        me = lax.axis_index("tp")
        out_ref[:, pl.ds(pl.multiple_of(me * part, part), part)] = block_ref[...]
        for k, stage in enumerate(stages):
            wide = part << k
            start = pl.multiple_of((me // (1 << k)) * wide, wide)
            piece = out_ref.at[:, pl.ds(start, wide)]
            swap(piece, piece, send_sem.at[k], recv_sem.at[k], stage).wait()

    return pl.pallas_call(
        kernel,
        out_shape=jax.ShapeDtypeStruct((rows, part * count), block.dtype),
        in_specs=[pl.BlockSpec(memory_space=VMEM)],
        out_specs=pl.BlockSpec(memory_space=VMEM),
        scratch_shapes=[pltpu.SemaphoreType.DMA((len(stages),))] * 2,
        compiler_params=pltpu.CompilerParams(collective_id=3, has_side_effects=True),
        name="gather_columns",
    )(block)


def sum_over_tp(block):
    stages = bits_of("tp")
    rows, part = block.shape

    def kernel(block_ref, out_ref, held, got, send_sem, recv_sem):
        greet(stages)
        for k, stage in enumerate(stages):
            source = block_ref if k == 0 else held.at[k]
            swap(source, got.at[k], send_sem.at[k], recv_sem.at[k], stage).wait()
            total = source[...].astype(jnp.float32) + got[k].astype(jnp.float32)
            if k + 1 < len(stages):
                held[k + 1] = total.astype(jnp.bfloat16)
            else:
                out_ref[...] = total

    count = len(stages)
    return pl.pallas_call(
        kernel,
        out_shape=jax.ShapeDtypeStruct((rows, part), jnp.float32),
        in_specs=[pl.BlockSpec(memory_space=VMEM)],
        out_specs=pl.BlockSpec(memory_space=VMEM),
        scratch_shapes=[
            VMEM((count, rows, part), jnp.bfloat16),
            VMEM((count, rows, part), jnp.bfloat16),
            pltpu.SemaphoreType.DMA((count,)),
            pltpu.SemaphoreType.DMA((count,)),
        ],
        compiler_params=pltpu.CompilerParams(collective_id=4, has_side_effects=True),
        name="sum_over_tp",
    )(block)


HOPS = 4


def ring_place():
    s = lax.axis_index("seq")
    core = s % 2
    x = (s // 2) % 2
    z = s // 4
    return s, core, z + x * (7 - 2 * z)


def chip_at(place):
    q = (place + 16) % 8
    x = q // 4
    z = q + x * (7 - 2 * q)
    return z * 2 + x


def greet_all(blocks):
    s = lax.axis_index("seq")
    barrier = pltpu.get_barrier_semaphore()
    for d in range(1, blocks):
        pl.semaphore_signal(barrier, inc=1, device_id={"seq": (s + d) % blocks})
    pl.semaphore_signal(barrier, inc=1, device_id={"tp": 1 - lax.axis_index("tp")})
    pl.semaphore_wait(barrier, blocks)


def back(act, shares, w_down, resid, lengths, gain, w_head):
    tall, wide = resid.shape
    half = wide // 2
    hidden = act.shape[1]
    count = shares.shape[0]
    reqs = lengths.shape[0]
    cols = w_head.shape[1]
    padded = -(-cols // 128) * 128
    high = -(-reqs // 16) * 16
    cuts = 4
    per = -(-cols // (128 * cuts)) * 128
    spans = [(k * per, min(per, cols - k * per)) for k in range(cuts)]
    f32 = jnp.float32
    ty = tall // 2
    ts = tall - ty
    sems = 80
    bf16 = jnp.bfloat16
    G = 16
    units = [(HOPS, "o")] + [(t, b) for t in range(HOPS - 1, 0, -1) for b in ("s", "o")] + [(0, "o")]
    nu = len(units)

    def kernel(len_ref, share_ref, gain_ref, act_hbm, resid_hbm, wd_hbm, wh_hbm, out_ref, logs_ref,
               act_ref, resid_ref, wd, wh, part_ref, sib_buf, acc_y, acc_s, y_send, y_recv, ring_y, ring_s, far_y, far_s, last_recv,
               near, far, logit, got, stats, w_sem, send_sem, recv_sem):
        loads = []
        stores = ((wd_hbm, wd), (act_hbm, act_ref), (resid_hbm, resid_ref), (wh_hbm, wh))
        for n, (source, target) in enumerate(stores):
            loads.append(pltpu.make_async_copy(source, target, w_sem.at[n]))
            loads[n].start()
        s, core, r = ring_place()
        y = lax.axis_index("tp")
        step = 1 - 2 * core
        nxt = {"seq": chip_at(r + step) * 2 + core}
        sib = {"seq": s + step}
        other = {"tp": 1 - y}
        eye = lax.broadcasted_iota(jnp.int32, (tall, tall), 0) == lax.broadcasted_iota(
            jnp.int32, (tall, tall), 1
        )

        def project(place):
            rows = pl.ds(pl.multiple_of(place * tall, tall), tall)
            weight = jnp.sum(jnp.where(eye, share_ref[place], 0.0), -1, keepdims=True)
            product = jnp.dot(act_ref[rows], wd[...], preferred_element_type=f32)
            part_ref[rows] = (product * weight).astype(bf16)

        greet_all(count)
        loads[0].wait()
        loads[1].wait()
        used = iter(range(sems))
        own_cols = pl.ds(pl.multiple_of(y * half, half), half)
        far_cols = pl.ds(pl.multiple_of((1 - y) * half, half), half)

        def send(source, target, device):
            n = next(used)
            copy = pltpu.make_async_remote_copy(
                src_ref=source, dst_ref=target, send_sem=send_sem.at[n], recv_sem=recv_sem.at[n],
                device_id=device,
            )
            copy.start()
            return copy

        def rows_of(t, b, direction, c):
            return chip_at(r + direction * t) * 2 + (c if b == "o" else 1 - c)

        pair, cross, ring, sent = {}, {}, {}, []

        def lend(i):
            if i < nu:
                place = rows_of(*units[i], -step, 1 - core)
                project(place)
                start = pl.multiple_of(place * tall, tall)
                pair[i] = send(part_ref.at[pl.ds(start, tall)], sib_buf.at[i], sib)
                sent.append(pair[i])

        lend(0)
        lend(1)

        def summed(i):
            t, b = units[i]
            place = rows_of(t, b, step, core)
            project(place)
            start = place * tall
            pair[i].wait_recv()

            def body_y(g, _):
                rows = pl.ds(pl.multiple_of(g * G, G), G)
                here = pl.ds(pl.multiple_of(start + g * G, G), G)
                y_send[i, rows] = part_ref[here, far_cols] + sib_buf[i, rows, far_cols]
                acc_y[i, rows] = part_ref[here, own_cols] + sib_buf[i, rows, own_cols]
                return 0

            lax.fori_loop(0, ty // G, body_y, 0)
            cross[i] = send(y_send.at[i], y_recv.at[i], other)
            sent.append(cross[i])

            def body_s(g, _):
                rows = pl.ds(pl.multiple_of(g * G, G), G)
                below = pl.ds(pl.multiple_of(ty + g * G, G), G)
                here = pl.ds(pl.multiple_of(start + ty + g * G, G), G)
                acc_s[i, rows] = part_ref[here] + sib_buf[i, below]
                return 0

            lax.fori_loop(0, ts // G, body_s, 0)
            if not arriving(t, b) and t > 0:
                pass_s(i)
            lend(i + 2)

        def slot(t, b):
            return 2 * t + (0 if b == "o" else 1)

        def arriving(t, b):
            return (t + 1, b) in units and t > 0

        def pass_s(i):
            t, b = units[i]
            m = slot(t - 1, b)
            ring[t - 1, b, "s"] = send(acc_s.at[i], ring_s.at[m], nxt)
            sent.append(ring[t - 1, b, "s"])

        def passed(i):
            t, b = units[i]
            arrived = arriving(t, b)
            n = slot(t, b)
            if arrived:
                ring[t, b, "s"].wait_recv()

                def body_s(g, _):
                    rows = pl.ds(pl.multiple_of(g * G, G), G)
                    acc_s[i, rows] = acc_s[i, rows] + ring_s[n, rows]
                    return 0

                lax.fori_loop(0, ts // G, body_s, 0)
                pass_s(i)
                ring[t, b, "y"].wait_recv()
            cross[i].wait_recv()

            def body_y(g, _):
                rows = pl.ds(pl.multiple_of(g * G, G), G)
                total = acc_y[i, rows] + y_recv[i, rows]
                if arrived:
                    total = total + ring_y[n, rows]
                acc_y[i, rows] = total
                return 0

            lax.fori_loop(0, ty // G, body_y, 0)
            if t > 0:
                m = slot(t - 1, b)
                ring[t - 1, b, "y"] = send(acc_y.at[i], ring_y.at[m], nxt)
                sent.append(ring[t - 1, b, "y"])

        summed(0)
        summed(1)
        for i in range(nu):
            if i + 2 < nu:
                summed(i + 2)
            passed(i)
        m, n, i = slot(0, "s"), slot(0, "o"), nu - 1
        ring[0, "s", "s"].wait_recv()
        far_copy_s = send(ring_s.at[m], far_s, sib)
        ring[0, "s", "y"].wait_recv()
        far_copy_y = send(ring_y.at[m], far_y, sib)
        sent.extend((far_copy_s, far_copy_y))
        ring[0, "o", "s"].wait_recv()
        far_copy_s.wait_recv()

        def body_s(g, _):
            rows = pl.ds(pl.multiple_of(g * G, G), G)
            acc_s[i, rows] = acc_s[i, rows] + ring_s[n, rows] + far_s[rows]
            return 0

        lax.fori_loop(0, ts // G, body_s, 0)
        last = send(acc_s.at[i, :, far_cols], last_recv, other)
        sent.append(last)
        loads[2].wait()
        ring[0, "o", "y"].wait_recv()
        far_copy_y.wait_recv()

        def body_y(g, _):
            rows = pl.ds(pl.multiple_of(g * G, G), G)
            total = acc_y[i, rows].astype(f32) + ring_y[n, rows].astype(f32) + far_y[rows].astype(f32)
            out_ref[rows] = (total + resid_ref[rows, own_cols].astype(f32)).astype(bf16)
            return 0

        lax.fori_loop(0, ty // G, body_y, 0)
        last.wait_recv()

        def body_l(g, _):
            rows = pl.ds(pl.multiple_of(g * G, G), G)
            here = pl.ds(pl.multiple_of(ty + g * G, G), G)
            total = acc_s[i, rows, own_cols].astype(f32) + last_recv[rows].astype(f32)
            out_ref[here] = (total + resid_ref[here, own_cols].astype(f32)).astype(bf16)
            return 0

        lax.fori_loop(0, ts // G, body_l, 0)
        row = lax.broadcasted_iota(jnp.int32, (high, tall), 0)
        place = lax.broadcasted_iota(jnp.int32, (high, tall), 1) + s * tall
        last = jnp.full((high, tall), -1, jnp.int32)
        end = 0
        for j in range(reqs):
            end = end + len_ref[j]
            last = jnp.where(row == j, end - 1, last)
        hit = (last == place).astype(f32).astype(bf16)
        near[0] = jnp.dot(hit, out_ref[...], preferred_element_type=f32).astype(bf16)

        def note(source, target, device):
            sent.append(send(source, target, device))
            return sent[-1]

        first = [
            note(near.at[0], near.at[d], {"seq": (s // 4) * 4 + (s + d) % 4}) for d in range(1, 4)
        ]
        for copy in first:
            copy.wait_recv()
        far[0] = (near[0] + near[1]) + (near[2] + near[3])
        second = [note(far.at[0], far.at[d], {"seq": (s + 4 * d) % count}) for d in range(1, 4)]
        for copy in second:
            copy.wait_recv()
        total = ((far[0] + far[1]) + (far[2] + far[3])).astype(f32)
        square = jnp.sum(total * total, -1, keepdims=True)
        scaled = (total * gain_ref[...].astype(f32)[None, :]).astype(bf16)
        logit[:, padded:] = jnp.broadcast_to(square[:reqs], (reqs, 128))
        loads[3].wait()
        swapped = [note(logit.at[:, padded:], got.at[:, padded:], other)]
        for k, (start, size) in enumerate(spans):
            product = lax.dot_general(
                scaled, wh[start : start + size], (((1,), (1,)), ((), ())), preferred_element_type=f32
            )
            logit[:, start : start + size] = product[:reqs]
            full = per if k < cuts - 1 else padded - start
            swapped.append(note(logit.at[:, start : start + full], got.at[:, start : start + full], other))
        for copy in swapped:
            copy.wait_recv()
        square = logit[:, padded : padded + 1] + got[:, padded : padded + 1]
        inv = lax.rsqrt(square / wide + EPS)
        both = (logit[:, :cols] + got[:, :cols]) * inv
        peak = jnp.max(both, -1, keepdims=True)
        mass = jnp.sum(jnp.exp(both - peak), -1, keepdims=True)
        lane = lax.broadcasted_iota(jnp.int32, (reqs, 128), 1)
        stats[0] = jnp.where(lane < 64, peak, mass)
        third = [note(stats.at[0], stats.at[d], {"seq": (s + d) % count}) for d in range(1, count)]
        for copy in third:
            copy.wait_recv()
        everyone = stats[...]
        peaks, masses = everyone[:, :, :1], everyone[:, :, 64:65]
        top = jnp.max(peaks, 0)
        whole = jnp.sum(masses * jnp.exp(peaks - top[None]), 0)
        logs_ref[...] = both - top - jnp.log(whole)
        for copy in sent:
            copy.wait_send()

    vmem, hbm = pl.BlockSpec(memory_space=VMEM), pl.BlockSpec(memory_space=pl.ANY)
    return pl.pallas_call(
        kernel,
        out_shape=(
            jax.ShapeDtypeStruct((tall, half), bf16),
            jax.ShapeDtypeStruct((reqs, cols), f32),
        ),
        in_specs=[pl.BlockSpec(memory_space=pltpu.SMEM)] + [vmem] * 2 + [hbm] * 4,
        out_specs=(vmem, vmem),
        scratch_shapes=[
            VMEM((count * tall, hidden), bf16),
            VMEM((tall, wide), bf16),
            VMEM((hidden, wide), bf16),
            VMEM((cols, half), bf16),
            VMEM((count * tall, wide), bf16),
            VMEM((nu, tall, wide), bf16),
            VMEM((nu, ty, half), bf16), VMEM((nu, ts, wide), bf16),
            VMEM((nu, ty, half), bf16), VMEM((nu, ty, half), bf16),
            VMEM((2 * HOPS, ty, half), bf16), VMEM((2 * HOPS, ts, wide), bf16),
            VMEM((ty, half), bf16), VMEM((ts, wide), bf16), VMEM((ts, half), bf16),
            VMEM((4, high, half), bf16), VMEM((4, high, half), bf16),
            VMEM((reqs, padded + 128), f32), VMEM((reqs, padded + 128), f32),
            VMEM((count, reqs, 128), f32),
            pltpu.SemaphoreType.DMA((4,)),
            pltpu.SemaphoreType.DMA((sems,)),
            pltpu.SemaphoreType.DMA((sems,)),
        ],
        compiler_params=pltpu.CompilerParams(
            collective_id=6, has_side_effects=True, vmem_limit_bytes=60 << 20
        ),
        name="back",
    )(lengths, shares, gain, act, resid, w_down, w_head.T)


def front(tokens, gain, w_query, w_key, w_value, w_out, prefix_keys, prefix_values, lengths,
          request_group, shard_group, moe_gain, w_router, routes, w_gate, w_up):
    tall, part = tokens.shape
    width = 2 * part
    local = w_query.shape[1]
    shard = prefix_keys.shape[0]
    shards = shard_group.shape[0]
    reqs = lengths.shape[0]
    cached = shard * shards
    experts = w_router.shape[1]
    topk = routes.shape[1]
    bf16, f32 = jnp.bfloat16, jnp.float32
    pair = 2 * HD
    groups = local // pair
    slots = SPAN + 1
    near = slots * tall
    hidden = w_gate.shape[1]
    blocks = 16
    q = tall // 4
    sems = 136
    turn = HD // 2
    freq = np.power(10000.0, -np.arange(turn) / turn)
    freq = np.stack([np.tile(freq, 2), np.repeat([-1.0, 1.0], turn)])
    freq = jnp.asarray(np.tile(freq, (4, 1)), jnp.float32)
    scale = HD ** (-0.5)
    nt = (((1,), (1,)), ((), ()))

    def kernel(len_ref, rg_ref, sg_ref, tok_ref, gain_ref, freq_ref, pk_ref, pv_ref, mg_ref,
               wr_ref, routes_ref, wq_ref, wk_ref, wv_ref, wo_ref, wg_ref, wu_ref, resid_ref, act_ref,
               share_out, wq, wk, wv, wo, wg, wu, x, normed, cache, kv, query, attended, bias, mix, mix_got,
               all_rows, share_own, w_sem, send_sem, recv_sem):
        loads = {}
        for n, (source, target) in enumerate((
            (wk_ref, wk), (wv_ref, wv), (wq_ref, wq), (wo_ref, wo), (wg_ref, wg), (wu_ref, wu)
        )):
            loads[n] = pltpu.make_async_copy(source, target, w_sem.at[n])
            loads[n].start()
        s, core, r = ring_place()
        y = lax.axis_index("tp")
        count = 16
        step = 1 - 2 * core
        ahead = 1 - 2 * ((s // 2) % 2)
        nxt = {"seq": chip_at(r + step) * 2 + core}
        sib = {"seq": s + step}
        side = {"seq": s + 2 * ahead}
        above = {"seq": (s + 4) % count}
        other = {"tp": 1 - y}
        own_cols = pl.ds(pl.multiple_of(y * part, part), part)
        x[:, own_cols] = tok_ref[...]
        own_rows = pl.ds(pl.multiple_of(s * shard, shard), shard)
        cache[0, own_rows] = pk_ref[...]
        cache[1, own_rows] = pv_ref[...]
        greet_all(count)
        used = iter(range(sems))
        sent = []

        def send(source, target, device):
            n = next(used)
            copy = pltpu.make_async_remote_copy(
                src_ref=source, dst_ref=target, send_sem=send_sem.at[n], recv_sem=recv_sem.at[n],
                device_id=device,
            )
            copy.start()
            sent.append(copy)
            return copy

        def move(chip, name, device):
            which, owner = name
            shift = core if owner == "o" else 1 - core
            rows = pl.ds(pl.multiple_of((chip * 2 + shift) * shard, shard), shard)
            view = cache.at[which, rows]
            return send(view, view, device)

        home = chip_at(r)
        swapped = [move(home, (which, "o"), sib) for which in range(2)]
        ring, twin = {}, {}
        for which in range(2):
            ring[1, (which, "o")] = move(home, (which, "o"), nxt)
        crossing = send(tok_ref, x.at[:, own_cols], other)
        for which in range(2):
            swapped[which].wait_recv()
            ring[1, (which, "s")] = move(home, (which, "s"), nxt)

        def hop(t):
            chip = chip_at(r - step * t)
            owners = ("o", "s") if t < HOPS else ("o",)
            for owner in owners:
                for which in range(2):
                    name = (which, owner)
                    ring[t, name].wait_recv()
                    if t < HOPS - 1 or (t == HOPS - 1 and owner == "o"):
                        ring[t + 1, name] = move(chip, name, nxt)
                    twin[t, name] = move(chip, name, sib)

        lane = lax.broadcasted_iota(jnp.int32, (tall, 128), 0) + s * tall
        mine = jnp.zeros((tall, 128), jnp.int32)
        ends, end = [], 0
        for j in range(reqs):
            end = end + len_ref[j]
            ends.append(end)
        for j in range(reqs):
            mine = mine + (lane >= ends[j]).astype(jnp.int32)
        group = jnp.zeros((tall, 128), jnp.int32)
        for j in range(reqs):
            group = jnp.where(mine == j, rg_ref[j], group)
        begun = jnp.zeros((tall, 128), jnp.int32)
        for j in range(reqs):
            begun = jnp.where(lane >= ends[j], ends[j], begun)
        position = (cached // 2 + lane - begun).astype(f32)
        angle = position * freq_ref[:1]
        cosine, sine = jnp.cos(angle), jnp.sin(angle) * freq_ref[1:2]
        own_index, own_request, own_group = lane[:, :1], mine[:, :1], group[:, :1]
        column = lax.broadcasted_iota(jnp.int32, (8, cached), 1)
        key_group = jnp.zeros((8, cached), jnp.int32)
        for j in range(shards):
            inside = (column >= j * shard) & (column < (j + 1) * shard)
            key_group = jnp.where(inside, sg_ref[j], key_group)
        bias[:, :cached] = jnp.where(own_group == key_group[:1], 0.0, NEGATIVE)
        chip = s // 2
        bases = (
            s * tall, (chip - 1) * 2 * tall, (chip - 1) * 2 * tall + tall, (chip - 2) * 2 * tall + tall,
            (chip - 2 + 2 * core) * 2 * tall,
        )
        for n in range(slots):
            place = lax.broadcasted_iota(jnp.int32, (8, tall), 1) + bases[n]
            theirs = jnp.zeros((8, tall), jnp.int32)
            for j in range(reqs):
                theirs = theirs + (place >= ends[j]).astype(jnp.int32)
            seen = (own_request == theirs[:1]) & (place[:1] <= own_index) & (place[:1] >= 0)
            start = cached + n * tall
            bias[:, start : start + tall] = jnp.where(seen, 0.0, NEGATIVE)
        hop(1)
        hop(2)
        crossing.wait_recv()
        rows = x[...].astype(f32)
        inv = lax.rsqrt(jnp.mean(rows * rows, -1, keepdims=True) + EPS)
        normed[...] = (rows * inv * gain_ref[...].astype(f32)[None, :]).astype(bf16)

        def turned(value):
            heads = []
            for n in range(pair // HD):
                head = value[:, n * HD : (n + 1) * HD]
                heads.append(head * cosine + pltpu.roll(head, HD // 2, 1) * sine)
            return jnp.concatenate(heads, 1).astype(bf16)

        back = 4 - core
        side_slot = 1 + core

        def slot_of(g, n):
            return kv.at[g, pl.ds(pl.multiple_of(n * tall, tall), tall)]

        up = {}

        def keys_of(g):
            cols = slice(g * pair, (g + 1) * pair)
            key = jnp.dot(normed[...], wk[:, cols], preferred_element_type=f32)
            kv[g, :tall, :pair] = turned(key)
            value = jnp.dot(normed[...], wv[:, cols], preferred_element_type=f32)
            kv[g, :tall, pair:] = value.astype(bf16)
            up[g] = send(slot_of(g, 0), slot_of(g, back), above)

        loads[0].wait()
        loads[1].wait()
        keys_of(0)
        hop(3)
        keys_of(1)
        hop(4)
        for g in range(2, groups):
            keys_of(g)
        loads[2].wait()
        for g in range(groups):
            cols = slice(g * pair, (g + 1) * pair)
            query[:, cols] = turned(jnp.dot(normed[...], wq[:, cols], preferred_element_type=f32))
        across, down, inner = {}, {}, {}
        for g in range(groups):
            up[g].wait_recv()
            across[g] = send(slot_of(g, (1 - ahead) // 2 * back), slot_of(g, side_slot), side)
            inner[g] = send(slot_of(g, 3 * core), slot_of(g, back), sib)
        for copy in twin.values():
            copy.wait_recv()
        for g in range(groups):
            across[g].wait_recv()
            down[g] = send(slot_of(g, side_slot), slot_of(g, side_slot), sib)
        for g in range(groups):
            inner[g].wait_recv()
            down[g].wait_recv()
            for n in range(pair // HD):
                cols = slice(g * pair + n * HD, g * pair + (n + 1) * HD)
                k_cols = slice(n * HD, (n + 1) * HD)
                v_cols = slice(pair + n * HD, pair + (n + 1) * HD)
                head = query[:, cols]
                scores = jnp.concatenate(
                    [
                        lax.dot_general(head, cache[0, :, cols], nt, preferred_element_type=f32),
                        lax.dot_general(head, kv[g, :, k_cols], nt, preferred_element_type=f32),
                    ],
                    1,
                )
                scores = scores * scale + bias[...]
                weights = jnp.exp(scores - jnp.max(scores, -1, keepdims=True))
                total = jnp.sum(weights, -1, keepdims=True)
                weights = weights.astype(bf16)
                summed = jnp.dot(weights[:, :cached], cache[1, :, cols], preferred_element_type=f32)
                summed += jnp.dot(weights[:, cached:], kv[g, :, v_cols], preferred_element_type=f32)
                attended[:, cols] = (summed / total).astype(bf16)
        loads[3].wait()
        mine, theirs = core * tall, (1 - core) * tall
        odd = (core + y) % 2
        spot = {
            "ao": mine + q * odd,
            "as": theirs + q * (1 - odd),
            "e1o": mine + 2 * q,
            "e1s": theirs + 2 * q,
            "e2o": mine + 3 * q,
            "e2s": theirs + 3 * q,
            "yo": mine + q * (1 - odd),
            "ys": theirs + q * odd,
        }
        inside = {"ao": q * odd, "e1o": 2 * q, "e2o": 3 * q, "yo": q * (1 - odd)}
        circle, cross, twins = {}, {}, {}

        def put(table, key, hops, name, device):
            start = chip_at(r + hops) * 2 * tall + spot[name]
            view = all_rows.at[pl.ds(pl.multiple_of(start, q), q)]
            table[key] = send(view, view, device)

        mixed = {}
        for n, (away, name) in enumerate((("yo", "ao"), ("e1o", "e1o"), ("e2o", "e2o"), ("ao", "yo"))):
            part_rows = pl.ds(pl.multiple_of(inside[away], q), q)
            product = jnp.dot(attended[part_rows], wo[...], preferred_element_type=f32)
            mix[part_rows] = product.astype(bf16)
            mixed[name] = send(mix.at[part_rows], mix_got.at[part_rows], other)

        def settle(name):
            mixed[name].wait_recv()
            rows = pl.ds(pl.multiple_of(inside[name], q), q)
            total = x[rows].astype(f32) + (mix[rows].astype(f32) + mix_got[rows].astype(f32))
            total = total.astype(bf16)
            resid_ref[rows] = total
            total = total.astype(f32)
            inv = lax.rsqrt(jnp.mean(total * total, -1, keepdims=True) + EPS)
            here = pl.ds(pl.multiple_of(home * 2 * tall + spot[name], q), q)
            all_rows[here] = (total * inv * mg_ref[...].astype(f32)[None, :]).astype(bf16)
            put(twins, (0, name), 0, name, sib)

        pieces = ("ao", "as", "e1o", "e1s", "e2o", "e2s")
        some = ("ao", "e1o", "e2o")
        order = [(t, p) for t in range(1, HOPS) for p in pieces] + [(HOPS, p) for p in some]

        def onward(t, p):
            if t < HOPS - 1 or (t == HOPS - 1 and p in some):
                put(circle, (t + 1, p), -step * t, p, nxt)

        for name in some:
            settle(name)
            onward(0, name)
            twins[0, name].wait_recv()
            onward(0, name[:-1] + "s")
        settle("yo")

        def experts_of(place):
            rows = pl.ds(pl.multiple_of(place * tall, tall), tall)
            gate = jnp.dot(all_rows[rows], wg[...], preferred_element_type=f32)
            raised = jnp.dot(all_rows[rows], wu[...], preferred_element_type=f32)
            act_ref[rows] = (gate / (1.0 + jnp.exp(-gate)) * raised).astype(bf16)

        def route():
            own = all_rows[pl.ds(pl.multiple_of(s * tall, tall), tall)]
            logits = lax.dot_general(wr_ref[...], own, nt, preferred_element_type=f32)
            odds = jnp.exp(logits - jnp.max(logits, 0, keepdims=True))
            probs = odds / jnp.sum(odds, 0, keepdims=True)
            expert = lax.broadcasted_iota(jnp.int32, (experts, tall), 0)
            named = jnp.zeros((experts, tall), f32)
            for n in range(topk):
                named = jnp.where(routes_ref[n : n + 1] == expert, 1.0, named)
            share = probs * named
            for n in range(experts):
                share_own[n] = share[n : n + 1]
            share_out[s] = share_own[s]
            for d in range(1, blocks):
                dest = (s + d) % blocks
                shares.append(send(share_own.at[dest], share_out.at[s], {"seq": dest}))

        shares = []

        def job(t, along, owner):
            def act():
                if owner == "first":
                    names = pieces if t < HOPS else some
                    if along < 0:
                        for p in names:
                            twins[t, p].wait_recv()
                        for p in ("ao", "as") if t < HOPS else ("ao",):
                            twins[t, "y" + p].wait_recv()
                experts_of(chip_at(r - step * t * along) * 2 + (0 if owner == "first" else 1))
            return act

        def own_job():
            experts_of(s)

        def sibling_job():
            twins[0, "yo"].wait_recv()
            experts_of(s + step)

        jobs = {0: [route], 1: [own_job], 3: [sibling_job]}
        for t in range(1, HOPS):
            at = 6 * t + (1 if t < HOPS - 1 else 0)
            for k, (along, owner) in enumerate(((1, "first"), (1, "second"), (-1, "first"), (-1, "second"))):
                jobs.setdefault(at + k, []).append(job(t, along, owner))
        late = []

        def drain(limit):
            while late and late[0][0] <= limit:
                _, t, p = late.pop(0)
                cross[t, p].wait_recv()
                put(twins, (t, "y" + p), -step * t, "y" + p[1], sib)

        loads[4].wait()
        loads[5].wait()
        for n, (t, p) in enumerate(order):
            circle[t, p].wait_recv()
            onward(t, p)
            if p in ("ao", "as"):
                put(cross, (t, p), -step * t, p, other)
                late.append((n, t, p))
            put(twins, (t, p), -step * t, p, sib)
            drain(n - 4)
            for act in jobs.pop(n, ()):
                act()
        drain(len(order))
        for n in sorted(jobs):
            for act in jobs[n]:
                act()
        for p in some + ("yao",):
            twins[HOPS, p].wait_recv()
        last = chip_at(r + HOPS) * 2
        experts_of(last)
        experts_of(last + 1)
        for copy in shares:
            copy.wait_recv()
        for copy in sent:
            copy.wait_send()

    vmem, smem = pl.BlockSpec(memory_space=VMEM), pl.BlockSpec(memory_space=pltpu.SMEM)
    return pl.pallas_call(
        kernel,
        out_shape=(
            jax.ShapeDtypeStruct((tall, width), bf16),
            jax.ShapeDtypeStruct((blocks * tall, hidden), bf16),
            jax.ShapeDtypeStruct((blocks, 1, tall), f32),
        ),
        in_specs=[smem] * 3 + [vmem] * 8 + [pl.BlockSpec(memory_space=pl.ANY)] * 6,
        out_specs=(vmem, vmem, vmem),
        scratch_shapes=[
            VMEM((width, local), bf16),
            VMEM((width, local), bf16),
            VMEM((width, local), bf16),
            VMEM((local, width), bf16),
            VMEM((width, hidden), bf16),
            VMEM((width, hidden), bf16),
            VMEM((tall, width), bf16),
            VMEM((tall, width), bf16),
            VMEM((2, cached, local), bf16),
            VMEM((groups, near, 2 * pair), bf16),
            VMEM((tall, local), bf16),
            VMEM((tall, local), bf16),
            VMEM((tall, cached + near), f32),
            VMEM((tall, width), bf16),
            VMEM((tall, width), bf16),
            VMEM((blocks * tall, width), bf16),
            VMEM((experts, 1, tall), f32),
            pltpu.SemaphoreType.DMA((6,)),
            pltpu.SemaphoreType.DMA((sems,)),
            pltpu.SemaphoreType.DMA((sems,)),
        ],
        compiler_params=pltpu.CompilerParams(
            collective_id=8, has_side_effects=True, vmem_limit_bytes=60 << 20
        ),
        name="front",
    )(lengths, request_group, shard_group, tokens, gain, freq, prefix_keys,
      prefix_values, moe_gain, w_router.T, routes.T, w_query, w_key, w_value, w_out,
      w_gate, w_up)


def attention(query, prefix_keys, prefix_values, suffix, bias):
    tall, wide = query.shape
    heads = wide // HD
    cached = prefix_keys.shape[0]
    keys = bias.shape[1]
    many = len(suffix)
    scale = HD ** (-0.5)

    def kernel(query_ref, cached_k, cached_v, bias_ref, *rest):
        suffix_k, suffix_v, out_ref = rest[:many], rest[many : 2 * many], rest[2 * many]
        head = query_ref[...]
        scores = [
            lax.dot_general(
                head, block[...], (((1,), (1,)), ((), ())), preferred_element_type=jnp.float32
            )
            for block in (cached_k, *suffix_k)
        ]
        scores = jnp.concatenate(scores, 1) * scale + bias_ref[...]
        weights = jnp.exp(scores - jnp.max(scores, -1, keepdims=True))
        total = jnp.sum(weights, -1, keepdims=True)
        weights = weights.astype(jnp.bfloat16)
        summed = jnp.dot(weights[:, :cached], cached_v[...], preferred_element_type=jnp.float32)
        for n, block in enumerate(suffix_v):
            start = cached + n * tall
            summed += jnp.dot(
                weights[:, start : start + tall], block[...], preferred_element_type=jnp.float32
            )
        out_ref[...] = (summed / total).astype(jnp.bfloat16)

    def column(rows, offset):
        return pl.BlockSpec((rows, HD), lambda h: (0, h + offset))

    return pl.pallas_call(
        kernel,
        out_shape=jax.ShapeDtypeStruct((tall, wide), jnp.bfloat16),
        grid=(heads,),
        in_specs=[column(tall, 0), column(cached, 0), column(cached, 0)]
        + [pl.BlockSpec((tall, keys), lambda h: (0, 0))]
        + [column(tall, 0)] * many
        + [column(tall, heads)] * many,
        out_specs=column(tall, 0),
        cost_estimate=pl.CostEstimate(
            flops=4 * tall * keys * wide, bytes_accessed=4 * keys * wide, transcendentals=0
        ),
        name="attention",
    )(query, prefix_keys, prefix_values, bias, *suffix, *suffix)


def on_device(
    tokens,
    attn_gain,
    w_query,
    w_key,
    w_value,
    w_out,
    prefix_keys,
    prefix_values,
    shard_group,
    request_group,
    lengths,
    moe_gain,
    w_router,
    w_gate,
    w_up,
    w_down,
    routes,
    final_gain,
    w_head,
):
    f32 = jnp.float32
    bf16 = jnp.bfloat16
    seq_index = lax.axis_index("seq")
    tp_index = lax.axis_index("tp")
    seq_count = lax.axis_size("seq")
    tp_count = lax.axis_size("tp")
    tok_dev = tokens.shape[0]
    width_part = tokens.shape[1]
    shard_rows = prefix_keys.shape[0]
    prefix_length = shard_rows * seq_count // 2
    ends = prefix_sums(lengths)
    experts = w_router.shape[1]
    topk = routes.shape[1]
    local_index = seq_index * tok_dev + jnp.arange(tok_dev)
    if seq_count == 16 and tp_count == 2 and experts == seq_count:
        resid_full, act, shares = front(
            tokens, attn_gain, w_query, w_key, w_value, w_out, prefix_keys, prefix_values, lengths,
            request_group, shard_group, moe_gain, w_router, routes,
            w_gate[0], w_up[0],
        )
        return back(act, shares, w_down[0], resid_full, lengths, final_gain, w_head)
    full_x = gather_columns(tokens)
    width = full_x.shape[1]
    normed = normalize(full_x.astype(f32), attn_gain).astype(bf16)
    heads = w_query.shape[1] // HD
    starts = ends - lengths
    own_request = request_of(local_index, ends)
    own_start = lookup(own_request, starts)
    own_group = lookup(own_request, request_group)
    position = (prefix_length + local_index - own_start).astype(f32)
    query = rotate(
        jnp.dot(normed, w_query, preferred_element_type=f32).reshape(tok_dev, heads, HD), position
    ).astype(bf16)
    key_rows = rotate(
        jnp.dot(normed, w_key, preferred_element_type=f32).reshape(tok_dev, heads, HD), position
    ).astype(bf16)
    key_rows = key_rows.reshape(tok_dev, heads * HD)
    value_rows = jnp.dot(normed, w_value, preferred_element_type=f32).astype(bf16)
    pieces = (
        lax.all_gather(prefix_keys, "seq", axis=0, tiled=True),
        lax.all_gather(prefix_values, "seq", axis=0, tiled=True),
    )
    count = pieces[0].shape[0]
    shard_ids = jnp.arange(count) // shard_rows
    key_group = lookup(shard_ids, shard_group)
    fold_allowed = own_group[:, None] == key_group[None, :]
    own_allowed = (own_request[:, None] == own_request[None, :]) & (
        local_index[None, :] <= local_index[:, None]
    )
    both_rows = jnp.concatenate([key_rows, value_rows], 1)
    suffix = [both_rows] + [from_behind(both_rows, "seq", step) for step in range(1, SPAN + 1)]
    permitted = [fold_allowed, own_allowed]
    for step in range(1, SPAN + 1):
        key_index = (seq_index - step) * tok_dev + jnp.arange(tok_dev)
        key_request = request_of(key_index, ends)
        permitted.append(
            (key_index >= 0)[None, :] & (own_request[:, None] == key_request[None, :])
        )
    bias = jnp.where(jnp.concatenate(permitted, 1), 0.0, NEGATIVE)
    attended = attention(query.reshape(tok_dev, heads * HD), *pieces, suffix, bias)
    mixed = jnp.dot(attended, w_out, preferred_element_type=f32).astype(bf16)
    resid_full = (full_x.astype(f32) + sum_over_tp(mixed)).astype(bf16)
    moe_in = normalize(resid_full.astype(f32), moe_gain).astype(bf16)
    probs = jax.nn.softmax(jnp.dot(moe_in, w_router, preferred_element_type=f32), -1)
    flat = routes.reshape(-1)
    hits = (flat[:, None] == jnp.arange(experts)[None, :]).astype(jnp.int32)
    line = jnp.arange(flat.shape[0])
    before = (line[:, None] > line[None, :]).astype(bf16)
    earlier = jnp.dot(before, hits.astype(bf16), preferred_element_type=f32).astype(jnp.int32)
    rank = jnp.sum(earlier * hits, 1)
    capacity = min(tok_dev, tp_count * max(1, 3 * tok_dev * topk // (2 * experts * tp_count)))
    target = flat * capacity + rank
    route_weight = jnp.sum(hits.reshape(tok_dev, topk, experts).astype(f32) * probs[:, None, :], -1)
    repeated = jnp.repeat(moe_in, topk, axis=0)
    outgoing = (
        jnp.zeros((experts * capacity, width), bf16)
        .at[target]
        .set(repeated)
        .reshape(experts, capacity, width)
    )
    arrived = lax.all_to_all(outgoing, "seq", split_axis=0, concat_axis=0, tiled=True)
    sources = arrived.shape[0]
    count = arrived.shape[1]
    rows = arrived.reshape(sources * count, width)
    gate = jnp.dot(rows, w_gate[0], preferred_element_type=f32)
    up = jnp.dot(rows, w_up[0], preferred_element_type=f32)
    act = (jax.nn.silu(gate) * up).astype(bf16)
    partial_out = jnp.dot(act, w_down[0], preferred_element_type=f32).reshape(sources, count, width)
    summed = lax.psum_scatter(partial_out, "tp", scatter_dimension=2, tiled=True).astype(bf16)
    returned = lax.all_to_all(summed, "seq", split_axis=0, concat_axis=0, tiled=True)
    picked = returned.reshape(experts * capacity, width_part)[target].reshape(
        tok_dev, topk, width_part
    )
    moe_part = jnp.sum(picked.astype(f32) * route_weight[:, :, None], 1)
    resid = lax.dynamic_slice_in_dim(resid_full, tp_index * width_part, width_part, 1)
    hidden = (resid.astype(f32) + moe_part).astype(bf16)
    last_hit = ((ends - 1)[:, None] == local_index[None, :]).astype(bf16)
    chosen = jnp.dot(last_hit, hidden, preferred_element_type=f32)
    final = last_rows(chosen, final_gain, width)
    log_probs = log_softmax(jnp.dot(final, w_head, preferred_element_type=f32))
    return (hidden, log_probs)


def solution(mesh):
    in_specs = (
        P("seq", "tp"),
        P(),
        P(None, "tp"),
        P(None, "tp"),
        P(None, "tp"),
        P("tp", None),
        P("seq", "tp"),
        P("seq", "tp"),
        P(),
        P(),
        P(),
        P(),
        P(),
        P("seq", None, "tp"),
        P("seq", None, "tp"),
        P("seq", "tp", None),
        P("seq", None),
        P("tp"),
        P("tp", "seq"),
    )
    out_specs = (P("seq", "tp"), P(None, "seq"))
    return jax.shard_map(
        on_device, mesh=mesh, in_specs=in_specs, out_specs=out_specs, check_vma=False
    )
```

```python
import jax
import jax.numpy as jnp
import numpy as np
from jax import lax
from jax.experimental import pallas as pl
from jax.experimental.pallas import tpu as pltpu
from jax.sharding import PartitionSpec as P

HD = 128
SPAN = 4
VMEM = pltpu.VMEM


EPS = 1e-05
NEGATIVE = -1e30


def from_behind(value, axis, steps):
    count = lax.axis_size(axis)
    leading, last = (max(0, -steps), min(count, count - steps))
    return lax.ppermute(value, axis, [(source, source + steps) for source in range(leading, last)])


def normalize(rows, gain):
    inv = lax.rsqrt(jnp.mean(rows * rows, -1, keepdims=True) + EPS)
    return rows * inv * gain.astype(jnp.float32)


def rotate(vectors, position):
    half = vectors.shape[-1] // 2
    freq = 10000.0 ** (-jnp.arange(half).astype(jnp.float32) / half)
    angle = position[:, None] * freq[None, :]
    cosine = jnp.cos(angle)[:, None, :]
    sine = jnp.sin(angle)[:, None, :]
    first = vectors[..., :half]
    second = vectors[..., half:]
    return jnp.concatenate([first * cosine - second * sine, second * cosine + first * sine], -1)


def request_of(index, ends):
    return jnp.sum((index[:, None] >= ends[None, :]).astype(jnp.int32), 1)


def lookup(selector, table):
    hit = selector[:, None] == jnp.arange(table.shape[0])[None, :]
    return jnp.sum(jnp.where(hit, table[None, :], 0), 1)


def prefix_sums(values):
    order = jnp.arange(values.shape[0])
    return jnp.sum(jnp.where(order[:, None] >= order[None, :], values[None, :], 0), 1)


def partner(axis, bit):
    index = lax.axis_index(axis)
    span = 1 << bit
    other = index + span - 2 * span * ((index // span) % 2)
    return {axis: other}


def greet(stages):
    barrier = pltpu.get_barrier_semaphore()
    for axis, bit in stages:
        pl.semaphore_signal(barrier, inc=1, device_id=partner(axis, bit))
    pl.semaphore_wait(barrier, len(stages))


def swap(source, target, send_sem, recv_sem, stage):
    copy = pltpu.make_async_remote_copy(
        src_ref=source, dst_ref=target, send_sem=send_sem, recv_sem=recv_sem,
        device_id=partner(*stage),
    )
    copy.start()
    return copy


def bits_of(axis):
    return [(axis, bit) for bit in range(lax.axis_size(axis).bit_length() - 1)]


def last_rows(chosen, gain, width):
    seq_stages, tp_stages = bits_of("seq"), bits_of("tp")
    stages = seq_stages + tp_stages
    rows, part = chosen.shape

    def kernel(chosen_ref, gain_ref, out_ref, held, got, sq_held, sq_got, send_sem, recv_sem):
        greet(stages)
        held[0] = chosen_ref[...]
        count = len(seq_stages)
        for k, stage in enumerate(seq_stages):
            swap(held.at[k], got.at[k], send_sem.at[k], recv_sem.at[k], stage).wait()
            held[k + 1] = held[k] + got[k]
        total = held[count]
        sq_held[0] = jnp.broadcast_to(jnp.sum(total * total, -1, keepdims=True), (rows, 128))
        for k, stage in enumerate(tp_stages):
            n = count + k
            swap(sq_held.at[k], sq_got.at[k], send_sem.at[n], recv_sem.at[n], stage).wait()
            sq_held[k + 1] = sq_held[k] + sq_got[k]
        square = sq_held[len(tp_stages)][:, :1]
        scaled = total * lax.rsqrt(square / width + EPS) * gain_ref[...].astype(jnp.float32)
        out_ref[...] = scaled.astype(jnp.bfloat16)

    ns, nt = len(seq_stages), len(tp_stages)
    return pl.pallas_call(
        kernel,
        out_shape=jax.ShapeDtypeStruct((rows, part), jnp.bfloat16),
        in_specs=[pl.BlockSpec(memory_space=VMEM)] * 2,
        out_specs=pl.BlockSpec(memory_space=VMEM),
        scratch_shapes=[
            VMEM((ns + 1, rows, part), jnp.float32),
            VMEM((ns, rows, part), jnp.float32),
            VMEM((nt + 1, rows, 128), jnp.float32),
            VMEM((nt, rows, 128), jnp.float32),
            pltpu.SemaphoreType.DMA((ns + nt,)),
            pltpu.SemaphoreType.DMA((ns + nt,)),
        ],
        compiler_params=pltpu.CompilerParams(collective_id=1, has_side_effects=True),
        name="last_rows",
    )(chosen, gain.reshape(1, part))


def log_softmax(logits):
    seq_stages, tp_stages = bits_of("seq"), bits_of("tp")
    stages = tp_stages + seq_stages
    rows, part = logits.shape

    def kernel(logits_ref, out_ref, held, got, st_held, st_got, send_sem, recv_sem):
        greet(stages)
        held[0] = logits_ref[...]
        count = len(tp_stages)
        for k, stage in enumerate(tp_stages):
            swap(held.at[k], got.at[k], send_sem.at[k], recv_sem.at[k], stage).wait()
            held[k + 1] = held[k] + got[k]
        total = held[count]
        peak = jnp.max(total, -1, keepdims=True)
        mass = jnp.sum(jnp.exp(total - peak), -1, keepdims=True)
        st_held[0, :, :128] = jnp.broadcast_to(peak, (rows, 128))
        st_held[0, :, 128:] = jnp.broadcast_to(mass, (rows, 128))
        for k, stage in enumerate(seq_stages):
            n = count + k
            swap(st_held.at[k], st_got.at[k], send_sem.at[n], recv_sem.at[n], stage).wait()
            mine, theirs = st_held[k, :, :128], st_got[k, :, :128]
            top = jnp.maximum(mine, theirs)
            st_held[k + 1, :, :128] = top
            st_held[k + 1, :, 128:] = st_held[k, :, 128:] * jnp.exp(mine - top) + st_got[
                k, :, 128:
            ] * jnp.exp(theirs - top)
        last = len(seq_stages)
        out_ref[...] = total - st_held[last, :, :1] - jnp.log(st_held[last, :, 128:129])

    ns, nt = len(seq_stages), len(tp_stages)
    return pl.pallas_call(
        kernel,
        out_shape=jax.ShapeDtypeStruct((rows, part), jnp.float32),
        in_specs=[pl.BlockSpec(memory_space=VMEM)],
        out_specs=pl.BlockSpec(memory_space=VMEM),
        scratch_shapes=[
            VMEM((nt + 1, rows, part), jnp.float32),
            VMEM((nt, rows, part), jnp.float32),
            VMEM((ns + 1, rows, 256), jnp.float32),
            VMEM((ns, rows, 256), jnp.float32),
            pltpu.SemaphoreType.DMA((ns + nt,)),
            pltpu.SemaphoreType.DMA((ns + nt,)),
        ],
        compiler_params=pltpu.CompilerParams(collective_id=2, has_side_effects=True),
        name="log_softmax",
    )(logits)


def gather_columns(block):
    stages = bits_of("tp")
    rows, part = block.shape
    count = lax.axis_size("tp")

    def kernel(block_ref, out_ref, send_sem, recv_sem):
        greet(stages)
        me = lax.axis_index("tp")
        out_ref[:, pl.ds(pl.multiple_of(me * part, part), part)] = block_ref[...]
        for k, stage in enumerate(stages):
            wide = part << k
            start = pl.multiple_of((me // (1 << k)) * wide, wide)
            piece = out_ref.at[:, pl.ds(start, wide)]
            swap(piece, piece, send_sem.at[k], recv_sem.at[k], stage).wait()

    return pl.pallas_call(
        kernel,
        out_shape=jax.ShapeDtypeStruct((rows, part * count), block.dtype),
        in_specs=[pl.BlockSpec(memory_space=VMEM)],
        out_specs=pl.BlockSpec(memory_space=VMEM),
        scratch_shapes=[pltpu.SemaphoreType.DMA((len(stages),))] * 2,
        compiler_params=pltpu.CompilerParams(collective_id=3, has_side_effects=True),
        name="gather_columns",
    )(block)


def sum_over_tp(block):
    stages = bits_of("tp")
    rows, part = block.shape

    def kernel(block_ref, out_ref, held, got, send_sem, recv_sem):
        greet(stages)
        for k, stage in enumerate(stages):
            source = block_ref if k == 0 else held.at[k]
            swap(source, got.at[k], send_sem.at[k], recv_sem.at[k], stage).wait()
            total = source[...].astype(jnp.float32) + got[k].astype(jnp.float32)
            if k + 1 < len(stages):
                held[k + 1] = total.astype(jnp.bfloat16)
            else:
                out_ref[...] = total

    count = len(stages)
    return pl.pallas_call(
        kernel,
        out_shape=jax.ShapeDtypeStruct((rows, part), jnp.float32),
        in_specs=[pl.BlockSpec(memory_space=VMEM)],
        out_specs=pl.BlockSpec(memory_space=VMEM),
        scratch_shapes=[
            VMEM((count, rows, part), jnp.bfloat16),
            VMEM((count, rows, part), jnp.bfloat16),
            pltpu.SemaphoreType.DMA((count,)),
            pltpu.SemaphoreType.DMA((count,)),
        ],
        compiler_params=pltpu.CompilerParams(collective_id=4, has_side_effects=True),
        name="sum_over_tp",
    )(block)


HOPS = 4


def ring_place():
    s = lax.axis_index("seq")
    core = s % 2
    x = (s // 2) % 2
    z = s // 4
    return s, core, z + x * (7 - 2 * z)


def chip_at(place):
    q = (place + 16) % 8
    x = q // 4
    z = q + x * (7 - 2 * q)
    return z * 2 + x


def greet_all(blocks):
    s = lax.axis_index("seq")
    barrier = pltpu.get_barrier_semaphore()
    for d in range(1, blocks):
        pl.semaphore_signal(barrier, inc=1, device_id={"seq": (s + d) % blocks})
    pl.semaphore_signal(barrier, inc=1, device_id={"tp": 1 - lax.axis_index("tp")})
    pl.semaphore_wait(barrier, blocks)


def back(act, shares, w_down, resid, lengths, gain, w_head):
    tall, wide = resid.shape
    half = wide // 2
    hidden = act.shape[1]
    count = shares.shape[0]
    reqs = lengths.shape[0]
    cols = w_head.shape[1]
    padded = -(-cols // 128) * 128
    high = -(-reqs // 16) * 16
    fold = high // reqs
    slim = half // fold
    cuts = 4
    per = -(-cols // (128 * cuts)) * 128
    spans = [(k * per, min(per, cols - k * per)) for k in range(cuts)]
    f32 = jnp.float32
    ty = tall // 2
    ts = tall - ty
    sems = 80
    bf16 = jnp.bfloat16
    G = 16
    units = [(HOPS, "o")] + [(t, b) for t in range(HOPS - 1, 0, -1) for b in ("s", "o")] + [(0, "o")]
    nu = len(units)

    def kernel(len_ref, share_ref, gain_ref, act_hbm, resid_hbm, wd_hbm, wh_hbm, out_ref, logs_ref,
               act_ref, resid_ref, wd, wh, part_ref, sib_buf, acc_y, acc_s, y_send, y_recv, ring_y, ring_s, far_y, far_s, last_recv,
               near, far, logit, got, stats, w_sem, send_sem, recv_sem):
        loads = []
        stores = ((wd_hbm, wd), (act_hbm, act_ref), (resid_hbm, resid_ref), (wh_hbm, wh))
        for n, (source, target) in enumerate(stores):
            loads.append(pltpu.make_async_copy(source, target, w_sem.at[n]))
            loads[n].start()
        s, core, r = ring_place()
        y = lax.axis_index("tp")
        step = 1 - 2 * core
        nxt = {"seq": chip_at(r + step) * 2 + core}
        sib = {"seq": s + step}
        other = {"tp": 1 - y}
        eye = lax.broadcasted_iota(jnp.int32, (tall, tall), 0) == lax.broadcasted_iota(
            jnp.int32, (tall, tall), 1
        )

        def project(place):
            rows = pl.ds(pl.multiple_of(place * tall, tall), tall)
            weight = jnp.sum(jnp.where(eye, share_ref[place], 0.0), -1, keepdims=True)
            product = jnp.dot(act_ref[rows], wd[...], preferred_element_type=f32)
            part_ref[rows] = (product * weight).astype(bf16)

        greet_all(count)
        loads[0].wait()
        loads[1].wait()
        used = iter(range(sems))
        own_cols = pl.ds(pl.multiple_of(y * half, half), half)
        far_cols = pl.ds(pl.multiple_of((1 - y) * half, half), half)

        def send(source, target, device):
            n = next(used)
            copy = pltpu.make_async_remote_copy(
                src_ref=source, dst_ref=target, send_sem=send_sem.at[n], recv_sem=recv_sem.at[n],
                device_id=device,
            )
            copy.start()
            return copy

        def rows_of(t, b, direction, c):
            return chip_at(r + direction * t) * 2 + (c if b == "o" else 1 - c)

        pair, cross, ring, sent = {}, {}, {}, []

        def lend(i):
            if i < nu:
                place = rows_of(*units[i], -step, 1 - core)
                project(place)
                start = pl.multiple_of(place * tall, tall)
                pair[i] = send(part_ref.at[pl.ds(start, tall)], sib_buf.at[i], sib)
                sent.append(pair[i])

        lend(0)
        lend(1)

        def summed(i):
            t, b = units[i]
            place = rows_of(t, b, step, core)
            project(place)
            start = place * tall
            pair[i].wait_recv()

            def body_y(g, _):
                rows = pl.ds(pl.multiple_of(g * G, G), G)
                here = pl.ds(pl.multiple_of(start + g * G, G), G)
                y_send[i, rows] = part_ref[here, far_cols] + sib_buf[i, rows, far_cols]
                acc_y[i, rows] = part_ref[here, own_cols] + sib_buf[i, rows, own_cols]
                return 0

            lax.fori_loop(0, ty // G, body_y, 0)
            cross[i] = send(y_send.at[i], y_recv.at[i], other)
            sent.append(cross[i])

            def body_s(g, _):
                rows = pl.ds(pl.multiple_of(g * G, G), G)
                below = pl.ds(pl.multiple_of(ty + g * G, G), G)
                here = pl.ds(pl.multiple_of(start + ty + g * G, G), G)
                acc_s[i, rows] = part_ref[here] + sib_buf[i, below]
                return 0

            lax.fori_loop(0, ts // G, body_s, 0)
            if not arriving(t, b) and t > 0:
                pass_s(i)
            lend(i + 2)

        def slot(t, b):
            return 2 * t + (0 if b == "o" else 1)

        def arriving(t, b):
            return (t + 1, b) in units and t > 0

        def pass_s(i):
            t, b = units[i]
            m = slot(t - 1, b)
            ring[t - 1, b, "s"] = send(acc_s.at[i], ring_s.at[m], nxt)
            sent.append(ring[t - 1, b, "s"])

        def passed(i):
            t, b = units[i]
            arrived = arriving(t, b)
            n = slot(t, b)
            if arrived:
                ring[t, b, "s"].wait_recv()

                def body_s(g, _):
                    rows = pl.ds(pl.multiple_of(g * G, G), G)
                    acc_s[i, rows] = acc_s[i, rows] + ring_s[n, rows]
                    return 0

                lax.fori_loop(0, ts // G, body_s, 0)
                pass_s(i)
                ring[t, b, "y"].wait_recv()
            cross[i].wait_recv()

            def body_y(g, _):
                rows = pl.ds(pl.multiple_of(g * G, G), G)
                total = acc_y[i, rows] + y_recv[i, rows]
                if arrived:
                    total = total + ring_y[n, rows]
                acc_y[i, rows] = total
                return 0

            lax.fori_loop(0, ty // G, body_y, 0)
            if t > 0:
                m = slot(t - 1, b)
                ring[t - 1, b, "y"] = send(acc_y.at[i], ring_y.at[m], nxt)
                sent.append(ring[t - 1, b, "y"])

        summed(0)
        summed(1)
        for i in range(nu):
            if i + 2 < nu:
                summed(i + 2)
            passed(i)
        m, n, i = slot(0, "s"), slot(0, "o"), nu - 1
        ring[0, "s", "s"].wait_recv()
        far_copy_s = send(ring_s.at[m], far_s, sib)
        ring[0, "s", "y"].wait_recv()
        far_copy_y = send(ring_y.at[m], far_y, sib)
        sent.extend((far_copy_s, far_copy_y))
        ring[0, "o", "s"].wait_recv()
        far_copy_s.wait_recv()

        def body_s(g, _):
            rows = pl.ds(pl.multiple_of(g * G, G), G)
            acc_s[i, rows] = acc_s[i, rows] + ring_s[n, rows] + far_s[rows]
            return 0

        lax.fori_loop(0, ts // G, body_s, 0)
        last = send(acc_s.at[i, :, far_cols], last_recv, other)
        sent.append(last)
        loads[2].wait()
        ring[0, "o", "y"].wait_recv()
        far_copy_y.wait_recv()

        def body_y(g, _):
            rows = pl.ds(pl.multiple_of(g * G, G), G)
            total = acc_y[i, rows].astype(f32) + ring_y[n, rows].astype(f32) + far_y[rows].astype(f32)
            out_ref[rows] = (total + resid_ref[rows, own_cols].astype(f32)).astype(bf16)
            return 0

        lax.fori_loop(0, ty // G, body_y, 0)
        last.wait_recv()

        def body_l(g, _):
            rows = pl.ds(pl.multiple_of(g * G, G), G)
            here = pl.ds(pl.multiple_of(ty + g * G, G), G)
            total = acc_s[i, rows, own_cols].astype(f32) + last_recv[rows].astype(f32)
            out_ref[here] = (total + resid_ref[here, own_cols].astype(f32)).astype(bf16)
            return 0

        lax.fori_loop(0, ts // G, body_l, 0)
        row = lax.broadcasted_iota(jnp.int32, (high, tall), 0)
        place = lax.broadcasted_iota(jnp.int32, (high, tall), 1) + s * tall
        last = jnp.full((high, tall), -1, jnp.int32)
        end = 0
        for j in range(reqs):
            end = end + len_ref[j]
            last = jnp.where(row == j, end - 1, last)
        hit = (last == place).astype(f32).astype(bf16)
        chosen = jnp.dot(hit, out_ref[...], preferred_element_type=f32)
        chosen = [chosen[:reqs, n * slim : (n + 1) * slim] for n in range(fold)]
        near[0] = jnp.concatenate(chosen, 0).astype(bf16)

        def note(source, target, device):
            sent.append(send(source, target, device))
            return sent[-1]

        first = [
            note(near.at[0], near.at[d], {"seq": (s // 4) * 4 + (s + d) % 4}) for d in range(1, 4)
        ]
        for copy in first:
            copy.wait_recv()
        far[0] = (near[0] + near[1]) + (near[2] + near[3])
        second = [note(far.at[0], far.at[d], {"seq": (s + 4 * d) % count}) for d in range(1, 4)]
        for copy in second:
            copy.wait_recv()
        total = ((far[0] + far[1]) + (far[2] + far[3])).astype(f32)
        total = jnp.concatenate([total[n * reqs : (n + 1) * reqs] for n in range(fold)], 1)
        square = jnp.sum(total * total, -1, keepdims=True)
        scaled = total * gain_ref[...].astype(f32)[None, :]
        scaled = jnp.concatenate([scaled] + [jnp.zeros_like(scaled)] * (fold - 1), 0).astype(bf16)
        logit[:, padded:] = jnp.broadcast_to(square, (reqs, 128))
        loads[3].wait()
        swapped = [note(logit.at[:, padded:], got.at[:, padded:], other)]
        for k, (start, size) in enumerate(spans):
            product = lax.dot_general(
                scaled, wh[start : start + size], (((1,), (1,)), ((), ())), preferred_element_type=f32
            )
            logit[:, start : start + size] = product[:reqs]
            full = per if k < cuts - 1 else padded - start
            swapped.append(note(logit.at[:, start : start + full], got.at[:, start : start + full], other))
        for copy in swapped:
            copy.wait_recv()
        square = logit[:, padded : padded + 1] + got[:, padded : padded + 1]
        inv = lax.rsqrt(square / wide + EPS)
        both = (logit[:, :cols] + got[:, :cols]) * inv
        peak = jnp.max(both, -1, keepdims=True)
        mass = jnp.sum(jnp.exp(both - peak), -1, keepdims=True)
        lane = lax.broadcasted_iota(jnp.int32, (reqs, 128), 1)
        stats[0] = jnp.where(lane < 64, peak, mass)
        third = [note(stats.at[0], stats.at[d], {"seq": (s + d) % count}) for d in range(1, count)]
        for copy in third:
            copy.wait_recv()
        everyone = stats[...]
        peaks, masses = everyone[:, :, :1], everyone[:, :, 64:65]
        top = jnp.max(peaks, 0)
        whole = jnp.sum(masses * jnp.exp(peaks - top[None]), 0)
        logs_ref[...] = both - top - jnp.log(whole)
        for copy in sent:
            copy.wait_send()

    vmem, hbm = pl.BlockSpec(memory_space=VMEM), pl.BlockSpec(memory_space=pl.ANY)
    return pl.pallas_call(
        kernel,
        out_shape=(
            jax.ShapeDtypeStruct((tall, half), bf16),
            jax.ShapeDtypeStruct((reqs, cols), f32),
        ),
        in_specs=[pl.BlockSpec(memory_space=pltpu.SMEM)] + [vmem] * 2 + [hbm] * 4,
        out_specs=(vmem, vmem),
        scratch_shapes=[
            VMEM((count * tall, hidden), bf16),
            VMEM((tall, wide), bf16),
            VMEM((hidden, wide), bf16),
            VMEM((cols, half), bf16),
            VMEM((count * tall, wide), bf16),
            VMEM((nu, tall, wide), bf16),
            VMEM((nu, ty, half), bf16), VMEM((nu, ts, wide), bf16),
            VMEM((nu, ty, half), bf16), VMEM((nu, ty, half), bf16),
            VMEM((2 * HOPS, ty, half), bf16), VMEM((2 * HOPS, ts, wide), bf16),
            VMEM((ty, half), bf16), VMEM((ts, wide), bf16), VMEM((ts, half), bf16),
            VMEM((4, high, slim), bf16), VMEM((4, high, slim), bf16),
            VMEM((reqs, padded + 128), f32), VMEM((reqs, padded + 128), f32),
            VMEM((count, reqs, 128), f32),
            pltpu.SemaphoreType.DMA((4,)),
            pltpu.SemaphoreType.DMA((sems,)),
            pltpu.SemaphoreType.DMA((sems,)),
        ],
        compiler_params=pltpu.CompilerParams(
            collective_id=6, has_side_effects=True, vmem_limit_bytes=60 << 20
        ),
        name="back",
    )(lengths, shares, gain, act, resid, w_down, w_head.T)


def front(tokens, gain, w_query, w_key, w_value, w_out, prefix_keys, prefix_values, lengths,
          request_group, shard_group, moe_gain, w_router, routes, w_gate, w_up):
    tall, part = tokens.shape
    width = 2 * part
    local = w_query.shape[1]
    shard = prefix_keys.shape[0]
    shards = shard_group.shape[0]
    reqs = lengths.shape[0]
    cached = shard * shards
    experts = w_router.shape[1]
    topk = routes.shape[1]
    bf16, f32 = jnp.bfloat16, jnp.float32
    pair = 2 * HD
    groups = local // pair
    slots = SPAN + 1
    near = slots * tall
    hidden = w_gate.shape[1]
    blocks = 16
    q = tall // 4
    sems = 136
    turn = HD // 2
    freq = np.power(10000.0, -np.arange(turn) / turn)
    freq = np.stack([np.tile(freq, 2), np.repeat([-1.0, 1.0], turn)])
    freq = jnp.asarray(np.tile(freq, (4, 1)), jnp.float32)
    scale = HD ** (-0.5)
    nt = (((1,), (1,)), ((), ()))

    def kernel(len_ref, rg_ref, sg_ref, tok_ref, gain_ref, freq_ref, pk_ref, pv_ref, mg_ref,
               wr_ref, routes_ref, wq_ref, wk_ref, wv_ref, wo_ref, wg_ref, wu_ref, resid_ref, act_ref,
               share_out, wq, wk, wv, wo, wg, wu, x, normed, cache, kv, query, attended, bias, mix, mix_got,
               all_rows, share_own, w_sem, send_sem, recv_sem):
        loads = {}
        for n, (source, target) in enumerate((
            (wk_ref, wk), (wv_ref, wv), (wq_ref, wq), (wo_ref, wo), (wg_ref, wg), (wu_ref, wu)
        )):
            loads[n] = pltpu.make_async_copy(source, target, w_sem.at[n])
            loads[n].start()
        s, core, r = ring_place()
        y = lax.axis_index("tp")
        count = 16
        step = 1 - 2 * core
        ahead = 1 - 2 * ((s // 2) % 2)
        nxt = {"seq": chip_at(r + step) * 2 + core}
        sib = {"seq": s + step}
        side = {"seq": s + 2 * ahead}
        above = {"seq": (s + 4) % count}
        other = {"tp": 1 - y}
        own_cols = pl.ds(pl.multiple_of(y * part, part), part)
        x[:, own_cols] = tok_ref[...]
        own_rows = pl.ds(pl.multiple_of(s * shard, shard), shard)
        cache[0, own_rows] = pk_ref[...]
        cache[1, own_rows] = pv_ref[...]
        greet_all(count)
        used = iter(range(sems))
        sent = []

        def send(source, target, device):
            n = next(used)
            copy = pltpu.make_async_remote_copy(
                src_ref=source, dst_ref=target, send_sem=send_sem.at[n], recv_sem=recv_sem.at[n],
                device_id=device,
            )
            copy.start()
            sent.append(copy)
            return copy

        def move(chip, name, device):
            which, owner = name
            shift = core if owner == "o" else 1 - core
            rows = pl.ds(pl.multiple_of((chip * 2 + shift) * shard, shard), shard)
            view = cache.at[which, rows]
            return send(view, view, device)

        home = chip_at(r)
        swapped = [move(home, (which, "o"), sib) for which in range(2)]
        ring, twin = {}, {}
        for which in range(2):
            ring[1, (which, "o")] = move(home, (which, "o"), nxt)
        crossing = send(tok_ref, x.at[:, own_cols], other)
        for which in range(2):
            swapped[which].wait_recv()
            ring[1, (which, "s")] = move(home, (which, "s"), nxt)

        def hop(t):
            chip = chip_at(r - step * t)
            owners = ("o", "s") if t < HOPS else ("o",)
            for owner in owners:
                for which in range(2):
                    name = (which, owner)
                    ring[t, name].wait_recv()
                    if t < HOPS - 1 or (t == HOPS - 1 and owner == "o"):
                        ring[t + 1, name] = move(chip, name, nxt)
                    twin[t, name] = move(chip, name, sib)

        lane = lax.broadcasted_iota(jnp.int32, (tall, 128), 0) + s * tall
        mine = jnp.zeros((tall, 128), jnp.int32)
        ends, end = [], 0
        for j in range(reqs):
            end = end + len_ref[j]
            ends.append(end)
        for j in range(reqs):
            mine = mine + (lane >= ends[j]).astype(jnp.int32)
        group = jnp.zeros((tall, 128), jnp.int32)
        for j in range(reqs):
            group = jnp.where(mine == j, rg_ref[j], group)
        begun = jnp.zeros((tall, 128), jnp.int32)
        for j in range(reqs):
            begun = jnp.where(lane >= ends[j], ends[j], begun)
        position = (cached // 2 + lane - begun).astype(f32)
        angle = position * freq_ref[:1]
        cosine, sine = jnp.cos(angle), jnp.sin(angle) * freq_ref[1:2]
        own_index, own_request, own_group = lane[:, :1], mine[:, :1], group[:, :1]
        column = lax.broadcasted_iota(jnp.int32, (8, cached), 1)
        key_group = jnp.zeros((8, cached), jnp.int32)
        for j in range(shards):
            inside = (column >= j * shard) & (column < (j + 1) * shard)
            key_group = jnp.where(inside, sg_ref[j], key_group)
        bias[:, :cached] = jnp.where(own_group == key_group[:1], 0.0, NEGATIVE)
        chip = s // 2
        bases = (
            s * tall, (chip - 1) * 2 * tall, (chip - 1) * 2 * tall + tall, (chip - 2) * 2 * tall + tall,
            (chip - 2 + 2 * core) * 2 * tall,
        )
        for n in range(slots):
            place = lax.broadcasted_iota(jnp.int32, (8, tall), 1) + bases[n]
            theirs = jnp.zeros((8, tall), jnp.int32)
            for j in range(reqs):
                theirs = theirs + (place >= ends[j]).astype(jnp.int32)
            seen = (own_request == theirs[:1]) & (place[:1] <= own_index) & (place[:1] >= 0)
            start = cached + n * tall
            bias[:, start : start + tall] = jnp.where(seen, 0.0, NEGATIVE)
        hop(1)
        hop(2)
        crossing.wait_recv()
        rows = x[...].astype(f32)
        inv = lax.rsqrt(jnp.mean(rows * rows, -1, keepdims=True) + EPS)
        normed[...] = (rows * inv * gain_ref[...].astype(f32)[None, :]).astype(bf16)

        def turned(value):
            heads = []
            for n in range(pair // HD):
                head = value[:, n * HD : (n + 1) * HD]
                heads.append(head * cosine + pltpu.roll(head, HD // 2, 1) * sine)
            return jnp.concatenate(heads, 1).astype(bf16)

        back = 4 - core
        side_slot = 1 + core

        def slot_of(g, n):
            return kv.at[g, pl.ds(pl.multiple_of(n * tall, tall), tall)]

        up = {}

        def keys_of(g):
            cols = slice(g * pair, (g + 1) * pair)
            key = jnp.dot(normed[...], wk[:, cols], preferred_element_type=f32)
            kv[g, :tall, :pair] = turned(key)
            value = jnp.dot(normed[...], wv[:, cols], preferred_element_type=f32)
            kv[g, :tall, pair:] = value.astype(bf16)
            up[g] = send(slot_of(g, 0), slot_of(g, back), above)

        loads[0].wait()
        loads[1].wait()
        keys_of(0)
        hop(3)
        keys_of(1)
        hop(4)
        for g in range(2, groups):
            keys_of(g)
        loads[2].wait()
        for g in range(groups):
            cols = slice(g * pair, (g + 1) * pair)
            query[:, cols] = turned(jnp.dot(normed[...], wq[:, cols], preferred_element_type=f32))
        across, down, inner = {}, {}, {}
        for g in range(groups):
            up[g].wait_recv()
            across[g] = send(slot_of(g, (1 - ahead) // 2 * back), slot_of(g, side_slot), side)
            inner[g] = send(slot_of(g, 3 * core), slot_of(g, back), sib)
        for copy in twin.values():
            copy.wait_recv()
        for g in range(groups):
            across[g].wait_recv()
            down[g] = send(slot_of(g, side_slot), slot_of(g, side_slot), sib)
        for g in range(groups):
            inner[g].wait_recv()
            down[g].wait_recv()
            for n in range(pair // HD):
                cols = slice(g * pair + n * HD, g * pair + (n + 1) * HD)
                k_cols = slice(n * HD, (n + 1) * HD)
                v_cols = slice(pair + n * HD, pair + (n + 1) * HD)
                head = query[:, cols]
                scores = jnp.concatenate(
                    [
                        lax.dot_general(head, cache[0, :, cols], nt, preferred_element_type=f32),
                        lax.dot_general(head, kv[g, :, k_cols], nt, preferred_element_type=f32),
                    ],
                    1,
                )
                scores = scores * scale + bias[...]
                weights = jnp.exp(scores - jnp.max(scores, -1, keepdims=True))
                total = jnp.sum(weights, -1, keepdims=True)
                weights = weights.astype(bf16)
                summed = jnp.dot(weights[:, :cached], cache[1, :, cols], preferred_element_type=f32)
                summed += jnp.dot(weights[:, cached:], kv[g, :, v_cols], preferred_element_type=f32)
                attended[:, cols] = (summed / total).astype(bf16)
        loads[3].wait()
        mine, theirs = core * tall, (1 - core) * tall
        odd = (core + y) % 2
        spot = {
            "ao": mine + q * odd,
            "as": theirs + q * (1 - odd),
            "e1o": mine + 2 * q,
            "e1s": theirs + 2 * q,
            "e2o": mine + 3 * q,
            "e2s": theirs + 3 * q,
            "yo": mine + q * (1 - odd),
            "ys": theirs + q * odd,
        }
        inside = {"ao": q * odd, "e1o": 2 * q, "e2o": 3 * q, "yo": q * (1 - odd)}
        circle, cross, twins = {}, {}, {}

        def put(table, key, hops, name, device):
            start = chip_at(r + hops) * 2 * tall + spot[name]
            view = all_rows.at[pl.ds(pl.multiple_of(start, q), q)]
            table[key] = send(view, view, device)

        mixed = {}
        for n, (away, name) in enumerate((("yo", "ao"), ("e1o", "e1o"), ("e2o", "e2o"), ("ao", "yo"))):
            part_rows = pl.ds(pl.multiple_of(inside[away], q), q)
            product = jnp.dot(attended[part_rows], wo[...], preferred_element_type=f32)
            mix[part_rows] = product.astype(bf16)
            mixed[name] = send(mix.at[part_rows], mix_got.at[part_rows], other)

        def settle(name):
            mixed[name].wait_recv()
            rows = pl.ds(pl.multiple_of(inside[name], q), q)
            total = x[rows].astype(f32) + (mix[rows].astype(f32) + mix_got[rows].astype(f32))
            total = total.astype(bf16)
            resid_ref[rows] = total
            total = total.astype(f32)
            inv = lax.rsqrt(jnp.mean(total * total, -1, keepdims=True) + EPS)
            here = pl.ds(pl.multiple_of(home * 2 * tall + spot[name], q), q)
            all_rows[here] = (total * inv * mg_ref[...].astype(f32)[None, :]).astype(bf16)
            put(twins, (0, name), 0, name, sib)

        pieces = ("ao", "as", "e1o", "e1s", "e2o", "e2s")
        some = ("ao", "e1o", "e2o")
        order = [(t, p) for t in range(1, HOPS) for p in pieces] + [(HOPS, p) for p in some]

        def onward(t, p):
            if t < HOPS - 1 or (t == HOPS - 1 and p in some):
                put(circle, (t + 1, p), -step * t, p, nxt)

        for name in some:
            settle(name)
            onward(0, name)
            twins[0, name].wait_recv()
            onward(0, name[:-1] + "s")
        settle("yo")

        def experts_of(place):
            rows = pl.ds(pl.multiple_of(place * tall, tall), tall)
            gate = jnp.dot(all_rows[rows], wg[...], preferred_element_type=f32)
            raised = jnp.dot(all_rows[rows], wu[...], preferred_element_type=f32)
            act_ref[rows] = (gate / (1.0 + jnp.exp(-gate)) * raised).astype(bf16)

        def route():
            own = all_rows[pl.ds(pl.multiple_of(s * tall, tall), tall)]
            logits = lax.dot_general(wr_ref[...], own, nt, preferred_element_type=f32)
            odds = jnp.exp(logits - jnp.max(logits, 0, keepdims=True))
            probs = odds / jnp.sum(odds, 0, keepdims=True)
            expert = lax.broadcasted_iota(jnp.int32, (experts, tall), 0)
            named = jnp.zeros((experts, tall), f32)
            for n in range(topk):
                named = jnp.where(routes_ref[n : n + 1] == expert, 1.0, named)
            share = probs * named
            for n in range(experts):
                share_own[n] = share[n : n + 1]
            share_out[s] = share_own[s]
            for d in range(1, blocks):
                dest = (s + d) % blocks
                shares.append(send(share_own.at[dest], share_out.at[s], {"seq": dest}))

        shares = []

        def job(t, along, owner):
            def act():
                if owner == "first":
                    names = pieces if t < HOPS else some
                    if along < 0:
                        for p in names:
                            twins[t, p].wait_recv()
                        for p in ("ao", "as") if t < HOPS else ("ao",):
                            twins[t, "y" + p].wait_recv()
                experts_of(chip_at(r - step * t * along) * 2 + (0 if owner == "first" else 1))
            return act

        def own_job():
            experts_of(s)

        def sibling_job():
            twins[0, "yo"].wait_recv()
            experts_of(s + step)

        jobs = {0: [route], 1: [own_job], 3: [sibling_job]}
        for t in range(1, HOPS):
            at = 6 * t + (1 if t < HOPS - 1 else 0)
            for k, (along, owner) in enumerate(((1, "first"), (1, "second"), (-1, "first"), (-1, "second"))):
                jobs.setdefault(at + k, []).append(job(t, along, owner))
        late = []

        def drain(limit):
            while late and late[0][0] <= limit:
                _, t, p = late.pop(0)
                cross[t, p].wait_recv()
                put(twins, (t, "y" + p), -step * t, "y" + p[1], sib)

        loads[4].wait()
        loads[5].wait()
        for n, (t, p) in enumerate(order):
            circle[t, p].wait_recv()
            onward(t, p)
            if p in ("ao", "as"):
                put(cross, (t, p), -step * t, p, other)
                late.append((n, t, p))
            put(twins, (t, p), -step * t, p, sib)
            drain(n - 4)
            for act in jobs.pop(n, ()):
                act()
        drain(len(order))
        for n in sorted(jobs):
            for act in jobs[n]:
                act()
        for p in some + ("yao",):
            twins[HOPS, p].wait_recv()
        last = chip_at(r + HOPS) * 2
        experts_of(last)
        experts_of(last + 1)
        for copy in shares:
            copy.wait_recv()
        for copy in sent:
            copy.wait_send()

    vmem, smem = pl.BlockSpec(memory_space=VMEM), pl.BlockSpec(memory_space=pltpu.SMEM)
    return pl.pallas_call(
        kernel,
        out_shape=(
            jax.ShapeDtypeStruct((tall, width), bf16),
            jax.ShapeDtypeStruct((blocks * tall, hidden), bf16),
            jax.ShapeDtypeStruct((blocks, 1, tall), f32),
        ),
        in_specs=[smem] * 3 + [vmem] * 8 + [pl.BlockSpec(memory_space=pl.ANY)] * 6,
        out_specs=(vmem, vmem, vmem),
        scratch_shapes=[
            VMEM((width, local), bf16),
            VMEM((width, local), bf16),
            VMEM((width, local), bf16),
            VMEM((local, width), bf16),
            VMEM((width, hidden), bf16),
            VMEM((width, hidden), bf16),
            VMEM((tall, width), bf16),
            VMEM((tall, width), bf16),
            VMEM((2, cached, local), bf16),
            VMEM((groups, near, 2 * pair), bf16),
            VMEM((tall, local), bf16),
            VMEM((tall, local), bf16),
            VMEM((tall, cached + near), f32),
            VMEM((tall, width), bf16),
            VMEM((tall, width), bf16),
            VMEM((blocks * tall, width), bf16),
            VMEM((experts, 1, tall), f32),
            pltpu.SemaphoreType.DMA((6,)),
            pltpu.SemaphoreType.DMA((sems,)),
            pltpu.SemaphoreType.DMA((sems,)),
        ],
        compiler_params=pltpu.CompilerParams(
            collective_id=8, has_side_effects=True, vmem_limit_bytes=60 << 20
        ),
        name="front",
    )(lengths, request_group, shard_group, tokens, gain, freq, prefix_keys,
      prefix_values, moe_gain, w_router.T, routes.T, w_query, w_key, w_value, w_out,
      w_gate, w_up)


def attention(query, prefix_keys, prefix_values, suffix, bias):
    tall, wide = query.shape
    heads = wide // HD
    cached = prefix_keys.shape[0]
    keys = bias.shape[1]
    many = len(suffix)
    scale = HD ** (-0.5)

    def kernel(query_ref, cached_k, cached_v, bias_ref, *rest):
        suffix_k, suffix_v, out_ref = rest[:many], rest[many : 2 * many], rest[2 * many]
        head = query_ref[...]
        scores = [
            lax.dot_general(
                head, block[...], (((1,), (1,)), ((), ())), preferred_element_type=jnp.float32
            )
            for block in (cached_k, *suffix_k)
        ]
        scores = jnp.concatenate(scores, 1) * scale + bias_ref[...]
        weights = jnp.exp(scores - jnp.max(scores, -1, keepdims=True))
        total = jnp.sum(weights, -1, keepdims=True)
        weights = weights.astype(jnp.bfloat16)
        summed = jnp.dot(weights[:, :cached], cached_v[...], preferred_element_type=jnp.float32)
        for n, block in enumerate(suffix_v):
            start = cached + n * tall
            summed += jnp.dot(
                weights[:, start : start + tall], block[...], preferred_element_type=jnp.float32
            )
        out_ref[...] = (summed / total).astype(jnp.bfloat16)

    def column(rows, offset):
        return pl.BlockSpec((rows, HD), lambda h: (0, h + offset))

    return pl.pallas_call(
        kernel,
        out_shape=jax.ShapeDtypeStruct((tall, wide), jnp.bfloat16),
        grid=(heads,),
        in_specs=[column(tall, 0), column(cached, 0), column(cached, 0)]
        + [pl.BlockSpec((tall, keys), lambda h: (0, 0))]
        + [column(tall, 0)] * many
        + [column(tall, heads)] * many,
        out_specs=column(tall, 0),
        cost_estimate=pl.CostEstimate(
            flops=4 * tall * keys * wide, bytes_accessed=4 * keys * wide, transcendentals=0
        ),
        name="attention",
    )(query, prefix_keys, prefix_values, bias, *suffix, *suffix)


def on_device(
    tokens,
    attn_gain,
    w_query,
    w_key,
    w_value,
    w_out,
    prefix_keys,
    prefix_values,
    shard_group,
    request_group,
    lengths,
    moe_gain,
    w_router,
    w_gate,
    w_up,
    w_down,
    routes,
    final_gain,
    w_head,
):
    f32 = jnp.float32
    bf16 = jnp.bfloat16
    seq_index = lax.axis_index("seq")
    tp_index = lax.axis_index("tp")
    seq_count = lax.axis_size("seq")
    tp_count = lax.axis_size("tp")
    tok_dev = tokens.shape[0]
    width_part = tokens.shape[1]
    shard_rows = prefix_keys.shape[0]
    prefix_length = shard_rows * seq_count // 2
    ends = prefix_sums(lengths)
    experts = w_router.shape[1]
    topk = routes.shape[1]
    local_index = seq_index * tok_dev + jnp.arange(tok_dev)
    if seq_count == 16 and tp_count == 2 and experts == seq_count and 16 % lengths.shape[0] == 0:
        resid_full, act, shares = front(
            tokens, attn_gain, w_query, w_key, w_value, w_out, prefix_keys, prefix_values, lengths,
            request_group, shard_group, moe_gain, w_router, routes,
            w_gate[0], w_up[0],
        )
        return back(act, shares, w_down[0], resid_full, lengths, final_gain, w_head)
    full_x = gather_columns(tokens)
    width = full_x.shape[1]
    normed = normalize(full_x.astype(f32), attn_gain).astype(bf16)
    heads = w_query.shape[1] // HD
    starts = ends - lengths
    own_request = request_of(local_index, ends)
    own_start = lookup(own_request, starts)
    own_group = lookup(own_request, request_group)
    position = (prefix_length + local_index - own_start).astype(f32)
    query = rotate(
        jnp.dot(normed, w_query, preferred_element_type=f32).reshape(tok_dev, heads, HD), position
    ).astype(bf16)
    key_rows = rotate(
        jnp.dot(normed, w_key, preferred_element_type=f32).reshape(tok_dev, heads, HD), position
    ).astype(bf16)
    key_rows = key_rows.reshape(tok_dev, heads * HD)
    value_rows = jnp.dot(normed, w_value, preferred_element_type=f32).astype(bf16)
    pieces = (
        lax.all_gather(prefix_keys, "seq", axis=0, tiled=True),
        lax.all_gather(prefix_values, "seq", axis=0, tiled=True),
    )
    count = pieces[0].shape[0]
    shard_ids = jnp.arange(count) // shard_rows
    key_group = lookup(shard_ids, shard_group)
    fold_allowed = own_group[:, None] == key_group[None, :]
    own_allowed = (own_request[:, None] == own_request[None, :]) & (
        local_index[None, :] <= local_index[:, None]
    )
    both_rows = jnp.concatenate([key_rows, value_rows], 1)
    suffix = [both_rows] + [from_behind(both_rows, "seq", step) for step in range(1, SPAN + 1)]
    permitted = [fold_allowed, own_allowed]
    for step in range(1, SPAN + 1):
        key_index = (seq_index - step) * tok_dev + jnp.arange(tok_dev)
        key_request = request_of(key_index, ends)
        permitted.append(
            (key_index >= 0)[None, :] & (own_request[:, None] == key_request[None, :])
        )
    bias = jnp.where(jnp.concatenate(permitted, 1), 0.0, NEGATIVE)
    attended = attention(query.reshape(tok_dev, heads * HD), *pieces, suffix, bias)
    mixed = jnp.dot(attended, w_out, preferred_element_type=f32).astype(bf16)
    resid_full = (full_x.astype(f32) + sum_over_tp(mixed)).astype(bf16)
    moe_in = normalize(resid_full.astype(f32), moe_gain).astype(bf16)
    probs = jax.nn.softmax(jnp.dot(moe_in, w_router, preferred_element_type=f32), -1)
    flat = routes.reshape(-1)
    hits = (flat[:, None] == jnp.arange(experts)[None, :]).astype(jnp.int32)
    line = jnp.arange(flat.shape[0])
    before = (line[:, None] > line[None, :]).astype(bf16)
    earlier = jnp.dot(before, hits.astype(bf16), preferred_element_type=f32).astype(jnp.int32)
    rank = jnp.sum(earlier * hits, 1)
    capacity = min(tok_dev, tp_count * max(1, 3 * tok_dev * topk // (2 * experts * tp_count)))
    target = flat * capacity + rank
    route_weight = jnp.sum(hits.reshape(tok_dev, topk, experts).astype(f32) * probs[:, None, :], -1)
    repeated = jnp.repeat(moe_in, topk, axis=0)
    outgoing = (
        jnp.zeros((experts * capacity, width), bf16)
        .at[target]
        .set(repeated)
        .reshape(experts, capacity, width)
    )
    arrived = lax.all_to_all(outgoing, "seq", split_axis=0, concat_axis=0, tiled=True)
    sources = arrived.shape[0]
    count = arrived.shape[1]
    rows = arrived.reshape(sources * count, width)
    gate = jnp.dot(rows, w_gate[0], preferred_element_type=f32)
    up = jnp.dot(rows, w_up[0], preferred_element_type=f32)
    act = (jax.nn.silu(gate) * up).astype(bf16)
    partial_out = jnp.dot(act, w_down[0], preferred_element_type=f32).reshape(sources, count, width)
    summed = lax.psum_scatter(partial_out, "tp", scatter_dimension=2, tiled=True).astype(bf16)
    returned = lax.all_to_all(summed, "seq", split_axis=0, concat_axis=0, tiled=True)
    picked = returned.reshape(experts * capacity, width_part)[target].reshape(
        tok_dev, topk, width_part
    )
    moe_part = jnp.sum(picked.astype(f32) * route_weight[:, :, None], 1)
    resid = lax.dynamic_slice_in_dim(resid_full, tp_index * width_part, width_part, 1)
    hidden = (resid.astype(f32) + moe_part).astype(bf16)
    last_hit = ((ends - 1)[:, None] == local_index[None, :]).astype(bf16)
    chosen = jnp.dot(last_hit, hidden, preferred_element_type=f32)
    final = last_rows(chosen, final_gain, width)
    log_probs = log_softmax(jnp.dot(final, w_head, preferred_element_type=f32))
    return (hidden, log_probs)


def solution(mesh):
    in_specs = (
        P("seq", "tp"),
        P(),
        P(None, "tp"),
        P(None, "tp"),
        P(None, "tp"),
        P("tp", None),
        P("seq", "tp"),
        P("seq", "tp"),
        P(),
        P(),
        P(),
        P(),
        P(),
        P("seq", None, "tp"),
        P("seq", None, "tp"),
        P("seq", "tp", None),
        P("seq", None),
        P("tp"),
        P("tp", "seq"),
    )
    out_specs = (P("seq", "tp"), P(None, "seq"))
    return jax.shard_map(
        on_device, mesh=mesh, in_specs=in_specs, out_specs=out_specs, check_vma=False
    )
```
